256 devices in a mesh: atoms: 32 (over x_lo, z, core), beads: 8 (over x_hi, y).
Axes of the slice: x: 4 (x_hi: 2, x_lo: 2; x = x_hi * 2 + x_lo), y: 4, z: 8, core: 2. Of those that a mesh axis runs over, the one named last changes fastest.
Arguments:
- positions: float32 [32, 3, 4096], P('beads', None, 'atoms'), may hold values from 0 to 1
- velocities: float32 [32, 3, 4096], P('beads', None, 'atoms'), may hold values from -3 to 3
- charges_in: float32 [32, 4096], P('beads', 'atoms'), may hold values from -3 to 3
- species: int32 [4096], P('atoms'), may hold values from 0 to 7
- neighbors: int32 [8, 4096], P(None, 'atoms'), may hold values from -32 to 32
- k_index: int32 [3, 2048], replicated, may hold values from -8 to 8
- kernel: float32 [2048], replicated, may hold values from 0.1 to 1
- chi_table: float32 [8], replicated, may hold values from -2 to 2
- hard_table: float32 [8], replicated, may hold values from 1 to 4
- bond_table: float32 [8], replicated, may hold values from 0.2 to 0.8
- mass_table: float32 [8], replicated, may hold values from 1 to 8
Outputs:
- new_positions: float32 [32, 3, 4096], P('beads', None, 'atoms')
- new_velocities: float32 [32, 3, 4096], P('beads', None, 'atoms')
- charges: float32 [32, 4096], P('beads', 'atoms')
The draws below stay inside these ranges and needn't reach their ends.
Inputs may be any that keep to these rules, and one draw needn't show every extreme that they name: species index the tables. `neighbors`: neighbour offsets count in atom order, cyclically over 4096 atoms.
All inputs are finite; a program needn't handle non-finite values.
Results may differ from the reference program's by a relative error of at most 0.00021.
Values sent between devices are 32-bit elements; how exact they have to be, the bound alone decides.
A program may use at most 64 MiB of HBM per device.

```python
import math
import jax
import jax.numpy as jnp
from jax import lax

KVEC = 2048
KMAX = 8
QITERS = 2
NBR = 8
RIM = 32
SPECIES = 8
ATOMS = 4096
BEADS = 32


def touch_ends(drawn, rng, low, top_value):
    shape = drawn.shape
    spot = [jax.random.randint(jax.random.fold_in(rng, axis), (), 0, shape[axis]) for axis in range(len(shape))]
    drawn = drawn.at[tuple(spot)].set(low)
    longest = shape.index(max(shape))
    spot[longest] = (spot[longest] + 1) % shape[longest]
    return drawn.at[tuple(spot)].set(top_value)


def level_of(own_key, shape, pieces, smallest, high):
    level, own = 1.0, jax.random.fold_in(own_key, 6)
    for axis_at, blocks in pieces:
        draws = jnp.exp(jax.random.uniform(jax.random.fold_in(own, axis_at), (blocks,), jnp.float32, smallest / len(pieces), high / len(pieces)))
        level = level * jnp.repeat(draws, shape[axis_at] // blocks).reshape([-1 if axis == axis_at else 1 for axis in range(len(shape))])
    return level


def gaussian(own_key, dims, spread, most, split=(), kind=jnp.bfloat16):
    gain = level_of(own_key, dims, split, -0.22, 0.18) if split else 1.0
    values = jax.random.normal(own_key, dims, jnp.float32) * spread * gain
    return jnp.minimum(jnp.maximum(values, -most), most).astype(kind)


def setup_inputs(seed: int = 0) -> dict:
    splits = jax.random.split(jax.random.key(seed), 12)
    positions = jnp.clip(1.0 * jax.random.uniform(splits[0], (BEADS, 3, ATOMS), jnp.float32) ** level_of(splits[0], (BEADS, 3, ATOMS), ((0, 8), (2, 32)), -0.2, 0.2), 0.0, 1.0)
    velocities = gaussian(splits[1], (BEADS, 3, ATOMS), 0.5, 3.0, ((0, 8), (2, 32)), jnp.float32)
    charges_in = gaussian(splits[2], (BEADS, ATOMS), 0.5, 3.0, ((0, 8), (1, 32)), jnp.float32)
    species = touch_ends(jax.random.randint(splits[3], (ATOMS,), 0, SPECIES), jax.random.fold_in(splits[3], 1), 0, SPECIES - 1).astype(jnp.int32)
    neighbors = touch_ends(jax.random.randint(splits[4], (NBR, ATOMS), -RIM, RIM + 1), jax.random.fold_in(splits[4], 1), -RIM, RIM).astype(jnp.int32)
    k_index = touch_ends(jax.random.randint(splits[5], (3, KVEC), -KMAX, KMAX + 1), jax.random.fold_in(splits[5], 1), -KMAX, KMAX).astype(jnp.int32)
    kernel = jnp.clip(jnp.exp(jax.random.uniform(splits[6], (KVEC,), jnp.float32, math.log(0.1), math.log(1.0))), 0.1, 1.0)
    chi_table = jnp.clip(jax.random.uniform(splits[7], (SPECIES,), jnp.float32, -2.0, 2.0), -2.0, 2.0)
    hard_table = jnp.clip(jnp.exp(jax.random.uniform(splits[8], (SPECIES,), jnp.float32, math.log(1.0), math.log(4.0))), 1.0, 4.0)
    bond_table = jnp.clip(jax.random.uniform(splits[9], (SPECIES,), jnp.float32, 0.2, 0.8), 0.2, 0.8)
    mass_table = jnp.clip(jnp.exp(jax.random.uniform(splits[10], (SPECIES,), jnp.float32, math.log(1.0), math.log(8.0))), 1.0, 8.0)
    return dict(positions=positions, velocities=velocities, charges_in=charges_in, species=species, neighbors=neighbors, k_index=k_index, kernel=kernel, chi_table=chi_table, hard_table=hard_table, bond_table=bond_table, mass_table=mass_table)


two_pi = 2.0 * math.pi
ewald_gain = 4.0
mixing = 0.5
spring_rate = 0.5
time_step = 0.05
HIGH = lax.Precision.HIGHEST

def phase_tables(bead_pos, wave):
    angle = two_pi * (bead_pos[0][:, None] * wave[0] + bead_pos[1][:, None] * wave[1] + bead_pos[2][:, None] * wave[2])
    return (jnp.cos(angle), jnp.sin(angle))

def reference(positions, velocities, charges_in, species, neighbors, k_index, kernel, chi_table, hard_table, bond_table, mass_table):
    wave = k_index.astype(jnp.float32)
    ewald_scale = ewald_gain / math.sqrt(KVEC * ATOMS)
    onehot = (species[None, :] == jnp.arange(SPECIES, dtype=jnp.int32)[:, None]).astype(jnp.float32)

    def lookup(table):
        return lax.optimization_barrier(jnp.sum(table[:, None] * onehot, 0))
    electroneg = lookup(chi_table)
    hardness = lookup(hard_table)
    bond_term = lookup(bond_table)
    atom_mass = lookup(mass_table)
    neighbour_index = (jnp.arange(ATOMS, dtype=jnp.int32)[None, :] + neighbors) % ATOMS

    def factor_one(inputs):
        bead_pos, charge_row = inputs
        cosine, sine_part = phase_tables(bead_pos, wave)
        return jnp.stack([jnp.dot(charge_row, cosine, precision=HIGH), jnp.dot(charge_row, sine_part, precision=HIGH)], 0)

    def potential_one(inputs):
        bead_pos, pair = inputs
        cosine, sine_part = phase_tables(bead_pos, wave)
        coeff = kernel[None, :] * pair
        return jnp.dot(cosine, coeff[0], precision=HIGH) + jnp.dot(sine_part, coeff[1], precision=HIGH)

    def force_one(inputs):
        bead_pos, pair = inputs
        cosine, sine_part = phase_tables(bead_pos, wave)
        coeff = kernel[None, :] * pair
        mixed = sine_part * coeff[0][None, :] - cosine * coeff[1][None, :]
        return jnp.einsum('dk,ak->da', wave, mixed, precision=HIGH)
    charge = charges_in
    for rounds in range(QITERS):
        pair = lax.map(factor_one, (positions, charge))
        potential = ewald_scale * lax.map(potential_one, (positions, pair))
        weighted = bond_term[None, :] * charge
        neighbour_sum = lax.optimization_barrier(jnp.sum(weighted[:, neighbour_index], 1))
        relaxed = (1.0 - mixing) * charge + mixing * (-(electroneg + potential + bond_term * neighbour_sum) / hardness)
        charge = relaxed - lax.optimization_barrier(jnp.sum(relaxed, 1, keepdims=True)) / ATOMS
    pair = lax.map(factor_one, (positions, charge))
    ewald_force = two_pi * ewald_scale * charge[:, None, :] * lax.map(force_one, (positions, pair))
    laplace = 2.0 * positions - jnp.roll(positions, 1, 0) - jnp.roll(positions, -1, 0)
    acceleration = ewald_force / atom_mass[None, None, :] - spring_rate * laplace
    new_velocities = velocities + time_step * acceleration
    new_positions = positions + time_step * new_velocities
    return (new_positions, new_velocities, charge)
```

```python
import math

import jax
import jax.numpy as jnp
from jax import lax
from jax.experimental import pallas as pl
from jax.experimental.pallas import tpu as pltpu
from jax.sharding import PartitionSpec as P

KVEC = 2048
SPECIES = 8
ATOMS = 4096
GROUP = 32
BEAD_AXIS = 8
BLOCK = 128
SLOTS = 16
HALF = SLOTS * BLOCK
TILES = 38
ROWS = TILES * 8
EXROWS = ROWS + 8

two_pi = 2.0 * math.pi
ewald_scale = 4.0 / math.sqrt(KVEC * ATOMS)
time_step = 0.05
spring_rate = 0.5

COS = (1.0, -19.7392087, 64.9393891, -85.4566583, 60.2421313, -26.4046682, 7.80013144, -1.45311232)
SIN = (6.2831853, -41.3417004, 81.6051314, -76.7030154, 42.025927, -14.8998467, 3.2381375)

MESH = pl.DeviceIdType.MESH
NT = (((1,), (1,)), ((), ()))
f32 = jnp.float32
bf16 = jnp.bfloat16


def horner(coeffs, s):
    total = coeffs[-1] * s + coeffs[-2]
    for value in coeffs[-3::-1]:
        total = total * s + value
    return total


def harmonics(row):
    n = lax.broadcasted_iota(jnp.int32, (8, row.shape[1]), 0).astype(f32) + 1.0
    turns = n * row
    r = turns - jnp.floor(turns + 0.5)
    s = r * r
    return horner(COS, s), r * horner(SIN, s)


def split(x):
    high = x.astype(bf16)
    return high, x - high.astype(f32)


def tile(x, t):
    return x[8 * t : 8 * t + 8, :]


def flip(x):
    lane = lax.broadcasted_iota(jnp.int32, x.shape, 1)
    return jnp.where(lane < 16, pltpu.roll(x, 112, 1), pltpu.roll(x, 16, 1))


def core_tile(ta, tb, a):
    return 16 * ta + 8 * tb + a


def expand(coeff):
    high, low = split(coeff)
    return (high.astype(f32) + pltpu.roll(low, 32, 1) + pltpu.roll(high.astype(f32), 64, 1)).astype(bf16)


def kernel_body(
    pos_ref,
    vel_ref,
    chg_ref,
    spec_ref,
    nbr_ref,
    k_ref,
    kern_ref,
    chi_ref,
    hard_ref,
    bond_ref,
    mass_ref,
    npos_ref,
    nvel_ref,
    nchg_ref,
    send_s,
    buf,
    nbuf,
    utab,
    uhi,
    ulo,
    wtab,
    wst,
    acols,
    etab,
    ex_s,
    ex_r,
    factor,
    coef,
    lhs,
    phi_s,
    near_s,
    nbond_s,
    ext_s,
    fsend,
    frecv,
    halo,
    s_sem,
    r_sem,
    ns_sem,
    nr_sem,
    xs_sem,
    xr_sem,
    fs_sem,
    fr_sem,
    hs_sem,
    hr_sem,
):
    me = lax.axis_index("atoms")
    bead = lax.axis_index("beads")
    x_lo = me // 16
    z = (me // 2) % 8
    core = me % 2
    quad = z // 2
    partner = x_lo * 16 + z * 2 + (1 - core)
    next_bead = (bead + 1) % BEAD_AXIS
    prev_bead = (bead + BEAD_AXIS - 1) % BEAD_AXIS

    barrier = pltpu.get_barrier_semaphore()

    def greet(k, carry):
        pl.semaphore_signal(barrier, inc=1, device_id={"atoms": (me + k) % GROUP}, device_id_type=MESH)
        return carry

    lax.fori_loop(1, GROUP, greet, 0)
    for other in (next_bead, prev_bead):
        pl.semaphore_signal(barrier, inc=1, device_id={"beads": other}, device_id_type=MESH)

    species = spec_ref[...]

    def lookup(table):
        total = jnp.zeros((1, BLOCK), f32)
        for s in range(SPECIES):
            total = jnp.where(species == s, table[0, s], total)
        return total

    chi_row, hard_row, bond_row, mass_row = (lookup(t) for t in (chi_ref, hard_ref, bond_ref, mass_ref))
    for b in range(4):
        send_s[b, 0:3, :] = pos_ref[b]
        send_s[b, 3:4, :] = chg_ref[b : b + 1, :]
        send_s[b, 4:5, :] = chi_row
        send_s[b, 5:6, :] = hard_row
        send_s[b, 6:7, :] = bond_row
        send_s[b, 7:8, :] = bond_row

    pl.semaphore_wait(barrier, GROUP + 1)

    slot = z * 2 + core

    def far_dest(b, o):
        return (b >> 1) * 16 + (2 * ((quad + o) % 4) + (b & 1)) * 2 + x_lo

    def data_copy(b, o, dest):
        return pltpu.make_async_remote_copy(
            send_s.at[b], buf.at[slot], s_sem.at[4 * o + b], r_sem.at[slot], device_id={"atoms": dest}, device_id_type=MESH
        )

    def nbr_copy(b, o, dest):
        return pltpu.make_async_remote_copy(
            nbr_ref, nbuf.at[slot], ns_sem.at[4 * o + b], nr_sem.at[slot], device_id={"atoms": dest}, device_id_type=MESH
        )

    order = [(b, o) for o in (2, 1, 3, 0) for b in range(4)]
    for make, source, store, sem in (
        (data_copy, lambda b: send_s.at[b], buf, r_sem),
        (nbr_copy, lambda b: nbr_ref, nbuf, nr_sem),
    ):
        for b, o in order:
            dest = far_dest(b, o)
            if o:
                make(b, o, dest).start()
            else:

                @pl.when(dest != me)
                def _():
                    make(b, o, dest).start()

                @pl.when(dest == me)
                def _():
                    pltpu.make_async_copy(source(b), store.at[slot], sem.at[slot]).start()

    to_next = pltpu.make_async_remote_copy(
        pos_ref.at[3], halo.at[0], hs_sem.at[0], hr_sem.at[0], device_id={"beads": next_bead}, device_id_type=MESH
    )
    to_prev = pltpu.make_async_remote_copy(
        pos_ref.at[0], halo.at[1], hs_sem.at[1], hr_sem.at[1], device_id={"beads": prev_bead}, device_id_type=MESH
    )
    to_next.start()
    to_prev.start()

    nx, ny, nz = (k_ref[d : d + 1, :] for d in range(3))
    ax, ay, az = jnp.abs(nx), jnp.abs(ny), jnp.abs(nz)
    code = jnp.where(
        ax > 0,
        jnp.where(ay > 0, 8 * (ax - 1) + ay - 1, 72 + ax - 1),
        jnp.where(ay > 0, 64 + ay - 1, 80),
    )
    row_hot = jnp.where(lax.broadcasted_iota(jnp.int32, (96, KVEC), 0) == code, 1.0, 0.0).astype(bf16)
    lane_code = jnp.where(az > 0, az - 1, 8)
    lane_hot = lax.broadcasted_iota(jnp.int32, (16, KVEC), 0) == lane_code
    sx, sy, sz = (jnp.where(n < 0, -1.0, 1.0) for n in (nx, ny, nz))
    weight = kern_ref[...]
    parts = [[], []]
    for j, sign in enumerate((None, -sy * sz, -sx * sz, -sx * sy)):
        value = weight if sign is None else weight * sign
        high = value.astype(bf16).astype(f32)
        for part, piece in zip(parts, (high, value - high)):
            block = jnp.where(lane_hot, piece, 0.0)
            part += [block, -block if j in (1, 2) else block]
    grid = None
    for part in parts:
        term = lax.dot_general(row_hot, jnp.concatenate(part, 0).astype(bf16), NT, preferred_element_type=f32)
        grid = term if grid is None else grid + term
    lane = lax.broadcasted_iota(jnp.int32, (96, 128), 1)
    for j in range(4):
        moved = grid if j == 0 else pltpu.roll(grid, 128 - 32 * j, 1)
        etab[j] = jnp.where(lane < 32, moved, 0.0)

    factor[...] = jnp.zeros((ROWS, 128), f32)
    first = jnp.where(lax.broadcasted_iota(jnp.int32, (8, 512), 0) == 0, 1.0, 0.0)
    zero8 = jnp.zeros((8, 512), f32)

    def arrive(step, carry):
        offset = jnp.where(step == 0, 0, jnp.where(step == 1, 1, jnp.where(step == 2, 3, 2)))
        base = ((quad + offset) % 4) * 4
        for m in range(4):
            pltpu.make_async_remote_copy(
                send_s.at[0],
                buf.at[base + m],
                s_sem.at[0],
                r_sem.at[base + m],
                device_id={"atoms": partner},
                device_id_type=MESH,
            ).wait_recv()
        rows = [jnp.concatenate([buf[base + m, r : r + 1, :] for m in range(4)], 1) for r in range(4)]
        at = pl.ds(pl.multiple_of(base * BLOCK, 512), 512)
        (cu, su), (cv, sv), (cw, sw) = (harmonics(rows[d]) for d in range(3))

        def put(t, low_tile, high_tile):
            both = jnp.concatenate([low_tile, high_tile], 0)
            utab[8 * t : 8 * t + 16, at] = both
            high, low = split(both)
            uhi[8 * t : 8 * t + 16, at] = high
            ulo[8 * t : 8 * t + 16, at] = low.astype(bf16)

        for ta, u in ((0, cu), (1, su)):
            for tb, v in ((0, cv), (1, sv)):
                for a in range(0, 8, 2):
                    put(core_tile(ta, tb, a), u[a : a + 1, :] * v, u[a + 1 : a + 2, :] * v)
        put(32, cv, sv)
        put(34, cu, su)
        put(36, first, zero8)

        w = jnp.concatenate([cw, first, sw, zero8], 0)
        wtab[:, at] = w
        whi, wlo = split(w)
        wlo = wlo.astype(bf16)
        wst[0:32, at] = whi
        wst[32:64, at] = whi
        wst[64:96, at] = wlo
        wst[96:128, at] = jnp.zeros((32, 512), bf16)
        qhi, qlo = split(w * rows[3])
        a_block = jnp.concatenate([qhi, qlo.astype(bf16), whi, wlo], 0)
        acols[:, at] = a_block
        factor[...] += lax.dot_general(uhi[:, at], a_block, NT, preferred_element_type=f32) + lax.dot_general(
            ulo[:, at], a_block, NT, preferred_element_type=f32
        )
        return carry

    lax.fori_loop(0, 4, arrive, 0)

    charge = buf[:, 3, :]
    chi = buf[:, 4, :]
    inv_hard = 1.0 / buf[:, 5, :]
    bond = buf[:, 6, :]

    def start_exchange(r, weighted):
        ex_s[r, 0:ROWS, :] = factor[...]
        ends = jnp.concatenate(
            [weighted[0:1, :], weighted[15:16, :], bond[0:1, :], bond[15:16, :], jnp.zeros((4, 128), f32)], 0
        )
        ex_s[r, ROWS:EXROWS, :] = ends
        copy = pltpu.make_async_remote_copy(
            ex_s.at[r], ex_r.at[r], xs_sem.at[r], xr_sem.at[r], device_id={"atoms": partner}, device_id_type=MESH
        )
        copy.start()
        return copy

    def mix(r, centre):
        total = ex_s[r, 0:ROWS, :] + ex_r[r, 0:ROWS, :]
        total = total + pltpu.roll(total, 96, 1)
        mean = 0.0
        if centre:
            mean = total[8 * 36 : 8 * 36 + 1, 8:9] * (1.0 / ATOMS)
            total = total - mean * pltpu.roll(total, 64, 1)
        for ta in range(2):
            for tb in range(2):
                for a in range(8):
                    here = tile(total, core_tile(ta, tb, a))
                    both = tile(total, core_tile(1 - ta, 1 - tb, a))
                    over_b = flip(tile(total, core_tile(ta, 1 - tb, a)))
                    over_a = flip(tile(total, core_tile(1 - ta, tb, a)))
                    e = [etab[j, 8 * a : 8 * a + 8, :] for j in range(4)]
                    out = e[0] * here
                    out = out + e[3] * both if ta == tb else out - e[3] * both
                    out = out + e[1] * over_b if tb == 0 else out - e[1] * over_b
                    out = out + e[2] * over_a if ta == 0 else out - e[2] * over_a
                    t = core_tile(ta, tb, a)
                    coef[8 * t : 8 * t + 8, :] = out
        for first_tile, row, j in ((32, 64, 1), (34, 72, 2)):
            e0 = etab[0, row : row + 8, :]
            ej = etab[j, row : row + 8, :]
            c, s = tile(total, first_tile), tile(total, first_tile + 1)
            coef[8 * first_tile : 8 * first_tile + 8, :] = e0 * c + ej * flip(s)
            coef[8 * first_tile + 8 : 8 * first_tile + 16, :] = e0 * s - ej * flip(c)
        coef[8 * 36 : 8 * 37, :] = etab[0, 80:88, :] * tile(total, 36)
        coef[8 * 37 : 8 * 38, :] = jnp.zeros((8, 128), f32)
        return mean

    def potential():
        lhs[0:ROWS, :] = expand(coef[...])

        def visit(i, carry):
            at = pl.ds(pl.multiple_of(i * 256, 256), 256)
            fields = jnp.dot(lhs[0:ROWS, :], wst[:, at], preferred_element_type=f32)
            total = jnp.sum((fields * utab[:, at]).reshape(TILES, 8, 256), 0)
            row = jnp.sum(total, 0, keepdims=True)
            phi_s[pl.ds(2 * i, 1), :] = row[:, 0:128]
            phi_s[pl.ds(2 * i + 1, 1), :] = row[:, 128:256]
            return carry

        lax.fori_loop(0, SLOTS // 2, visit, 0)

    def near_sums(own, left, right, out):
        ext_s[0:1, :] = left
        ext_s[1:17, :] = own
        ext_s[17:18, :] = right
        lane_at = lax.broadcasted_iota(jnp.int32, (8, BLOCK), 1)

        def visit(j, carry):
            target = lane_at + nbuf[j]
            index = target & (BLOCK - 1)
            low, mid, high = (
                jnp.take_along_axis(
                    jnp.broadcast_to(ext_s[pl.ds(j + d, 1), :], (8, BLOCK)), index, axis=1, mode="promise_in_bounds"
                )
                for d in range(3)
            )
            got = jnp.where(target < 0, low, jnp.where(target >= BLOCK, high, mid))
            out[pl.ds(j, 1), :] = jnp.sum(got, 0, keepdims=True)
            return carry

        lax.fori_loop(0, SLOTS, visit, 0)

    def refactor(values):
        for j in range(SLOTS):
            at = slice(j * BLOCK, (j + 1) * BLOCK)
            qhi, qlo = split(wtab[:, at] * values[j : j + 1, :])
            acols[0:32, at] = qhi
            acols[32:64, at] = qlo.astype(bf16)
        factor[...] = lax.dot_general(uhi[...], acols[...], NT, preferred_element_type=f32) + lax.dot_general(
            ulo[...], acols[...], NT, preferred_element_type=f32
        )

    def relax(charge, near):
        potential_here = ewald_scale * phi_s[...]
        return 0.5 * charge + 0.5 * (-(chi + potential_here + bond * near) * inv_hard)

    weighted = bond * charge
    exchange = start_exchange(0, weighted)

    def wait_nbr(j, carry):
        pltpu.make_async_remote_copy(
            nbr_ref, nbuf.at[j], ns_sem.at[0], nr_sem.at[j], device_id={"atoms": partner}, device_id_type=MESH
        ).wait_recv()
        return carry

    lax.fori_loop(0, SLOTS, wait_nbr, 0)
    exchange.wait()
    ends = ex_r[0, ROWS:EXROWS, :]
    near_sums(bond, ends[3:4, :], ends[2:3, :], nbond_s)
    near_sums(weighted, ends[1:2, :], ends[0:1, :], near_s)
    mix(0, False)
    potential()
    relaxed = relax(charge, near_s[...])

    weighted = bond * relaxed
    refactor(relaxed)
    exchange = start_exchange(1, weighted)
    exchange.wait()
    ends = ex_r[1, ROWS:EXROWS, :]
    near_sums(weighted, ends[1:2, :], ends[0:1, :], near_s)
    mean = mix(1, True)
    potential()
    charge = relaxed - mean
    relaxed = relax(charge, near_s[...] - mean * nbond_s[...])

    refactor(relaxed)
    exchange = start_exchange(2, bond * relaxed)
    exchange.wait()
    mean = mix(2, True)
    near_s[...] = relaxed - mean

    lane = lax.broadcasted_iota(jnp.int32, (ROWS, 128), 1)
    number = jnp.where((lane & 15) < 8, (lane & 15) + 1, 0).astype(f32)
    slope = jnp.where(lane < 16, number, -number)
    whole = coef[...]
    lhs[0:ROWS, :] = expand(whole)
    lhs[ROWS : 2 * ROWS, :] = expand(jnp.where(lane < 32, flip(whole) * slope, 0.0))
    ones = lax.broadcasted_iota(jnp.int32, (8, 256), 0).astype(f32) + 1.0

    def force(i, carry):
        at = pl.ds(pl.multiple_of(quad * 512 + i * 256, 256), 256)
        fields = jnp.dot(lhs[...], wst[:, at], preferred_element_type=f32)
        basis = [utab[8 * t : 8 * t + 8, at] for t in range(37)]

        def plain(t):
            return fields[8 * t : 8 * t + 8, :]

        dz = basis[0] * fields[ROWS : ROWS + 8, :]
        for t in range(1, 37):
            dz = dz + basis[t] * fields[ROWS + 8 * t : ROWS + 8 * t + 8, :]
        dx = jnp.zeros((8, 256), f32)
        for a in range(8):
            term = jnp.zeros((8, 256), f32)
            for tb in range(2):
                c, s = core_tile(0, tb, a), core_tile(1, tb, a)
                term = term + basis[c] * plain(s) - basis[s] * plain(c)
            dx = dx + (a + 1.0) * term
        dx = dx + ones * (basis[34] * plain(35) - basis[35] * plain(34))
        dy = basis[32] * plain(33) - basis[33] * plain(32)
        for ta in range(2):
            for a in range(8):
                c, s = core_tile(ta, 0, a), core_tile(ta, 1, a)
                dy = dy + basis[c] * plain(s) - basis[s] * plain(c)
        dy = dy * ones
        dx, dy, dz = (jnp.sum(d, 0, keepdims=True) for d in (dx, dy, dz))
        for m in range(2):
            own = near_s[pl.ds(quad * 4 + 2 * i + m, 1), :]
            piece = slice(128 * m, 128 * m + 128)
            fsend[2 * i + m] = jnp.concatenate(
                [dx[:, piece], dy[:, piece], dz[:, piece], own, jnp.zeros((4, 128), f32)], 0
            )
        return carry

    lax.fori_loop(0, 2, force, 0)

    my_bead = 2 * x_lo + z % 2

    def force_copy(m):
        home = core * 16 + (2 * quad + (m >> 1)) * 2 + (m & 1)
        return home, pltpu.make_async_remote_copy(
            fsend.at[m], frecv.at[my_bead], fs_sem.at[m], fr_sem.at[my_bead], device_id={"atoms": home}, device_id_type=MESH
        )

    for m in range(4):
        home, copy = force_copy(m)

        @pl.when(home != me)
        def _():
            copy.start()

        @pl.when(home == me)
        def _():
            pltpu.make_async_copy(fsend.at[m], frecv.at[my_bead], fr_sem.at[my_bead]).start()

    for make in (data_copy, nbr_copy):
        for b, o in order:
            dest = far_dest(b, o)
            if o:
                make(b, o, dest).wait_send()
            else:

                @pl.when(dest != me)
                def _():
                    make(b, o, dest).wait_send()

    to_next.wait()
    to_prev.wait()
    inv_mass = 1.0 / mass_row
    for b in range(4):
        pltpu.make_async_remote_copy(
            fsend.at[0], frecv.at[b], fs_sem.at[0], fr_sem.at[b], device_id={"atoms": partner}, device_id_type=MESH
        ).wait_recv()
        got = frecv[b]
        charges = got[3:4, :]
        nchg_ref[b : b + 1, :] = charges
        ewald_force = (-two_pi * ewald_scale) * charges * got[0:3, :]
        here = pos_ref[b]
        before = halo[0] if b == 0 else pos_ref[b - 1]
        after = halo[1] if b == 3 else pos_ref[b + 1]
        laplace = 2.0 * here - before - after
        speed = vel_ref[b] + time_step * (ewald_force * inv_mass - spring_rate * laplace)
        nvel_ref[b] = speed
        npos_ref[b] = here + time_step * speed
    for m in range(4):
        home, copy = force_copy(m)

        @pl.when(home != me)
        def _():
            copy.wait_send()


def step(positions, velocities, charges_in, species, neighbors, k_index, kernel, chi, hard, bond, mass):
    vmem = pl.BlockSpec(memory_space=pltpu.VMEM)
    smem = pl.BlockSpec(memory_space=pltpu.SMEM)
    dma = pltpu.SemaphoreType.DMA
    return pl.pallas_call(
        kernel_body,
        out_shape=(
            jax.ShapeDtypeStruct(positions.shape, f32),
            jax.ShapeDtypeStruct(velocities.shape, f32),
            jax.ShapeDtypeStruct(charges_in.shape, f32),
        ),
        in_specs=[vmem] * 7 + [smem] * 4,
        out_specs=(vmem, vmem, vmem),
        scratch_shapes=[
            pltpu.VMEM((4, 8, 128), f32),
            pltpu.VMEM((SLOTS, 8, 128), f32),
            pltpu.VMEM((SLOTS, 8, 128), jnp.int32),
            pltpu.VMEM((ROWS, HALF), f32),
            pltpu.VMEM((ROWS, HALF), bf16),
            pltpu.VMEM((ROWS, HALF), bf16),
            pltpu.VMEM((32, HALF), f32),
            pltpu.VMEM((128, HALF), bf16),
            pltpu.VMEM((128, HALF), bf16),
            pltpu.VMEM((4, 96, 128), f32),
            pltpu.VMEM((3, EXROWS, 128), f32),
            pltpu.VMEM((3, EXROWS, 128), f32),
            pltpu.VMEM((ROWS, 128), f32),
            pltpu.VMEM((ROWS, 128), f32),
            pltpu.VMEM((2 * ROWS, 128), bf16),
            pltpu.VMEM((SLOTS, 128), f32),
            pltpu.VMEM((SLOTS, 128), f32),
            pltpu.VMEM((SLOTS, 128), f32),
            pltpu.VMEM((24, 128), f32),
            pltpu.VMEM((4, 8, 128), f32),
            pltpu.VMEM((4, 8, 128), f32),
            pltpu.VMEM((2, 3, 128), f32),
            dma((16,)),
            dma((16,)),
            dma((16,)),
            dma((16,)),
            dma((3,)),
            dma((3,)),
            dma((4,)),
            dma((4,)),
            dma((2,)),
            dma((2,)),
        ],
        compiler_params=pltpu.CompilerParams(collective_id=0, has_side_effects=True, vmem_limit_bytes=48 * 1024 * 1024),
        name="pimd_step",
    )(
        positions,
        velocities,
        charges_in,
        species.reshape(1, BLOCK),
        neighbors,
        k_index,
        kernel.reshape(1, KVEC),
        *(t.reshape(1, SPECIES) for t in (chi, hard, bond, mass)),
    )


def solution(mesh):
    return jax.shard_map(
        step,
        mesh=mesh,
        in_specs=(
            P("beads", None, "atoms"),
            P("beads", None, "atoms"),
            P("beads", "atoms"),
            P("atoms"),
            P(None, "atoms"),
            P(),
            P(),
            P(),
            P(),
            P(),
            P(),
        ),
        out_specs=(P("beads", None, "atoms"), P("beads", None, "atoms"), P("beads", "atoms")),
        check_vma=False,
    )
```

```python
import math

import jax
import jax.numpy as jnp
from jax import lax
from jax.experimental import pallas as pl
from jax.experimental.pallas import tpu as pltpu
from jax.sharding import PartitionSpec as P

KVEC = 2048
SPECIES = 8
ATOMS = 4096
GROUP = 32
BEAD_AXIS = 8
BLOCK = 128
SLOTS = 16
HALF = SLOTS * BLOCK
TILES = 38
ROWS = TILES * 8
EXROWS = ROWS + 8

two_pi = 2.0 * math.pi
ewald_scale = 4.0 / math.sqrt(KVEC * ATOMS)
time_step = 0.05
spring_rate = 0.5

COS = (1.0, -19.7392087, 64.9393891, -85.4566583, 60.2421313, -26.4046682, 7.80013144, -1.45311232)
SIN = (6.2831853, -41.3417004, 81.6051314, -76.7030154, 42.025927, -14.8998467, 3.2381375)

MESH = pl.DeviceIdType.MESH
NT = (((1,), (1,)), ((), ()))
f32 = jnp.float32
bf16 = jnp.bfloat16


def horner(coeffs, s):
    total = coeffs[-1] * s + coeffs[-2]
    for value in coeffs[-3::-1]:
        total = total * s + value
    return total


def harmonics(row):
    n = lax.broadcasted_iota(jnp.int32, (8, row.shape[1]), 0).astype(f32) + 1.0
    turns = n * row
    r = turns - jnp.floor(turns + 0.5)
    s = r * r
    return horner(COS, s), r * horner(SIN, s)


def split(x):
    high = x.astype(bf16)
    return high, x - high.astype(f32)


def tile(x, t):
    return x[8 * t : 8 * t + 8, :]


def flip(x):
    lane = lax.broadcasted_iota(jnp.int32, x.shape, 1)
    return jnp.where(lane < 16, pltpu.roll(x, 112, 1), pltpu.roll(x, 16, 1))


def core_tile(ta, tb, a):
    return 16 * ta + 8 * tb + a


def expand(coeff):
    high, low = split(coeff)
    return (high.astype(f32) + pltpu.roll(low, 32, 1) + pltpu.roll(high.astype(f32), 64, 1)).astype(bf16)


def kernel_body(
    pos_hbm,
    vel_hbm,
    chg_hbm,
    spec_hbm,
    nbr_hbm,
    k_hbm,
    kern_hbm,
    chi_hbm,
    hard_hbm,
    bond_hbm,
    mass_hbm,
    out_ref,
    pos_s,
    vel_s,
    chg_s,
    spec_s,
    nbr_ref,
    k_ref,
    kern_ref,
    tables,
    send_s,
    buf,
    nbuf,
    utab,
    uhi,
    ulo,
    wtab,
    wst,
    acols,
    etab,
    ex_s,
    ex_r,
    factor,
    coef,
    lhs,
    phi_s,
    near_s,
    nbond_s,
    ext_s,
    fsend,
    frecv,
    halo,
    in_sem,
    s_sem,
    r_sem,
    ns_sem,
    nr_sem,
    xs_sem,
    xr_sem,
    fs_sem,
    fr_sem,
    hs_sem,
    hr_sem,
):
    me = lax.axis_index("atoms")
    bead = lax.axis_index("beads")
    x_lo = me // 16
    z = (me // 2) % 8
    core = me % 2
    quad = z // 2
    partner = x_lo * 16 + z * 2 + (1 - core)
    next_bead = (bead + 1) % BEAD_AXIS
    prev_bead = (bead + BEAD_AXIS - 1) % BEAD_AXIS

    loads = [
        pltpu.make_async_copy(source, target, in_sem.at[i])
        for i, (source, target) in enumerate(
            (
                (pos_hbm, pos_s),
                (chg_hbm, chg_s),
                (spec_hbm, spec_s),
                (chi_hbm, tables.at[0]),
                (hard_hbm, tables.at[1]),
                (bond_hbm, tables.at[2]),
                (mass_hbm, tables.at[3]),
                (nbr_hbm, nbr_ref),
                (k_hbm, k_ref),
                (kern_hbm, kern_ref),
                (vel_hbm, vel_s),
            )
        )
    ]
    for load in loads:
        load.start()

    barrier = pltpu.get_barrier_semaphore()

    def greet(k, carry):
        pl.semaphore_signal(barrier, inc=1, device_id={"atoms": (me + k) % GROUP}, device_id_type=MESH)
        return carry

    lax.fori_loop(1, GROUP, greet, 0)
    for other in (next_bead, prev_bead):
        pl.semaphore_signal(barrier, inc=1, device_id={"beads": other}, device_id_type=MESH)

    for load in loads[0:7]:
        load.wait()
    species = spec_s[...]

    def lookup(t):
        total = jnp.zeros((1, BLOCK), f32)
        for s in range(SPECIES):
            total = jnp.where(species == s, tables[t, s], total)
        return total

    chi_row, hard_row, bond_row, mass_row = (lookup(t) for t in range(4))
    for b in range(4):
        for d in range(3):
            send_s[b, d : d + 1, :] = pos_s[d, b : b + 1, :]
        send_s[b, 3:4, :] = chg_s[b : b + 1, :]
        send_s[b, 4:5, :] = chi_row
        send_s[b, 5:6, :] = hard_row
        send_s[b, 6:7, :] = bond_row
        send_s[b, 7:8, :] = bond_row
    loads[7].wait()

    pl.semaphore_wait(barrier, GROUP + 1)

    slot = z * 2 + core

    def far_dest(b, o):
        return (b >> 1) * 16 + (2 * ((quad + o) % 4) + (b & 1)) * 2 + x_lo

    def data_copy(b, o, dest):
        return pltpu.make_async_remote_copy(
            send_s.at[b], buf.at[slot], s_sem.at[4 * o + b], r_sem.at[slot], device_id={"atoms": dest}, device_id_type=MESH
        )

    def nbr_copy(b, o, dest):
        return pltpu.make_async_remote_copy(
            nbr_ref, nbuf.at[slot], ns_sem.at[4 * o + b], nr_sem.at[slot], device_id={"atoms": dest}, device_id_type=MESH
        )

    order = [(b, o) for o in (2, 1, 3, 0) for b in range(4)]
    for make, source, store, sem in (
        (data_copy, lambda b: send_s.at[b], buf, r_sem),
        (nbr_copy, lambda b: nbr_ref, nbuf, nr_sem),
    ):
        for b, o in order:
            dest = far_dest(b, o)
            if o:
                make(b, o, dest).start()
            else:

                @pl.when(dest != me)
                def _():
                    make(b, o, dest).start()

                @pl.when(dest == me)
                def _():
                    pltpu.make_async_copy(source(b), store.at[slot], sem.at[slot]).start()

    to_next = pltpu.make_async_remote_copy(
        send_s.at[3], halo.at[0], hs_sem.at[0], hr_sem.at[0], device_id={"beads": next_bead}, device_id_type=MESH
    )
    to_prev = pltpu.make_async_remote_copy(
        send_s.at[0], halo.at[1], hs_sem.at[1], hr_sem.at[1], device_id={"beads": prev_bead}, device_id_type=MESH
    )
    to_next.start()
    to_prev.start()

    for load in loads[8:]:
        load.wait()
    nx, ny, nz = (k_ref[d : d + 1, :] for d in range(3))
    ax, ay, az = jnp.abs(nx), jnp.abs(ny), jnp.abs(nz)
    code = jnp.where(
        ax > 0,
        jnp.where(ay > 0, 8 * (ax - 1) + ay - 1, 72 + ax - 1),
        jnp.where(ay > 0, 64 + ay - 1, 80),
    )
    row_hot = jnp.where(lax.broadcasted_iota(jnp.int32, (96, KVEC), 0) == code, 1.0, 0.0).astype(bf16)
    lane_code = jnp.where(az > 0, az - 1, 8)
    lane_hot = lax.broadcasted_iota(jnp.int32, (16, KVEC), 0) == lane_code
    sx, sy, sz = (jnp.where(n < 0, -1.0, 1.0) for n in (nx, ny, nz))
    weight = kern_ref[...]
    parts = [[], []]
    for j, sign in enumerate((None, -sy * sz, -sx * sz, -sx * sy)):
        value = weight if sign is None else weight * sign
        high = value.astype(bf16).astype(f32)
        for part, piece in zip(parts, (high, value - high)):
            block = jnp.where(lane_hot, piece, 0.0)
            part += [block, -block if j in (1, 2) else block]
    grid = None
    for part in parts:
        term = lax.dot_general(row_hot, jnp.concatenate(part, 0).astype(bf16), NT, preferred_element_type=f32)
        grid = term if grid is None else grid + term
    lane = lax.broadcasted_iota(jnp.int32, (96, 128), 1)
    for j in range(4):
        moved = grid if j == 0 else pltpu.roll(grid, 128 - 32 * j, 1)
        etab[j] = jnp.where(lane < 32, moved, 0.0)

    factor[...] = jnp.zeros((ROWS, 128), f32)
    first = jnp.where(lax.broadcasted_iota(jnp.int32, (8, 512), 0) == 0, 1.0, 0.0)
    zero8 = jnp.zeros((8, 512), f32)

    def arrive(step, carry):
        offset = jnp.where(step == 0, 0, jnp.where(step == 1, 1, jnp.where(step == 2, 3, 2)))
        base = ((quad + offset) % 4) * 4
        for m in range(4):
            pltpu.make_async_remote_copy(
                send_s.at[0],
                buf.at[base + m],
                s_sem.at[0],
                r_sem.at[base + m],
                device_id={"atoms": partner},
                device_id_type=MESH,
            ).wait_recv()
        rows = [jnp.concatenate([buf[base + m, r : r + 1, :] for m in range(4)], 1) for r in range(4)]
        at = pl.ds(pl.multiple_of(base * BLOCK, 512), 512)
        (cu, su), (cv, sv), (cw, sw) = (harmonics(rows[d]) for d in range(3))

        def put(t, low_tile, high_tile):
            both = jnp.concatenate([low_tile, high_tile], 0)
            utab[8 * t : 8 * t + 16, at] = both
            high, low = split(both)
            uhi[8 * t : 8 * t + 16, at] = high
            ulo[8 * t : 8 * t + 16, at] = low.astype(bf16)

        for ta, u in ((0, cu), (1, su)):
            for tb, v in ((0, cv), (1, sv)):
                for a in range(0, 8, 2):
                    put(core_tile(ta, tb, a), u[a : a + 1, :] * v, u[a + 1 : a + 2, :] * v)
        put(32, cv, sv)
        put(34, cu, su)
        put(36, first, zero8)

        w = jnp.concatenate([cw, first, sw, zero8], 0)
        wtab[:, at] = w
        whi, wlo = split(w)
        wlo = wlo.astype(bf16)
        wst[0:32, at] = whi
        wst[32:64, at] = whi
        wst[64:96, at] = wlo
        wst[96:128, at] = jnp.zeros((32, 512), bf16)
        qhi, qlo = split(w * rows[3])
        a_block = jnp.concatenate([qhi, qlo.astype(bf16), whi, wlo], 0)
        acols[:, at] = a_block
        factor[...] += lax.dot_general(uhi[:, at], a_block, NT, preferred_element_type=f32) + lax.dot_general(
            ulo[:, at], a_block, NT, preferred_element_type=f32
        )
        return carry

    lax.fori_loop(0, 4, arrive, 0)

    charge = buf[:, 3, :]
    chi = buf[:, 4, :]
    inv_hard = 1.0 / buf[:, 5, :]
    bond = buf[:, 6, :]

    def start_exchange(r, weighted):
        ex_s[r, 0:ROWS, :] = factor[...]
        ends = jnp.concatenate(
            [weighted[0:1, :], weighted[15:16, :], bond[0:1, :], bond[15:16, :], jnp.zeros((4, 128), f32)], 0
        )
        ex_s[r, ROWS:EXROWS, :] = ends
        copy = pltpu.make_async_remote_copy(
            ex_s.at[r], ex_r.at[r], xs_sem.at[r], xr_sem.at[r], device_id={"atoms": partner}, device_id_type=MESH
        )
        copy.start()
        return copy

    def mix(r, centre):
        total = ex_s[r, 0:ROWS, :] + ex_r[r, 0:ROWS, :]
        total = total + pltpu.roll(total, 96, 1)
        mean = 0.0
        if centre:
            mean = total[8 * 36 : 8 * 36 + 1, 8:9] * (1.0 / ATOMS)
            total = total - mean * pltpu.roll(total, 64, 1)
        for ta in range(2):
            for tb in range(2):
                for a in range(8):
                    here = tile(total, core_tile(ta, tb, a))
                    both = tile(total, core_tile(1 - ta, 1 - tb, a))
                    over_b = flip(tile(total, core_tile(ta, 1 - tb, a)))
                    over_a = flip(tile(total, core_tile(1 - ta, tb, a)))
                    e = [etab[j, 8 * a : 8 * a + 8, :] for j in range(4)]
                    out = e[0] * here
                    out = out + e[3] * both if ta == tb else out - e[3] * both
                    out = out + e[1] * over_b if tb == 0 else out - e[1] * over_b
                    out = out + e[2] * over_a if ta == 0 else out - e[2] * over_a
                    t = core_tile(ta, tb, a)
                    coef[8 * t : 8 * t + 8, :] = out
        for first_tile, row, j in ((32, 64, 1), (34, 72, 2)):
            e0 = etab[0, row : row + 8, :]
            ej = etab[j, row : row + 8, :]
            c, s = tile(total, first_tile), tile(total, first_tile + 1)
            coef[8 * first_tile : 8 * first_tile + 8, :] = e0 * c + ej * flip(s)
            coef[8 * first_tile + 8 : 8 * first_tile + 16, :] = e0 * s - ej * flip(c)
        coef[8 * 36 : 8 * 37, :] = etab[0, 80:88, :] * tile(total, 36)
        coef[8 * 37 : 8 * 38, :] = jnp.zeros((8, 128), f32)
        return mean

    def potential():
        lhs[0:ROWS, :] = expand(coef[...])

        for i in range(SLOTS // 2):
            at = slice(i * 256, i * 256 + 256)
            fields = jnp.dot(lhs[0:ROWS, :], wst[:, at], preferred_element_type=f32)
            total = jnp.sum((fields * utab[:, at]).reshape(TILES, 8, 256), 0)
            row = jnp.sum(total, 0, keepdims=True)
            phi_s[2 * i : 2 * i + 1, :] = row[:, 0:128]
            phi_s[2 * i + 1 : 2 * i + 2, :] = row[:, 128:256]

    lane_at = lax.broadcasted_iota(jnp.int32, (8, BLOCK), 1)

    def near_sums(blocks, out):
        for j in blocks:
            target = lane_at + nbuf[j]
            index = target & (BLOCK - 1)
            low, mid, high = (
                jnp.take_along_axis(
                    jnp.broadcast_to(ext_s[j + d : j + d + 1, :], (8, BLOCK)), index, axis=1, mode="promise_in_bounds"
                )
                for d in range(3)
            )
            got = jnp.where(target < 0, low, jnp.where(target >= BLOCK, high, mid))
            out[j : j + 1, :] = jnp.sum(got, 0, keepdims=True)

    def inner_near(own, out):
        ext_s[1:17, :] = own
        near_sums(range(1, SLOTS - 1), out)

    def outer_near(own, left, right, out):
        ext_s[0:1, :] = left
        ext_s[1:17, :] = own
        ext_s[17:18, :] = right
        near_sums((0, SLOTS - 1), out)

    def refactor(values):
        for j in range(SLOTS):
            at = slice(j * BLOCK, (j + 1) * BLOCK)
            qhi, qlo = split(wtab[:, at] * values[j : j + 1, :])
            acols[0:32, at] = qhi
            acols[32:64, at] = qlo.astype(bf16)
        factor[...] = lax.dot_general(uhi[...], acols[...], NT, preferred_element_type=f32) + lax.dot_general(
            ulo[...], acols[...], NT, preferred_element_type=f32
        )

    def relax(charge, near):
        potential_here = ewald_scale * phi_s[...]
        return 0.5 * charge + 0.5 * (-(chi + potential_here + bond * near) * inv_hard)

    weighted = bond * charge
    exchange = start_exchange(0, weighted)

    def wait_nbr(j, carry):
        pltpu.make_async_remote_copy(
            nbr_ref, nbuf.at[j], ns_sem.at[0], nr_sem.at[j], device_id={"atoms": partner}, device_id_type=MESH
        ).wait_recv()
        return carry

    lax.fori_loop(0, SLOTS, wait_nbr, 0)
    inner_near(bond, nbond_s)
    inner_near(weighted, near_s)
    exchange.wait()
    ends = ex_r[0, ROWS:EXROWS, :]
    outer_near(bond, ends[3:4, :], ends[2:3, :], nbond_s)
    outer_near(weighted, ends[1:2, :], ends[0:1, :], near_s)
    mix(0, False)
    potential()
    relaxed = relax(charge, near_s[...])

    weighted = bond * relaxed
    refactor(relaxed)
    exchange = start_exchange(1, weighted)
    inner_near(weighted, near_s)
    exchange.wait()
    ends = ex_r[1, ROWS:EXROWS, :]
    outer_near(weighted, ends[1:2, :], ends[0:1, :], near_s)
    mean = mix(1, True)
    potential()
    charge = relaxed - mean
    relaxed = relax(charge, near_s[...] - mean * nbond_s[...])

    refactor(relaxed)
    exchange = start_exchange(2, bond * relaxed)
    exchange.wait()
    mean = mix(2, True)
    near_s[...] = relaxed - mean

    lane = lax.broadcasted_iota(jnp.int32, (ROWS, 128), 1)
    number = jnp.where((lane & 15) < 8, (lane & 15) + 1, 0).astype(f32)
    slope = jnp.where(lane < 16, number, -number)
    whole = coef[...]
    lhs[0:ROWS, :] = expand(whole)
    lhs[ROWS : 2 * ROWS, :] = expand(jnp.where(lane < 32, flip(whole) * slope, 0.0))
    ones = lax.broadcasted_iota(jnp.int32, (8, 256), 0).astype(f32) + 1.0

    def force(i, carry):
        at = pl.ds(pl.multiple_of(quad * 512 + i * 256, 256), 256)
        fields = jnp.dot(lhs[...], wst[:, at], preferred_element_type=f32)
        basis = [utab[8 * t : 8 * t + 8, at] for t in range(37)]

        def plain(t):
            return fields[8 * t : 8 * t + 8, :]

        dz = basis[0] * fields[ROWS : ROWS + 8, :]
        for t in range(1, 37):
            dz = dz + basis[t] * fields[ROWS + 8 * t : ROWS + 8 * t + 8, :]
        dx = jnp.zeros((8, 256), f32)
        for a in range(8):
            term = jnp.zeros((8, 256), f32)
            for tb in range(2):
                c, s = core_tile(0, tb, a), core_tile(1, tb, a)
                term = term + basis[c] * plain(s) - basis[s] * plain(c)
            dx = dx + (a + 1.0) * term
        dx = dx + ones * (basis[34] * plain(35) - basis[35] * plain(34))
        dy = basis[32] * plain(33) - basis[33] * plain(32)
        for ta in range(2):
            for a in range(8):
                c, s = core_tile(ta, 0, a), core_tile(ta, 1, a)
                dy = dy + basis[c] * plain(s) - basis[s] * plain(c)
        dy = dy * ones
        dx, dy, dz = (jnp.sum(d, 0, keepdims=True) for d in (dx, dy, dz))
        for m in range(2):
            own = near_s[pl.ds(quad * 4 + 2 * i + m, 1), :]
            piece = slice(128 * m, 128 * m + 128)
            fsend[2 * i + m] = jnp.concatenate(
                [dx[:, piece], dy[:, piece], dz[:, piece], own, jnp.zeros((4, 128), f32)], 0
            )
        return carry

    lax.fori_loop(0, 2, force, 0)

    my_bead = 2 * x_lo + z % 2

    def force_copy(m):
        home = core * 16 + (2 * quad + (m >> 1)) * 2 + (m & 1)
        return home, pltpu.make_async_remote_copy(
            fsend.at[m], frecv.at[my_bead], fs_sem.at[m], fr_sem.at[my_bead], device_id={"atoms": home}, device_id_type=MESH
        )

    for m in range(4):
        home, copy = force_copy(m)

        @pl.when(home != me)
        def _():
            copy.start()

        @pl.when(home == me)
        def _():
            pltpu.make_async_copy(fsend.at[m], frecv.at[my_bead], fr_sem.at[my_bead]).start()

    for make in (data_copy, nbr_copy):
        for b, o in order:
            dest = far_dest(b, o)
            if o:
                make(b, o, dest).wait_send()
            else:

                @pl.when(dest != me)
                def _():
                    make(b, o, dest).wait_send()

    to_next.wait()
    to_prev.wait()
    inv_mass = 1.0 / mass_row
    for b in range(4):
        pltpu.make_async_remote_copy(
            fsend.at[0], frecv.at[b], fs_sem.at[0], fr_sem.at[b], device_id={"atoms": partner}, device_id_type=MESH
        ).wait_recv()
    charges = frecv[:, 3, :]
    out_ref[6] = charges
    for d in range(3):
        ewald_force = (-two_pi * ewald_scale) * charges * frecv[:, d, :]
        here = pos_s[d]
        before = jnp.concatenate([halo[0, d : d + 1, :], here[0:3, :]], 0)
        after = jnp.concatenate([here[1:4, :], halo[1, d : d + 1, :]], 0)
        laplace = 2.0 * here - before - after
        speed = vel_s[d] + time_step * (ewald_force * inv_mass - spring_rate * laplace)
        out_ref[3 + d] = speed
        out_ref[d] = here + time_step * speed
    for m in range(4):
        home, copy = force_copy(m)

        @pl.when(home != me)
        def _():
            copy.wait_send()


def emit_body(packed, npos_hbm, nvel_hbm, nchg_hbm, sems):
    copies = [
        pltpu.make_async_copy(source, target, sems.at[i])
        for i, (source, target) in enumerate(
            ((packed.at[0:3], npos_hbm), (packed.at[3:6], nvel_hbm), (packed.at[6], nchg_hbm))
        )
    ]
    for copy in copies:
        copy.start()
    for copy in copies:
        copy.wait()


def step(positions, velocities, charges_in, species, neighbors, k_index, kernel, chi, hard, bond, mass):
    vmem = pl.BlockSpec(memory_space=pltpu.VMEM)
    hbm = pl.BlockSpec(memory_space=pltpu.HBM)
    dma = pltpu.SemaphoreType.DMA
    packed = pl.pallas_call(
        kernel_body,
        out_shape=jax.ShapeDtypeStruct((7, 4, BLOCK), f32),
        in_specs=[hbm] * 11,
        out_specs=vmem,
        scratch_shapes=[
            pltpu.VMEM((3, 4, BLOCK), f32),
            pltpu.VMEM((3, 4, BLOCK), f32),
            pltpu.VMEM((4, BLOCK), f32),
            pltpu.VMEM((1, BLOCK), jnp.int32),
            pltpu.VMEM((8, BLOCK), jnp.int32),
            pltpu.VMEM((3, KVEC), jnp.int32),
            pltpu.VMEM((1, KVEC), f32),
            pltpu.SMEM((4, SPECIES), f32),
            pltpu.VMEM((4, 8, 128), f32),
            pltpu.VMEM((SLOTS, 8, 128), f32),
            pltpu.VMEM((SLOTS, 8, 128), jnp.int32),
            pltpu.VMEM((ROWS, HALF), f32),
            pltpu.VMEM((ROWS, HALF), bf16),
            pltpu.VMEM((ROWS, HALF), bf16),
            pltpu.VMEM((32, HALF), f32),
            pltpu.VMEM((128, HALF), bf16),
            pltpu.VMEM((128, HALF), bf16),
            pltpu.VMEM((4, 96, 128), f32),
            pltpu.VMEM((3, EXROWS, 128), f32),
            pltpu.VMEM((3, EXROWS, 128), f32),
            pltpu.VMEM((ROWS, 128), f32),
            pltpu.VMEM((ROWS, 128), f32),
            pltpu.VMEM((2 * ROWS, 128), bf16),
            pltpu.VMEM((SLOTS, 128), f32),
            pltpu.VMEM((SLOTS, 128), f32),
            pltpu.VMEM((SLOTS, 128), f32),
            pltpu.VMEM((24, 128), f32),
            pltpu.VMEM((4, 8, 128), f32),
            pltpu.VMEM((4, 8, 128), f32),
            pltpu.VMEM((2, 8, 128), f32),
            dma((11,)),
            dma((16,)),
            dma((16,)),
            dma((16,)),
            dma((16,)),
            dma((3,)),
            dma((3,)),
            dma((4,)),
            dma((4,)),
            dma((2,)),
            dma((2,)),
        ],
        compiler_params=pltpu.CompilerParams(collective_id=0, has_side_effects=True),
        name="pimd_step",
    )(
        positions.transpose(1, 0, 2),
        velocities.transpose(1, 0, 2),
        charges_in,
        species.reshape(1, BLOCK),
        neighbors,
        k_index,
        kernel.reshape(1, KVEC),
        chi,
        hard,
        bond,
        mass,
    )
    spatial = jax.ShapeDtypeStruct((3, 4, BLOCK), f32)
    new_positions, new_velocities, charges = pl.pallas_call(
        emit_body,
        out_shape=(spatial, spatial, jax.ShapeDtypeStruct((4, BLOCK), f32)),
        in_specs=[vmem],
        out_specs=(hbm, hbm, hbm),
        scratch_shapes=[dma((3,))],
        name="emit",
    )(packed)
    return new_positions.transpose(1, 0, 2), new_velocities.transpose(1, 0, 2), charges


def solution(mesh):
    return jax.shard_map(
        step,
        mesh=mesh,
        in_specs=(
            P("beads", None, "atoms"),
            P("beads", None, "atoms"),
            P("beads", "atoms"),
            P("atoms"),
            P(None, "atoms"),
            P(),
            P(),
            P(),
            P(),
            P(),
            P(),
        ),
        out_specs=(P("beads", None, "atoms"), P("beads", None, "atoms"), P("beads", "atoms")),
        check_vma=False,
    )
```

```python
import math

import jax
import jax.numpy as jnp
from jax import lax
from jax.experimental import pallas as pl
from jax.experimental.pallas import tpu as pltpu
from jax.sharding import PartitionSpec as P

KVEC = 2048
SPECIES = 8
ATOMS = 4096
BEAD_AXIS = 8
BLOCK = 128
SLOTS = 16
HALF = SLOTS * BLOCK
TILES = 38
ROWS = TILES * 8
EXROWS = ROWS + 8
REST = 6
PARTS = ((0, REST + 12, (0, 1, 2)), (REST + 12, TILES, (3, 4, 5, 6, 7)))

two_pi = 2.0 * math.pi
ewald_scale = 4.0 / math.sqrt(KVEC * ATOMS)
time_step = 0.05
spring_rate = 0.5

COS = (1.0, -19.7392087, 64.9393891, -85.4566583, 60.2421313, -26.4046682, 7.80013144, -1.45311232)
SIN = (6.2831853, -41.3417004, 81.6051314, -76.7030154, 42.025927, -14.8998467, 3.2381375)

MESH = pl.DeviceIdType.MESH
NT = (((1,), (1,)), ((), ()))
f32 = jnp.float32
bf16 = jnp.bfloat16


def horner(coeffs, s):
    total = coeffs[-1] * s + coeffs[-2]
    for value in coeffs[-3::-1]:
        total = total * s + value
    return total


def harmonics(row):
    n = lax.broadcasted_iota(jnp.int32, (8, row.shape[1]), 0).astype(f32) + 1.0
    turns = n * row
    r = turns - jnp.floor(turns + 0.5)
    s = r * r
    return horner(COS, s), r * horner(SIN, s)


def split(x):
    high = x.astype(bf16)
    return high, x - high.astype(f32)


def tile(x, t):
    return x[8 * t : 8 * t + 8, :]


def flip(x):
    return pltpu.roll(x, 16, 1)


def core_tile(ta, tb, a):
    return REST + 4 * a + 2 * ta + tb


def expand(coeff):
    high, low = split(coeff)
    group = lax.broadcasted_iota(jnp.int32, coeff.shape, 1) // 32
    return jnp.where(group == 1, low, high.astype(f32)).astype(bf16)


def kernel_body(
    pos_hbm,
    vel_hbm,
    chg_hbm,
    spec_hbm,
    nbr_hbm,
    k_hbm,
    kern_hbm,
    chi_hbm,
    hard_hbm,
    bond_hbm,
    mass_hbm,
    out_ref,
    pos_s,
    vel_s,
    chg_s,
    spec_s,
    nbr_ref,
    k_ref,
    kern_ref,
    tables,
    send_s,
    buf,
    nbuf,
    utab,
    ubf,
    wtab,
    wst,
    acols,
    etab,
    ex_s,
    ex_r,
    acc,
    gtab,
    lhs,
    phi_s,
    near_s,
    nbond_s,
    ext_s,
    fsend,
    frecv,
    halo,
    in_sem,
    s_sem,
    r_sem,
    ns_sem,
    nr_sem,
    xs_sem,
    xr_sem,
    fs_sem,
    fr_sem,
    hs_sem,
    hr_sem,
):
    me = lax.axis_index("atoms")
    bead = lax.axis_index("beads")
    x_lo = me // 16
    z = (me // 2) % 8
    core = me % 2
    quad = z // 2
    partner = x_lo * 16 + z * 2 + (1 - core)
    next_bead = (bead + 1) % BEAD_AXIS
    prev_bead = (bead + BEAD_AXIS - 1) % BEAD_AXIS

    loads = [
        pltpu.make_async_copy(source, target, in_sem.at[i])
        for i, (source, target) in enumerate(
            (
                (pos_hbm, pos_s),
                (chg_hbm, chg_s),
                (spec_hbm, spec_s),
                (chi_hbm, tables.at[0]),
                (hard_hbm, tables.at[1]),
                (bond_hbm, tables.at[2]),
                (mass_hbm, tables.at[3]),
                (nbr_hbm, nbr_ref),
                (k_hbm, k_ref),
                (kern_hbm, kern_ref),
                (vel_hbm, vel_s),
            )
        )
    ]
    for load in loads:
        load.start()

    barrier = pltpu.get_barrier_semaphore()

    def greet(x, zz, c):
        pl.semaphore_signal(barrier, inc=1, device_id={"atoms": 16 * x + 2 * zz + c}, device_id_type=MESH)

    odd = x_lo ^ core
    for o in (4, 3, 5, 2, 6, 1, 7, 0):
        zz = (z + o) % 8
        greet(1 - x_lo, zz, core)
        greet(x_lo, zz, 1 - core)
        if o:
            greet(x_lo ^ odd, zz, core ^ odd)
        else:

            @pl.when(odd == 1)
            def _():
                greet(x_lo ^ odd, zz, core ^ odd)

    for other in (next_bead, prev_bead):
        pl.semaphore_signal(barrier, inc=1, device_id={"beads": other}, device_id_type=MESH)

    for load in loads[0:7]:
        load.wait()
    species = spec_s[...]

    def lookup(t):
        total = jnp.zeros((1, BLOCK), f32)
        for s in range(SPECIES):
            total = jnp.where(species == s, tables[t, s], total)
        return total

    chi_row, hard_row, bond_row, mass_row = (lookup(t) for t in range(4))
    for b in range(4):
        for d in range(3):
            send_s[b, d : d + 1, :] = pos_s[d, b : b + 1, :]
        send_s[b, 3:4, :] = chg_s[b : b + 1, :]
        send_s[b, 4:5, :] = chi_row
        send_s[b, 5:6, :] = hard_row
        send_s[b, 6:7, :] = bond_row
        send_s[b, 7:8, :] = bond_row
    loads[7].wait()

    pl.semaphore_wait(barrier, 25 + odd)

    slot = z * 2 + core

    def far_dest(b, o):
        return (b >> 1) * 16 + (2 * ((quad + o) % 4) + (b & 1)) * 2 + x_lo

    def data_copy(b, o, dest):
        return pltpu.make_async_remote_copy(
            send_s.at[b], buf.at[slot], s_sem.at[4 * o + b], r_sem.at[slot], device_id={"atoms": dest}, device_id_type=MESH
        )

    def nbr_copy(b, o, dest):
        return pltpu.make_async_remote_copy(
            nbr_ref, nbuf.at[slot], ns_sem.at[4 * o + b], nr_sem.at[slot], device_id={"atoms": dest}, device_id_type=MESH
        )

    order = [(b, o) for o in (2, 1, 3, 0) for b in range(4)]
    for make, source, store, sem in (
        (data_copy, lambda b: send_s.at[b], buf, r_sem),
        (nbr_copy, lambda b: nbr_ref, nbuf, nr_sem),
    ):
        for b, o in order:
            dest = far_dest(b, o)
            if o:
                make(b, o, dest).start()
            else:

                @pl.when(dest != me)
                def _():
                    make(b, o, dest).start()

                @pl.when(dest == me)
                def _():
                    pltpu.make_async_copy(source(b), store.at[slot], sem.at[slot]).start()

    to_next = pltpu.make_async_remote_copy(
        send_s.at[3], halo.at[0], hs_sem.at[0], hr_sem.at[0], device_id={"beads": next_bead}, device_id_type=MESH
    )
    to_prev = pltpu.make_async_remote_copy(
        send_s.at[0], halo.at[1], hs_sem.at[1], hr_sem.at[1], device_id={"beads": prev_bead}, device_id_type=MESH
    )
    to_next.start()
    to_prev.start()

    for load in loads[8:]:
        load.wait()
    nx, ny, nz = (k_ref[d : d + 1, :] for d in range(3))
    ax, ay, az = jnp.abs(nx), jnp.abs(ny), jnp.abs(nz)
    code = jnp.where(
        ax > 0,
        jnp.where(ay > 0, 8 * (ax - 1) + ay - 1, 72 + ax - 1),
        jnp.where(ay > 0, 64 + ay - 1, 80),
    )
    row_hot = jnp.where(lax.broadcasted_iota(jnp.int32, (96, KVEC), 0) == code, 1.0, 0.0).astype(bf16)
    lane_code = jnp.where(az > 0, az - 1, 8)
    lane_hot = lax.broadcasted_iota(jnp.int32, (16, KVEC), 0) == lane_code
    sx, sy, sz = (jnp.where(n < 0, -1.0, 1.0) for n in (nx, ny, nz))
    weight = kern_ref[...]
    parts = [[], []]
    for j, sign in enumerate((None, -sy * sz, -sx * sz, -sx * sy)):
        value = weight if sign is None else weight * sign
        high = value.astype(bf16).astype(f32)
        for part, piece in zip(parts, (high, value - high)):
            block = jnp.where(lane_hot, piece, 0.0)
            part += [block, -block if j in (1, 2) else block]
    grid = None
    for part in parts:
        term = lax.dot_general(row_hot, jnp.concatenate(part, 0).astype(bf16), NT, preferred_element_type=f32)
        grid = term if grid is None else grid + term
    lane = lax.broadcasted_iota(jnp.int32, (96, 128), 1)
    for j in range(4):
        kept = jnp.where(lane // 32 == j, grid, 0.0)
        kept = kept + pltpu.roll(kept, 64, 1)
        etab[j] = kept + pltpu.roll(kept, 32, 1)

    ex_s[0, 8:EXROWS, :] = jnp.zeros((ROWS, 128), f32)
    ex_s[3, 8:EXROWS, :] = jnp.zeros((ROWS, 128), f32)
    ex_s[3, 0:8, :] = jnp.zeros((8, 128), f32)

    def ubf_rows(part):
        low, high, _ = PARTS[part]
        return slice(16 * low, 16 * high)

    def fold(part, product):
        half = 8 * (PARTS[part][1] - PARTS[part][0])
        return product[0:half, :] + product[half:, :]

    def accumulate(part, rows, at, columns):
        product = fold(part, lax.dot_general(ubf[rows, at], columns, NT, preferred_element_type=f32))
        low, high, _ = PARTS[part]
        ex_s[0, 8 + 8 * low : 8 + 8 * high, :] += product[:, 0:128]
        ex_s[3, 8 + 8 * low : 8 + 8 * high, :] += product[:, 128:256]
    first = jnp.where(lax.broadcasted_iota(jnp.int32, (8, 512), 0) == 0, 1.0, 0.0)
    zero8 = jnp.zeros((8, 512), f32)

    def arrive(step, carry):
        offset = jnp.where(step == 0, 0, jnp.where(step == 1, 1, jnp.where(step == 2, 3, 2)))
        base = ((quad + offset) % 4) * 4
        for m in range(4):
            pltpu.make_async_remote_copy(
                send_s.at[0],
                buf.at[base + m],
                s_sem.at[0],
                r_sem.at[base + m],
                device_id={"atoms": partner},
                device_id_type=MESH,
            ).wait_recv()
        rows = [jnp.concatenate([buf[base + m, r : r + 1, :] for m in range(4)], 1) for r in range(4)]
        at = pl.ds(pl.multiple_of(base * BLOCK, 512), 512)
        (cu, su), (cv, sv), (cw, sw) = (harmonics(rows[d]) for d in range(3))

        def put(t, low_tile, high_tile):
            both = jnp.concatenate([low_tile, high_tile], 0)
            utab[8 * t : 8 * t + 16, at] = both
            high, low = split(both)
            first_row = 8 * (t + (0 if t < PARTS[1][0] else PARTS[1][0]))
            ubf[first_row : first_row + 16, at] = high
            first_row += 8 * (PARTS[0][1] if t < PARTS[1][0] else TILES - PARTS[1][0])
            ubf[first_row : first_row + 16, at] = low.astype(bf16)

        put(0, first, zero8)
        put(2, cv, sv)
        put(4, cu, su)
        for a in range(8):
            for ta, u in ((0, cu), (1, su)):
                here = u[a : a + 1, :]
                put(core_tile(ta, 0, a), here * cv, here * sv)

        w = jnp.concatenate([cw, first, sw, zero8], 0)
        wtab[:, at] = w
        whi, wlo = split(w)
        wlo = wlo.astype(bf16)
        wst[0:32, at] = whi
        wst[32:64, at] = whi
        wst[64:96, at] = wlo
        wst[96:128, at] = jnp.zeros((32, 512), bf16)
        qhi, qlo = split(w * rows[3])
        qlo = qlo.astype(bf16)
        for part in range(2):
            accumulate(part, ubf_rows(part), at, jnp.concatenate([qhi, qlo, qhi, qlo, whi, wlo, whi, wlo], 0))
        return carry

    lax.fori_loop(0, 4, arrive, 0)

    charge = buf[:, 3, :]
    chi = buf[:, 4, :]
    inv_hard = 1.0 / buf[:, 5, :]
    bond = buf[:, 6, :]

    def share(r, part):
        low, high, _ = PARTS[part]
        rows = pl.ds(0, 8 + 8 * high) if part == 0 else pl.ds(8 + 8 * low, 8 * (high - low))
        return pltpu.make_async_remote_copy(
            ex_s.at[r, rows],
            ex_r.at[r, rows],
            xs_sem.at[r, part],
            xr_sem.at[r, part],
            device_id={"atoms": partner},
            device_id_type=MESH,
        )

    def put_ends(r, weighted):
        ex_s[r, 0:8, :] = jnp.concatenate(
            [weighted[0:1, :], weighted[15:16, :], bond[0:1, :], bond[15:16, :], jnp.zeros((4, 128), f32)], 0
        )

    ones_share = pltpu.make_async_remote_copy(
        ex_s.at[3], ex_r.at[3], xs_sem.at[3, 0], xr_sem.at[3, 0], device_id={"atoms": partner}, device_id_type=MESH
    )

    lane16 = lax.broadcasted_iota(jnp.int32, (16, 128), 1)
    number = jnp.where((lane16 & 15) < 8, (lane16 & 15) + 1, 0).astype(f32)
    slope = jnp.where((lane16 & 16) == 0, number, -number)

    def mix(r, part, mean, slopes):
        low, high, numbers = PARTS[part]
        rows = slice(8 + 8 * low, 8 + 8 * high)
        total = ex_s[r, rows, :] + ex_r[r, rows, :]
        total = total + pltpu.roll(total, 32, 1)
        if r > 0:
            if part == 0:
                mean = total[0:1, 8:9] * (1.0 / ATOMS)
            total = total - mean * gtab[8 * low : 8 * high, :]
        swapped = flip(total)

        def store(t, pair):
            lhs[8 * t : 8 * t + 16, :] = expand(pair)
            if slopes:
                lhs[ROWS + 8 * t : ROWS + 8 * t + 16, :] = expand(flip(pair) * slope)

        if part == 0:
            zero = jnp.zeros((8, 128), f32)
            store(0, jnp.concatenate([etab[0, 80:88, :] * tile(total, 0), zero], 0))
            for t, row, j in ((2, 64, 1), (4, 72, 2)):
                e0 = etab[0, row : row + 8, :]
                ej = etab[j, row : row + 8, :]
                pair = [
                    e0 * tile(total, t) + ej * tile(swapped, t + 1),
                    e0 * tile(total, t + 1) - ej * tile(swapped, t),
                ]
                store(t, jnp.concatenate(pair, 0))
        for a in numbers:
            e = [etab[j, 8 * a : 8 * a + 8, :] for j in range(4)]
            for ta in range(2):
                pair = []
                for tb in range(2):
                    both = tile(total, core_tile(1 - ta, 1 - tb, a) - low)
                    over_b = tile(swapped, core_tile(ta, 1 - tb, a) - low)
                    over_a = tile(swapped, core_tile(1 - ta, tb, a) - low)
                    out = e[0] * tile(total, core_tile(ta, tb, a) - low)
                    out = out + e[3] * both if ta == tb else out - e[3] * both
                    out = out + e[1] * over_b if tb == 0 else out - e[1] * over_b
                    out = out + e[2] * over_a if ta == 0 else out - e[2] * over_a
                    pair.append(out)
                store(core_tile(ta, 0, a), jnp.concatenate(pair, 0))
        return mean

    def potential(part):
        low, high, _ = PARTS[part]
        rows = slice(8 * low, 8 * high)
        for i in range(SLOTS // 2):
            at = slice(i * 256, i * 256 + 256)
            fields = jnp.dot(lhs[rows, :], wst[:, at], preferred_element_type=f32)
            sums = [None] * 4
            for t in range(low, high):
                term = tile(fields, t - low) * utab[8 * t : 8 * t + 8, at]
                sums[t % 4] = term if sums[t % 4] is None else sums[t % 4] + term
            total = (sums[0] + sums[1]) + (sums[2] + sums[3])
            if part == 0:
                acc[0, :, at] = total
            else:
                row = jnp.sum(total + acc[0, :, at], 0, keepdims=True)
                phi_s[2 * i : 2 * i + 1, :] = row[:, 0:128]
                phi_s[2 * i + 1 : 2 * i + 2, :] = row[:, 128:256]

    lane_at = lax.broadcasted_iota(jnp.int32, (8, BLOCK), 1)

    def near_sums(blocks, out):
        for j in blocks:
            target = lane_at + nbuf[j]
            index = target & (BLOCK - 1)
            low, mid, high = (
                jnp.take_along_axis(
                    jnp.broadcast_to(ext_s[j + d : j + d + 1, :], (8, BLOCK)), index, axis=1, mode="promise_in_bounds"
                )
                for d in range(3)
            )
            got = jnp.where(target < 0, low, jnp.where(target >= BLOCK, high, mid))
            out[j : j + 1, :] = jnp.sum(got, 0, keepdims=True)

    def inner_near(own, out):
        ext_s[1:17, :] = own
        near_sums(range(1, SLOTS - 1), out)

    def outer_near(own, left, right, out):
        ext_s[0:1, :] = left
        ext_s[1:17, :] = own
        ext_s[17:18, :] = right
        near_sums((0, SLOTS - 1), out)

    def refactor(r, values):
        total = None
        rows = ubf_rows(0)
        for k in range(4):
            for j in range(4 * k, 4 * k + 4):
                at = slice(j * BLOCK, (j + 1) * BLOCK)
                qhi, qlo = split(wtab[:, at] * values[j : j + 1, :])
                qlo = qlo.astype(bf16)
                acols[:, at] = jnp.concatenate([qhi, qlo, qhi, qlo], 0)
            at = slice(512 * k, 512 * k + 512)
            term = lax.dot_general(ubf[rows, at], acols[:, at], NT, preferred_element_type=f32)
            total = term if total is None else total + term
        ex_s[r, 8 : 8 + 8 * PARTS[0][1], :] = fold(0, total)
        share(r, 0).start()
        ex_s[r, 8 + 8 * PARTS[1][0] : EXROWS, :] = fold(
            1, lax.dot_general(ubf[ubf_rows(1), :], acols[...], NT, preferred_element_type=f32)
        )
        share(r, 1).start()

    def relax(charge, near):
        potential_here = ewald_scale * phi_s[...]
        return 0.5 * charge + 0.5 * (-(chi + potential_here + bond * near) * inv_hard)

    weighted = bond * charge
    put_ends(0, weighted)
    share(0, 0).start()
    share(0, 1).start()
    ones_share.start()

    def wait_nbr(j, carry):
        pltpu.make_async_remote_copy(
            nbr_ref, nbuf.at[j], ns_sem.at[0], nr_sem.at[j], device_id={"atoms": partner}, device_id_type=MESH
        ).wait_recv()
        return carry

    lax.fori_loop(0, SLOTS, wait_nbr, 0)
    inner_near(bond, nbond_s)
    inner_near(weighted, near_s)
    share(0, 0).wait()
    mix(0, 0, None, False)
    potential(0)
    ends = ex_r[0, 0:8, :]
    outer_near(bond, ends[3:4, :], ends[2:3, :], nbond_s)
    outer_near(weighted, ends[1:2, :], ends[0:1, :], near_s)
    share(0, 1).wait()
    mix(0, 1, None, False)
    potential(1)
    relaxed = relax(charge, near_s[...])
    ones_share.wait()
    weight_of_ones = ex_s[3, 8:EXROWS, :] + ex_r[3, 8:EXROWS, :]
    gtab[...] = weight_of_ones + pltpu.roll(weight_of_ones, 32, 1)

    weighted = bond * relaxed
    put_ends(1, weighted)
    refactor(1, relaxed)
    inner_near(weighted, near_s)
    share(1, 0).wait()
    mean = mix(1, 0, None, False)
    potential(0)
    ends = ex_r[1, 0:8, :]
    outer_near(weighted, ends[1:2, :], ends[0:1, :], near_s)
    share(1, 1).wait()
    mix(1, 1, mean, False)
    potential(1)
    charge = relaxed - mean
    relaxed = relax(charge, near_s[...] - mean * nbond_s[...])

    put_ends(2, relaxed)
    refactor(2, relaxed)

    ones = lax.broadcasted_iota(jnp.int32, (8, 256), 0).astype(f32) + 1.0

    def force(part):
        low, high, numbers = PARTS[part]
        for i in range(2):
            at = pl.ds(pl.multiple_of(quad * 512 + i * 256, 256), 256)
            keep = slice(i * 256, i * 256 + 256)
            plain = jnp.dot(lhs[8 * low : 8 * high, :], wst[:, at], preferred_element_type=f32)
            sloped = jnp.dot(lhs[ROWS + 8 * low : ROWS + 8 * high, :], wst[:, at], preferred_element_type=f32)
            basis = {t: utab[8 * t : 8 * t + 8, at] for t in range(low, high)}
            f = {t: tile(plain, t - low) for t in range(low, high)}
            dz = [None] * 4
            for t in range(low, high):
                term = basis[t] * tile(sloped, t - low)
                dz[t % 4] = term if dz[t % 4] is None else dz[t % 4] + term
            dz = (dz[0] + dz[1]) + (dz[2] + dz[3])

            def turn(c, s):
                return basis[c] * f[s] - basis[s] * f[c]

            dx = dy = None
            for a in numbers:
                along_x = turn(core_tile(0, 0, a), core_tile(1, 0, a)) + turn(core_tile(0, 1, a), core_tile(1, 1, a))
                along_y = turn(core_tile(0, 0, a), core_tile(0, 1, a)) + turn(core_tile(1, 0, a), core_tile(1, 1, a))
                along_x = (a + 1.0) * along_x
                dx = along_x if dx is None else dx + along_x
                dy = along_y if dy is None else dy + along_y
            if part == 0:
                acc[0, :, keep] = dx + ones * turn(4, 5)
                acc[1, :, keep] = ones * (dy + turn(2, 3))
                acc[2, :, keep] = dz
            else:
                dx = dx + acc[0, :, keep]
                dy = ones * dy + acc[1, :, keep]
                dz = dz + acc[2, :, keep]
                dx, dy, dz = (jnp.sum(d, 0, keepdims=True) for d in (dx, dy, dz))
                for m in range(2):
                    own = near_s[pl.ds(quad * 4 + 2 * i + m, 1), :]
                    piece = slice(128 * m, 128 * m + 128)
                    fsend[2 * i + m] = jnp.concatenate(
                        [dx[:, piece], dy[:, piece], dz[:, piece], own, jnp.zeros((4, 128), f32)], 0
                    )

    share(2, 0).wait()
    mean = mix(2, 0, None, True)
    near_s[...] = relaxed - mean
    force(0)
    share(2, 1).wait()
    mix(2, 1, mean, True)
    force(1)

    my_bead = 2 * x_lo + z % 2

    def force_copy(m):
        home = core * 16 + (2 * quad + (m >> 1)) * 2 + (m & 1)
        return home, pltpu.make_async_remote_copy(
            fsend.at[m], frecv.at[my_bead], fs_sem.at[m], fr_sem.at[my_bead], device_id={"atoms": home}, device_id_type=MESH
        )

    for m in range(4):
        home, copy = force_copy(m)

        @pl.when(home != me)
        def _():
            copy.start()

        @pl.when(home == me)
        def _():
            pltpu.make_async_copy(fsend.at[m], frecv.at[my_bead], fr_sem.at[my_bead]).start()

    for make in (data_copy, nbr_copy):
        for b, o in order:
            dest = far_dest(b, o)
            if o:
                make(b, o, dest).wait_send()
            else:

                @pl.when(dest != me)
                def _():
                    make(b, o, dest).wait_send()

    to_next.wait()
    to_prev.wait()
    inv_mass = 1.0 / mass_row
    for b in range(4):
        pltpu.make_async_remote_copy(
            fsend.at[0], frecv.at[b], fs_sem.at[0], fr_sem.at[b], device_id={"atoms": partner}, device_id_type=MESH
        ).wait_recv()
    charges = frecv[:, 3, :]
    out_ref[6] = charges
    for d in range(3):
        ewald_force = (-two_pi * ewald_scale) * charges * frecv[:, d, :]
        here = pos_s[d]
        before = jnp.concatenate([halo[0, d : d + 1, :], here[0:3, :]], 0)
        after = jnp.concatenate([here[1:4, :], halo[1, d : d + 1, :]], 0)
        laplace = 2.0 * here - before - after
        speed = vel_s[d] + time_step * (ewald_force * inv_mass - spring_rate * laplace)
        out_ref[3 + d] = speed
        out_ref[d] = here + time_step * speed
    for m in range(4):
        home, copy = force_copy(m)

        @pl.when(home != me)
        def _():
            copy.wait_send()


def emit_body(packed, npos_hbm, nvel_hbm, nchg_hbm, sems):
    copies = [
        pltpu.make_async_copy(source, target, sems.at[i])
        for i, (source, target) in enumerate(
            ((packed.at[0:3], npos_hbm), (packed.at[3:6], nvel_hbm), (packed.at[6], nchg_hbm))
        )
    ]
    for copy in copies:
        copy.start()
    for copy in copies:
        copy.wait()


def step(positions, velocities, charges_in, species, neighbors, k_index, kernel, chi, hard, bond, mass):
    vmem = pl.BlockSpec(memory_space=pltpu.VMEM)
    hbm = pl.BlockSpec(memory_space=pltpu.HBM)
    dma = pltpu.SemaphoreType.DMA
    packed = pl.pallas_call(
        kernel_body,
        out_shape=pltpu.VMEM((7, 4, BLOCK), f32),
        in_specs=[hbm] * 11,
        out_specs=vmem,
        scratch_shapes=[
            pltpu.VMEM((3, 4, BLOCK), f32),
            pltpu.VMEM((3, 4, BLOCK), f32),
            pltpu.VMEM((4, BLOCK), f32),
            pltpu.VMEM((1, BLOCK), jnp.int32),
            pltpu.VMEM((8, BLOCK), jnp.int32),
            pltpu.VMEM((3, KVEC), jnp.int32),
            pltpu.VMEM((1, KVEC), f32),
            pltpu.SMEM((4, SPECIES), f32),
            pltpu.VMEM((4, 8, 128), f32),
            pltpu.VMEM((SLOTS, 8, 128), f32),
            pltpu.VMEM((SLOTS, 8, 128), jnp.int32),
            pltpu.VMEM((ROWS, HALF), f32),
            pltpu.VMEM((2 * ROWS, HALF), bf16),
            pltpu.VMEM((32, HALF), f32),
            pltpu.VMEM((128, HALF), bf16),
            pltpu.VMEM((128, HALF), bf16),
            pltpu.VMEM((4, 96, 128), f32),
            pltpu.VMEM((4, EXROWS, 128), f32),
            pltpu.VMEM((4, EXROWS, 128), f32),
            pltpu.VMEM((3, 8, HALF), f32),
            pltpu.VMEM((ROWS, 128), f32),
            pltpu.VMEM((2 * ROWS, 128), bf16),
            pltpu.VMEM((SLOTS, 128), f32),
            pltpu.VMEM((SLOTS, 128), f32),
            pltpu.VMEM((SLOTS, 128), f32),
            pltpu.VMEM((24, 128), f32),
            pltpu.VMEM((4, 8, 128), f32),
            pltpu.VMEM((4, 8, 128), f32),
            pltpu.VMEM((2, 8, 128), f32),
            dma((11,)),
            dma((16,)),
            dma((16,)),
            dma((16,)),
            dma((16,)),
            dma((4, 2)),
            dma((4, 2)),
            dma((4,)),
            dma((4,)),
            dma((2,)),
            dma((2,)),
        ],
        compiler_params=pltpu.CompilerParams(collective_id=0, has_side_effects=True),
        name="pimd_step",
    )(
        positions.transpose(1, 0, 2),
        velocities.transpose(1, 0, 2),
        charges_in,
        species.reshape(1, BLOCK),
        neighbors,
        k_index,
        kernel.reshape(1, KVEC),
        chi,
        hard,
        bond,
        mass,
    )
    spatial = jax.ShapeDtypeStruct((3, 4, BLOCK), f32)
    new_positions, new_velocities, charges = pl.pallas_call(
        emit_body,
        out_shape=(spatial, spatial, jax.ShapeDtypeStruct((4, BLOCK), f32)),
        in_specs=[vmem],
        out_specs=(hbm, hbm, hbm),
        scratch_shapes=[dma((3,))],
        name="emit",
    )(pltpu.with_memory_space_constraint(packed, pltpu.VMEM))
    return new_positions.transpose(1, 0, 2), new_velocities.transpose(1, 0, 2), charges


def solution(mesh):
    return jax.shard_map(
        step,
        mesh=mesh,
        in_specs=(
            P("beads", None, "atoms"),
            P("beads", None, "atoms"),
            P("beads", "atoms"),
            P("atoms"),
            P(None, "atoms"),
            P(),
            P(),
            P(),
            P(),
            P(),
            P(),
        ),
        out_specs=(P("beads", None, "atoms"), P("beads", None, "atoms"), P("beads", "atoms")),
        check_vma=False,
    )
```

```python
import math

import jax
import jax.numpy as jnp
from jax import lax
from jax.experimental import pallas as pl
from jax.experimental.pallas import tpu as pltpu
from jax.sharding import PartitionSpec as P

KVEC = 2048
SPECIES = 8
ATOMS = 4096
BEAD_AXIS = 8
BLOCK = 128
SLOTS = 16
HALF = SLOTS * BLOCK
TILES = 38
ROWS = TILES * 8
GROWS = 176
EXROWS = GROWS + 8
REST = 6
PARTS = ((0, REST + 12, (0, 1, 2)), (REST + 12, TILES, (3, 4, 5, 6, 7)))
GPARTS = ((0, REST + 4), (REST + 4, GROWS // 8))

two_pi = 2.0 * math.pi
ewald_scale = 4.0 / math.sqrt(KVEC * ATOMS)
time_step = 0.05
spring_rate = 0.5

COS = (1.0, -19.7392087, 64.9393891, -85.4566583, 60.2421313, -26.4046682, 7.80013144, -1.45311232)
SIN = (6.2831853, -41.3417004, 81.6051314, -76.7030154, 42.025927, -14.8998467, 3.2381375)

MESH = pl.DeviceIdType.MESH
NT = (((1,), (1,)), ((), ()))
f32 = jnp.float32
bf16 = jnp.bfloat16


def horner(coeffs, s):
    total = coeffs[-1] * s + coeffs[-2]
    for value in coeffs[-3::-1]:
        total = total * s + value
    return total


def harmonics(row):
    n = lax.broadcasted_iota(jnp.int32, (8, row.shape[1]), 0).astype(f32) + 1.0
    turns = n * row
    r = turns - jnp.floor(turns + 0.5)
    s = r * r
    return horner(COS, s), r * horner(SIN, s)


def split(x):
    high = x.astype(bf16)
    return high, x - high.astype(f32)


def tile(x, t):
    return x[8 * t : 8 * t + 8, :]


def flip(x):
    return pltpu.roll(x, 16, 1)


def core_tile(ta, tb, a):
    return REST + 4 * a + 2 * ta + tb


def expand(coeff):
    high, low = split(coeff)
    group = lax.broadcasted_iota(jnp.int32, coeff.shape, 1) // 32
    return jnp.where(group == 1, low, high.astype(f32)).astype(bf16)


def kernel_body(
    pos_hbm,
    vel_hbm,
    chg_hbm,
    spec_hbm,
    nbr_hbm,
    k_hbm,
    kern_hbm,
    chi_hbm,
    hard_hbm,
    bond_hbm,
    mass_hbm,
    out_ref,
    pos_s,
    vel_s,
    chg_s,
    spec_s,
    nbr_ref,
    k_ref,
    kern_ref,
    tables,
    send_s,
    buf,
    nbuf,
    utab,
    gbf,
    gone,
    wcol,
    wst,
    etab,
    ex_s,
    ex_r,
    acc,
    gtab,
    lhs,
    phi_s,
    near_s,
    nbond_s,
    ext_s,
    fsend,
    frecv,
    halo,
    in_sem,
    s_sem,
    r_sem,
    ns_sem,
    nr_sem,
    xs_sem,
    xr_sem,
    fs_sem,
    fr_sem,
    hs_sem,
    hr_sem,
):
    me = lax.axis_index("atoms")
    bead = lax.axis_index("beads")
    x_lo = me // 16
    z = (me // 2) % 8
    core = me % 2
    quad = z // 2
    partner = x_lo * 16 + z * 2 + (1 - core)
    next_bead = (bead + 1) % BEAD_AXIS
    prev_bead = (bead + BEAD_AXIS - 1) % BEAD_AXIS

    barrier = pltpu.get_barrier_semaphore()

    def greet(x, zz, c):
        pl.semaphore_signal(barrier, inc=1, device_id={"atoms": 16 * x + 2 * zz + c}, device_id_type=MESH)

    odd = x_lo ^ core
    for o in (4, 3, 5, 2, 6, 1, 7, 0):
        zz = (z + o) % 8
        greet(1 - x_lo, zz, core)
        greet(x_lo, zz, 1 - core)
        if o:
            greet(x_lo ^ odd, zz, core ^ odd)
        else:

            @pl.when(odd == 1)
            def _():
                greet(x_lo ^ odd, zz, core ^ odd)

    for other in (next_bead, prev_bead):
        pl.semaphore_signal(barrier, inc=1, device_id={"beads": other}, device_id_type=MESH)

    loads = [
        pltpu.make_async_copy(source, target, in_sem.at[i])
        for i, (source, target) in enumerate(
            (
                (pos_hbm, pos_s),
                (chg_hbm, chg_s),
                (spec_hbm, spec_s),
                (chi_hbm, tables.at[0]),
                (hard_hbm, tables.at[1]),
                (bond_hbm, tables.at[2]),
                (mass_hbm, tables.at[3]),
                (nbr_hbm, nbr_ref),
                (k_hbm, k_ref),
                (kern_hbm, kern_ref),
                (vel_hbm, vel_s),
            )
        )
    ]
    for load in loads:
        load.start()

    for load in loads[0:7]:
        load.wait()
    species = spec_s[...]

    def lookup(t):
        total = jnp.zeros((1, BLOCK), f32)
        for s in range(SPECIES):
            total = jnp.where(species == s, tables[t, s], total)
        return total

    chi_row, hard_row, bond_row, mass_row = (lookup(t) for t in range(4))
    for b in range(4):
        for d in range(3):
            send_s[b, d : d + 1, :] = pos_s[d, b : b + 1, :]
        send_s[b, 3:4, :] = chg_s[b : b + 1, :]
        send_s[b, 4:5, :] = chi_row
        send_s[b, 5:6, :] = hard_row
        send_s[b, 6:7, :] = bond_row
        send_s[b, 7:8, :] = bond_row
    loads[7].wait()

    pl.semaphore_wait(barrier, 25 + odd)

    slot = z * 2 + core

    def far_dest(b, o):
        return (b >> 1) * 16 + (2 * ((quad + o) % 4) + (b & 1)) * 2 + x_lo

    def data_copy(b, o, dest):
        return pltpu.make_async_remote_copy(
            send_s.at[b], buf.at[slot], s_sem.at[4 * o + b], r_sem.at[slot], device_id={"atoms": dest}, device_id_type=MESH
        )

    def nbr_copy(b, o, dest):
        return pltpu.make_async_remote_copy(
            nbr_ref, nbuf.at[slot], ns_sem.at[4 * o + b], nr_sem.at[slot], device_id={"atoms": dest}, device_id_type=MESH
        )

    order = [(b, o) for o in (2, 1, 3, 0) for b in range(4)]
    for make, source, store, sem in (
        (data_copy, lambda b: send_s.at[b], buf, r_sem),
        (nbr_copy, lambda b: nbr_ref, nbuf, nr_sem),
    ):
        for b, o in order:
            dest = far_dest(b, o)
            if o:
                make(b, o, dest).start()
            else:

                @pl.when(dest != me)
                def _():
                    make(b, o, dest).start()

                @pl.when(dest == me)
                def _():
                    pltpu.make_async_copy(source(b), store.at[slot], sem.at[slot]).start()

    to_next = pltpu.make_async_remote_copy(
        send_s.at[3], halo.at[0], hs_sem.at[0], hr_sem.at[0], device_id={"beads": next_bead}, device_id_type=MESH
    )
    to_prev = pltpu.make_async_remote_copy(
        send_s.at[0], halo.at[1], hs_sem.at[1], hr_sem.at[1], device_id={"beads": prev_bead}, device_id_type=MESH
    )
    to_next.start()
    to_prev.start()

    for load in loads[8:]:
        load.wait()
    nx, ny, nz = (k_ref[d : d + 1, :] for d in range(3))
    ax, ay, az = jnp.abs(nx), jnp.abs(ny), jnp.abs(nz)
    code = jnp.where(
        ax > 0,
        jnp.where(ay > 0, 8 * (ax - 1) + ay - 1, 72 + ax - 1),
        jnp.where(ay > 0, 64 + ay - 1, 80),
    )
    row_hot = jnp.where(lax.broadcasted_iota(jnp.int32, (96, KVEC), 0) == code, 1.0, 0.0).astype(bf16)
    lane_code = jnp.where(az > 0, az - 1, 8)
    lane_hot = lax.broadcasted_iota(jnp.int32, (16, KVEC), 0) == lane_code
    sx, sy, sz = (jnp.where(n < 0, -1.0, 1.0) for n in (nx, ny, nz))
    weight = kern_ref[...]
    parts = [[], []]
    for j, sign in enumerate((None, -sy * sz, -sx * sz, -sx * sy)):
        value = weight if sign is None else weight * sign
        high = value.astype(bf16).astype(f32)
        for part, piece in zip(parts, (high, value - high)):
            block = jnp.where(lane_hot, piece, 0.0)
            part += [block, -block if j in (1, 2) else block]
    grid = None
    for part in parts:
        term = lax.dot_general(row_hot, jnp.concatenate(part, 0).astype(bf16), NT, preferred_element_type=f32)
        grid = term if grid is None else grid + term
    lane = lax.broadcasted_iota(jnp.int32, (96, 128), 1)
    for j in range(4):
        kept = jnp.where(lane // 32 == j, grid, 0.0)
        kept = kept + pltpu.roll(kept, 64, 1)
        etab[j] = kept + pltpu.roll(kept, 32, 1)

    ex_s[0] = jnp.zeros((EXROWS, 256), f32)
    ex_s[3] = jnp.zeros((EXROWS, 256), f32)
    ex_s[1, 0:8, :] = jnp.zeros((8, 256), f32)
    ex_s[2, 0:8, :] = jnp.zeros((8, 256), f32)

    def gbf_rows(part):
        low, high = GPARTS[part]
        return slice(16 * low, 16 * high)

    def ex_rows(part):
        low, high = GPARTS[part]
        return slice(8 + 8 * low, 8 + 8 * high)

    def columns(values):
        high, low = split(values)
        high = high.astype(f32)
        pieces = [high[0:64], low[0:64], high[64:96], low[64:96], high[64:96], low[64:96]]
        return jnp.concatenate(pieces, 0)

    def put_split(target, g, at, both):
        part = 0 if g < GPARTS[0][1] else 1
        low, high = GPARTS[part]
        row = 8 * (g + low)
        ghigh, glow = split(both)
        target[row : row + 16, at] = ghigh
        row += 8 * (high - low)
        target[row : row + 16, at] = glow.astype(bf16)

    def fold(product):
        half = product.shape[0] // 2
        return product[0:half, :] + product[half:, :]

    first = jnp.where(lax.broadcasted_iota(jnp.int32, (8, 512), 0) == 0, 1.0, 0.0)
    zero8 = jnp.zeros((8, 512), f32)

    def arrive(step, carry):
        offset = jnp.where(step == 0, 0, jnp.where(step == 1, 1, jnp.where(step == 2, 3, 2)))
        base = ((quad + offset) % 4) * 4
        for m in range(4):
            pltpu.make_async_remote_copy(
                send_s.at[0],
                buf.at[base + m],
                s_sem.at[0],
                r_sem.at[base + m],
                device_id={"atoms": partner},
                device_id_type=MESH,
            ).wait_recv()
        rows = [jnp.concatenate([buf[base + m, r : r + 1, :] for m in range(4)], 1) for r in range(4)]
        at = pl.ds(pl.multiple_of(base * BLOCK, 512), 512)
        (cu, su), (cv, sv), (cw, sw) = (harmonics(rows[d]) for d in range(3))

        def put(t, low_tile, high_tile, g):
            both = jnp.concatenate([low_tile, high_tile], 0)
            utab[8 * t : 8 * t + 16, at] = both
            if g is not None:
                put_split(gbf, g, at, both * rows[3])
                put_split(gone, g, slice(None), both)

        put(0, first, zero8, 0)
        put(2, cv, sv, 2)
        put(4, cu, su, 4)
        for a in range(8):
            for ta, u in ((0, cu), (1, su)):
                here = u[a : a + 1, :]
                put(core_tile(ta, 0, a), here * cv, here * sv, REST + 2 * (a - 1) + 2 * ta if a % 2 else None)

        w = jnp.concatenate([cw, first, sw, zero8], 0)
        whi, wlo = split(w)
        w3 = jnp.concatenate([w, w * cu[0:1, :], w * su[0:1, :]], 0)
        wcol[at, :] = columns(w3).T.astype(bf16)
        wlo = wlo.astype(bf16)
        wst[0:32, at] = whi
        wst[32:64, at] = whi
        wst[64:96, at] = wlo
        wst[96:128, at] = jnp.zeros((32, 512), bf16)
        for part in range(2):
            mine = gbf_rows(part)
            ex_s[0, ex_rows(part), :] += fold(jnp.dot(gbf[mine, at], wcol[at, :], preferred_element_type=f32))
            ex_s[3, ex_rows(part), :] += fold(jnp.dot(gone[mine, :], wcol[at, :], preferred_element_type=f32))
        return carry

    lax.fori_loop(0, 4, arrive, 0)

    charge = buf[:, 3, :]
    chi = buf[:, 4, :]
    inv_hard = 1.0 / buf[:, 5, :]
    bond = buf[:, 6, :]

    def share(r, part):
        low, high = GPARTS[part]
        rows = pl.ds(0, 8 + 8 * high) if part == 0 else pl.ds(8 + 8 * low, 8 * (high - low))
        return pltpu.make_async_remote_copy(
            ex_s.at[r, rows],
            ex_r.at[r, rows],
            xs_sem.at[r, part],
            xr_sem.at[r, part],
            device_id={"atoms": partner},
            device_id_type=MESH,
        )

    def put_ends(r, weighted):
        ex_s[r, 0:8, 0:128] = jnp.concatenate(
            [weighted[0:1, :], weighted[15:16, :], bond[0:1, :], bond[15:16, :], jnp.zeros((4, 128), f32)], 0
        )

    ones_share = pltpu.make_async_remote_copy(
        ex_s.at[3], ex_r.at[3], xs_sem.at[3, 0], xr_sem.at[3, 0], device_id={"atoms": partner}, device_id_type=MESH
    )

    lane16 = lax.broadcasted_iota(jnp.int32, (16, 128), 1)
    number = jnp.where((lane16 & 15) < 8, (lane16 & 15) + 1, 0).astype(f32)
    slope = jnp.where((lane16 & 16) == 0, number, -number)

    def tensor(r, part):
        rows = ex_rows(part)
        sums = ex_s[r, rows, :] + ex_r[r, rows, :]
        plain, sines = sums[:, 0:128], sums[:, 128:256]
        plain = plain + pltpu.roll(plain, 64, 1)
        moved = pltpu.roll(plain, 32, 1)
        even = (lax.broadcasted_iota(jnp.int32, plain.shape, 1) & 32) == 0
        ones, cosines = jnp.where(even, plain, moved), jnp.where(even, moved, plain)
        sines = sines + pltpu.roll(sines, 32, 1)
        tiles = []
        base = 0
        if part == 0:
            tiles += [ones[0 : 8 * REST, :], cosines[16:32, :], sines[16:32, :]]
            base = REST
        for n in range(base, rows.stop // 8 - rows.start // 8, 4):
            both = slice(8 * n, 8 * n + 32)
            c, s = slice(8 * n, 8 * n + 16), slice(8 * n + 16, 8 * n + 32)
            tiles += [ones[both, :], cosines[c, :] - sines[s, :], cosines[s, :] + sines[c, :]]
        size = 8 * (PARTS[part][1] - PARTS[part][0])
        return jnp.concatenate(tiles, 0)[0:size, :]

    def mix(r, part, mean, slopes):
        low, high, numbers = PARTS[part]
        total = tensor(r, part)
        if r > 0:
            if part == 0:
                mean = total[0:1, 8:9] * (1.0 / ATOMS)
            total = total - mean * gtab[8 * low : 8 * high, :]
        swapped = flip(total)

        def store(t, pair):
            lhs[8 * t : 8 * t + 16, :] = expand(pair)
            if slopes:
                lhs[ROWS + 8 * t : ROWS + 8 * t + 16, :] = expand(flip(pair) * slope)

        if part == 0:
            zero = jnp.zeros((8, 128), f32)
            store(0, jnp.concatenate([etab[0, 80:88, :] * tile(total, 0), zero], 0))
            for t, row, j in ((2, 64, 1), (4, 72, 2)):
                e0 = etab[0, row : row + 8, :]
                ej = etab[j, row : row + 8, :]
                pair = [
                    e0 * tile(total, t) + ej * tile(swapped, t + 1),
                    e0 * tile(total, t + 1) - ej * tile(swapped, t),
                ]
                store(t, jnp.concatenate(pair, 0))
        for a in numbers:
            e = [etab[j, 8 * a : 8 * a + 8, :] for j in range(4)]
            for ta in range(2):
                pair = []
                for tb in range(2):
                    both = tile(total, core_tile(1 - ta, 1 - tb, a) - low)
                    over_b = tile(swapped, core_tile(ta, 1 - tb, a) - low)
                    over_a = tile(swapped, core_tile(1 - ta, tb, a) - low)
                    out = e[0] * tile(total, core_tile(ta, tb, a) - low)
                    out = out + e[3] * both if ta == tb else out - e[3] * both
                    out = out + e[1] * over_b if tb == 0 else out - e[1] * over_b
                    out = out + e[2] * over_a if ta == 0 else out - e[2] * over_a
                    pair.append(out)
                store(core_tile(ta, 0, a), jnp.concatenate(pair, 0))
        return mean

    def potential(part):
        low, high, _ = PARTS[part]
        rows = slice(8 * low, 8 * high)
        for i in range(SLOTS // 2):
            at = slice(i * 256, i * 256 + 256)
            fields = jnp.dot(lhs[rows, :], wst[:, at], preferred_element_type=f32)
            sums = [None] * 4
            for t in range(low, high):
                term = tile(fields, t - low) * utab[8 * t : 8 * t + 8, at]
                sums[t % 4] = term if sums[t % 4] is None else sums[t % 4] + term
            total = (sums[0] + sums[1]) + (sums[2] + sums[3])
            if part == 0:
                acc[0, :, at] = total
            else:
                row = jnp.sum(total + acc[0, :, at], 0, keepdims=True)
                phi_s[2 * i : 2 * i + 1, :] = row[:, 0:128]
                phi_s[2 * i + 1 : 2 * i + 2, :] = row[:, 128:256]

    lane_at = lax.broadcasted_iota(jnp.int32, (8, BLOCK), 1)

    def near_sums(blocks, out):
        for j in blocks:
            target = lane_at + nbuf[j]
            index = target & (BLOCK - 1)
            low, mid, high = (
                jnp.take_along_axis(
                    jnp.broadcast_to(ext_s[j + d : j + d + 1, :], (8, BLOCK)), index, axis=1, mode="promise_in_bounds"
                )
                for d in range(3)
            )
            got = jnp.where(target < 0, low, jnp.where(target >= BLOCK, high, mid))
            out[j : j + 1, :] = jnp.sum(got, 0, keepdims=True)

    def inner_near(own, out):
        ext_s[1:17, :] = own
        near_sums(range(1, SLOTS - 1), out)

    def outer_near(own, left, right, out):
        ext_s[0:1, :] = left
        ext_s[1:17, :] = own
        ext_s[17:18, :] = right
        near_sums((0, SLOTS - 1), out)

    def refactor(r, values):
        for part in range(2):
            for j in range(SLOTS):
                at = slice(j * BLOCK, (j + 1) * BLOCK)
                row = values[j : j + 1, :]
                for g in range(GPARTS[part][0], GPARTS[part][1], 2):
                    n, ta = (g - REST) // 4, ((g - REST) // 2) % 2
                    t = g if g < REST else core_tile(ta, 0, 2 * n + 1)
                    put_split(gbf, g, at, utab[8 * t : 8 * t + 16, at] * row)
            ex_s[r, ex_rows(part), :] = fold(jnp.dot(gbf[gbf_rows(part), :], wcol[...], preferred_element_type=f32))
            share(r, part).start()

    def relax(charge, near):
        potential_here = ewald_scale * phi_s[...]
        return 0.5 * charge + 0.5 * (-(chi + potential_here + bond * near) * inv_hard)

    weighted = bond * charge
    put_ends(0, weighted)
    share(0, 0).start()
    share(0, 1).start()
    ones_share.start()

    def wait_nbr(j, carry):
        pltpu.make_async_remote_copy(
            nbr_ref, nbuf.at[j], ns_sem.at[0], nr_sem.at[j], device_id={"atoms": partner}, device_id_type=MESH
        ).wait_recv()
        return carry

    lax.fori_loop(0, SLOTS, wait_nbr, 0)
    inner_near(bond, nbond_s)
    inner_near(weighted, near_s)
    share(0, 0).wait()
    mix(0, 0, None, False)
    potential(0)
    ends = ex_r[0, 0:8, 0:128]
    outer_near(bond, ends[3:4, :], ends[2:3, :], nbond_s)
    outer_near(weighted, ends[1:2, :], ends[0:1, :], near_s)
    share(0, 1).wait()
    mix(0, 1, None, False)
    potential(1)
    relaxed = relax(charge, near_s[...])
    ones_share.wait()
    for part in range(2):
        gtab[8 * PARTS[part][0] : 8 * PARTS[part][1], :] = tensor(3, part)

    weighted = bond * relaxed
    put_ends(1, weighted)
    refactor(1, relaxed)
    inner_near(weighted, near_s)
    share(1, 0).wait()
    mean = mix(1, 0, None, False)
    potential(0)
    ends = ex_r[1, 0:8, 0:128]
    outer_near(weighted, ends[1:2, :], ends[0:1, :], near_s)
    share(1, 1).wait()
    mix(1, 1, mean, False)
    potential(1)
    charge = relaxed - mean
    relaxed = relax(charge, near_s[...] - mean * nbond_s[...])

    put_ends(2, relaxed)
    refactor(2, relaxed)

    ones = lax.broadcasted_iota(jnp.int32, (8, 256), 0).astype(f32) + 1.0

    def force(part):
        low, high, numbers = PARTS[part]
        for i in range(2):
            at = pl.ds(pl.multiple_of(quad * 512 + i * 256, 256), 256)
            keep = slice(i * 256, i * 256 + 256)
            plain = jnp.dot(lhs[8 * low : 8 * high, :], wst[:, at], preferred_element_type=f32)
            sloped = jnp.dot(lhs[ROWS + 8 * low : ROWS + 8 * high, :], wst[:, at], preferred_element_type=f32)
            basis = {t: utab[8 * t : 8 * t + 8, at] for t in range(low, high)}
            f = {t: tile(plain, t - low) for t in range(low, high)}
            dz = [None] * 4
            for t in range(low, high):
                term = basis[t] * tile(sloped, t - low)
                dz[t % 4] = term if dz[t % 4] is None else dz[t % 4] + term
            dz = (dz[0] + dz[1]) + (dz[2] + dz[3])

            def turn(c, s):
                return basis[c] * f[s] - basis[s] * f[c]

            dx = dy = None
            for a in numbers:
                along_x = turn(core_tile(0, 0, a), core_tile(1, 0, a)) + turn(core_tile(0, 1, a), core_tile(1, 1, a))
                along_y = turn(core_tile(0, 0, a), core_tile(0, 1, a)) + turn(core_tile(1, 0, a), core_tile(1, 1, a))
                along_x = (a + 1.0) * along_x
                dx = along_x if dx is None else dx + along_x
                dy = along_y if dy is None else dy + along_y
            if part == 0:
                acc[0, :, keep] = dx + ones * turn(4, 5)
                acc[1, :, keep] = ones * (dy + turn(2, 3))
                acc[2, :, keep] = dz
            else:
                dx = dx + acc[0, :, keep]
                dy = ones * dy + acc[1, :, keep]
                dz = dz + acc[2, :, keep]
                dx, dy, dz = (jnp.sum(d, 0, keepdims=True) for d in (dx, dy, dz))
                for m in range(2):
                    own = near_s[pl.ds(quad * 4 + 2 * i + m, 1), :]
                    piece = slice(128 * m, 128 * m + 128)
                    fsend[2 * i + m] = jnp.concatenate(
                        [dx[:, piece], dy[:, piece], dz[:, piece], own, jnp.zeros((4, 128), f32)], 0
                    )

    share(2, 0).wait()
    mean = mix(2, 0, None, True)
    near_s[...] = relaxed - mean
    force(0)
    share(2, 1).wait()
    mix(2, 1, mean, True)
    force(1)

    my_bead = 2 * x_lo + z % 2

    def force_copy(m):
        home = core * 16 + (2 * quad + (m >> 1)) * 2 + (m & 1)
        return home, pltpu.make_async_remote_copy(
            fsend.at[m], frecv.at[my_bead], fs_sem.at[m], fr_sem.at[my_bead], device_id={"atoms": home}, device_id_type=MESH
        )

    for m in range(4):
        home, copy = force_copy(m)

        @pl.when(home != me)
        def _():
            copy.start()

        @pl.when(home == me)
        def _():
            pltpu.make_async_copy(fsend.at[m], frecv.at[my_bead], fr_sem.at[my_bead]).start()

    for make in (data_copy, nbr_copy):
        for b, o in order:
            dest = far_dest(b, o)
            if o:
                make(b, o, dest).wait_send()
            else:

                @pl.when(dest != me)
                def _():
                    make(b, o, dest).wait_send()

    to_next.wait()
    to_prev.wait()
    inv_mass = 1.0 / mass_row
    for b in range(4):
        pltpu.make_async_remote_copy(
            fsend.at[0], frecv.at[b], fs_sem.at[0], fr_sem.at[b], device_id={"atoms": partner}, device_id_type=MESH
        ).wait_recv()
    charges = frecv[:, 3, :]
    out_ref[6] = charges
    for d in range(3):
        ewald_force = (-two_pi * ewald_scale) * charges * frecv[:, d, :]
        here = pos_s[d]
        before = jnp.concatenate([halo[0, d : d + 1, :], here[0:3, :]], 0)
        after = jnp.concatenate([here[1:4, :], halo[1, d : d + 1, :]], 0)
        laplace = 2.0 * here - before - after
        speed = vel_s[d] + time_step * (ewald_force * inv_mass - spring_rate * laplace)
        out_ref[3 + d] = speed
        out_ref[d] = here + time_step * speed
    for m in range(4):
        home, copy = force_copy(m)

        @pl.when(home != me)
        def _():
            copy.wait_send()


def emit_body(packed, npos_hbm, nvel_hbm, nchg_hbm, sems):
    copies = [
        pltpu.make_async_copy(source, target, sems.at[i])
        for i, (source, target) in enumerate(
            ((packed.at[0:3], npos_hbm), (packed.at[3:6], nvel_hbm), (packed.at[6], nchg_hbm))
        )
    ]
    for copy in copies:
        copy.start()
    for copy in copies:
        copy.wait()


def step(positions, velocities, charges_in, species, neighbors, k_index, kernel, chi, hard, bond, mass):
    vmem = pl.BlockSpec(memory_space=pltpu.VMEM)
    hbm = pl.BlockSpec(memory_space=pltpu.HBM)
    dma = pltpu.SemaphoreType.DMA
    packed = pl.pallas_call(
        kernel_body,
        out_shape=pltpu.VMEM((7, 4, BLOCK), f32),
        in_specs=[hbm] * 11,
        out_specs=vmem,
        scratch_shapes=[
            pltpu.VMEM((3, 4, BLOCK), f32),
            pltpu.VMEM((3, 4, BLOCK), f32),
            pltpu.VMEM((4, BLOCK), f32),
            pltpu.VMEM((1, BLOCK), jnp.int32),
            pltpu.VMEM((8, BLOCK), jnp.int32),
            pltpu.VMEM((3, KVEC), jnp.int32),
            pltpu.VMEM((1, KVEC), f32),
            pltpu.SMEM((4, SPECIES), f32),
            pltpu.VMEM((4, 8, 128), f32),
            pltpu.VMEM((SLOTS, 8, 128), f32),
            pltpu.VMEM((SLOTS, 8, 128), jnp.int32),
            pltpu.VMEM((ROWS, HALF), f32),
            pltpu.VMEM((2 * GROWS, HALF), bf16),
            pltpu.VMEM((2 * GROWS, 512), bf16),
            pltpu.VMEM((HALF, 256), bf16),
            pltpu.VMEM((128, HALF), bf16),
            pltpu.VMEM((4, 96, 128), f32),
            pltpu.VMEM((4, EXROWS, 256), f32),
            pltpu.VMEM((4, EXROWS, 256), f32),
            pltpu.VMEM((3, 8, HALF), f32),
            pltpu.VMEM((ROWS, 128), f32),
            pltpu.VMEM((2 * ROWS, 128), bf16),
            pltpu.VMEM((SLOTS, 128), f32),
            pltpu.VMEM((SLOTS, 128), f32),
            pltpu.VMEM((SLOTS, 128), f32),
            pltpu.VMEM((24, 128), f32),
            pltpu.VMEM((4, 8, 128), f32),
            pltpu.VMEM((4, 8, 128), f32),
            pltpu.VMEM((2, 8, 128), f32),
            dma((11,)),
            dma((16,)),
            dma((16,)),
            dma((16,)),
            dma((16,)),
            dma((4, 2)),
            dma((4, 2)),
            dma((4,)),
            dma((4,)),
            dma((2,)),
            dma((2,)),
        ],
        compiler_params=pltpu.CompilerParams(collective_id=0, has_side_effects=True),
        name="pimd_step",
    )(
        positions.transpose(1, 0, 2),
        velocities.transpose(1, 0, 2),
        charges_in,
        species.reshape(1, BLOCK),
        neighbors,
        k_index,
        kernel.reshape(1, KVEC),
        chi,
        hard,
        bond,
        mass,
    )
    spatial = jax.ShapeDtypeStruct((3, 4, BLOCK), f32)
    new_positions, new_velocities, charges = pl.pallas_call(
        emit_body,
        out_shape=(spatial, spatial, jax.ShapeDtypeStruct((4, BLOCK), f32)),
        in_specs=[vmem],
        out_specs=(hbm, hbm, hbm),
        scratch_shapes=[dma((3,))],
        name="emit",
    )(pltpu.with_memory_space_constraint(packed, pltpu.VMEM))
    return new_positions.transpose(1, 0, 2), new_velocities.transpose(1, 0, 2), charges


def solution(mesh):
    return jax.shard_map(
        step,
        mesh=mesh,
        in_specs=(
            P("beads", None, "atoms"),
            P("beads", None, "atoms"),
            P("beads", "atoms"),
            P("atoms"),
            P(None, "atoms"),
            P(),
            P(),
            P(),
            P(),
            P(),
            P(),
        ),
        out_specs=(P("beads", None, "atoms"), P("beads", None, "atoms"), P("beads", "atoms")),
        check_vma=False,
    )
```

```python
import math

import jax
import jax.numpy as jnp
from jax import lax
from jax.experimental import pallas as pl
from jax.experimental.pallas import tpu as pltpu
from jax.sharding import PartitionSpec as P

KVEC = 2048
SPECIES = 8
ATOMS = 4096
BEAD_AXIS = 8
BLOCK = 128
SLOTS = 16
HALF = SLOTS * BLOCK
TILES = 38
ROWS = TILES * 8
GROWS = 176
EXROWS = GROWS + 8
REST = 6
PARTS = ((0, REST + 12, (0, 1, 2)), (REST + 12, TILES, (3, 4, 5, 6, 7)))
GPARTS = ((0, REST + 4), (REST + 4, GROWS // 8))

two_pi = 2.0 * math.pi
ewald_scale = 4.0 / math.sqrt(KVEC * ATOMS)
time_step = 0.05
spring_rate = 0.5

COS = (1.0, -19.7392087, 64.9393891, -85.4566583, 60.2421313, -26.4046682, 7.80013144, -1.45311232)
SIN = (6.2831853, -41.3417004, 81.6051314, -76.7030154, 42.025927, -14.8998467, 3.2381375)

MESH = pl.DeviceIdType.MESH
NT = (((1,), (1,)), ((), ()))
f32 = jnp.float32
bf16 = jnp.bfloat16


def horner(coeffs, s):
    total = coeffs[-1] * s + coeffs[-2]
    for value in coeffs[-3::-1]:
        total = total * s + value
    return total


def harmonics(row):
    n = lax.broadcasted_iota(jnp.int32, (8, row.shape[1]), 0).astype(f32) + 1.0
    turns = n * row
    r = turns - jnp.floor(turns + 0.5)
    s = r * r
    return horner(COS, s), r * horner(SIN, s)


def split(x):
    high = x.astype(bf16)
    return high, x - high.astype(f32)


def tile(x, t):
    return x[8 * t : 8 * t + 8, :]


def flip(x):
    return pltpu.roll(x, 16, 1)


def core_tile(ta, tb, a):
    return REST + 4 * a + 2 * ta + tb


def expand(coeff):
    high, low = split(coeff)
    group = lax.broadcasted_iota(jnp.int32, coeff.shape, 1) // 32
    return jnp.where(group == 1, low, high.astype(f32)).astype(bf16)


def kernel_body(
    pos_hbm,
    vel_hbm,
    chg_hbm,
    spec_hbm,
    nbr_hbm,
    k_hbm,
    kern_hbm,
    chi_hbm,
    hard_hbm,
    bond_hbm,
    mass_hbm,
    out_ref,
    pos_s,
    vel_s,
    chg_s,
    spec_s,
    nbr_ref,
    k_ref,
    kern_ref,
    tables,
    send_s,
    buf,
    nbuf,
    utab,
    gbf,
    gone,
    wcol,
    wst,
    etab,
    ex_s,
    ex_r,
    acc,
    gtab,
    lhs,
    phi_s,
    near_s,
    nbond_s,
    ext_s,
    fsend,
    frecv,
    halo,
    in_sem,
    s_sem,
    r_sem,
    ns_sem,
    nr_sem,
    xs_sem,
    xr_sem,
    fs_sem,
    fr_sem,
    hs_sem,
    hr_sem,
):
    me = lax.axis_index("atoms")
    bead = lax.axis_index("beads")
    x_lo = me // 16
    z = (me // 2) % 8
    core = me % 2
    quad = z // 2
    partner = x_lo * 16 + z * 2 + (1 - core)
    next_bead = (bead + 1) % BEAD_AXIS
    prev_bead = (bead + BEAD_AXIS - 1) % BEAD_AXIS

    barrier = pltpu.get_barrier_semaphore()

    def greet(x, zz, c):
        pl.semaphore_signal(barrier, inc=1, device_id={"atoms": 16 * x + 2 * zz + c}, device_id_type=MESH)

    odd = x_lo ^ core
    for o in (4, 3, 5, 2, 6, 1, 7, 0):
        zz = (z + o) % 8
        greet(1 - x_lo, zz, core)
        greet(x_lo, zz, 1 - core)
        if o:
            greet(x_lo ^ odd, zz, core ^ odd)
        else:

            @pl.when(odd == 1)
            def _():
                greet(x_lo ^ odd, zz, core ^ odd)

    for other in (next_bead, prev_bead):
        pl.semaphore_signal(barrier, inc=1, device_id={"beads": other}, device_id_type=MESH)

    loads = [
        pltpu.make_async_copy(source, target, in_sem.at[i])
        for i, (source, target) in enumerate(
            (
                (pos_hbm, pos_s),
                (chg_hbm, chg_s),
                (spec_hbm, spec_s),
                (chi_hbm, tables.at[0]),
                (hard_hbm, tables.at[1]),
                (bond_hbm, tables.at[2]),
                (mass_hbm, tables.at[3]),
                (nbr_hbm, nbr_ref),
                (k_hbm, k_ref),
                (kern_hbm, kern_ref),
                (vel_hbm, vel_s),
            )
        )
    ]
    for load in loads:
        load.start()

    for load in loads[0:7]:
        load.wait()
    species = spec_s[...]

    def lookup(t):
        total = jnp.zeros((1, BLOCK), f32)
        for s in range(SPECIES):
            total = jnp.where(species == s, tables[t, s], total)
        return total

    chi_row, hard_row, bond_row, mass_row = (lookup(t) for t in range(4))
    for b in range(4):
        for d in range(3):
            send_s[b, d : d + 1, :] = pos_s[d, b : b + 1, :]
        send_s[b, 3:4, :] = chg_s[b : b + 1, :]
        send_s[b, 4:5, :] = chi_row
        send_s[b, 5:6, :] = hard_row
        send_s[b, 6:7, :] = bond_row
        send_s[b, 7:8, :] = bond_row
    loads[7].wait()

    pl.semaphore_wait(barrier, 25 + odd)

    slot = z * 2 + core

    def far_dest(b, o):
        return (b >> 1) * 16 + (2 * ((quad + o) % 4) + (b & 1)) * 2 + x_lo

    def data_copy(b, o, dest):
        return pltpu.make_async_remote_copy(
            send_s.at[b], buf.at[slot], s_sem.at[4 * o + b], r_sem.at[slot], device_id={"atoms": dest}, device_id_type=MESH
        )

    def nbr_copy(b, o, dest):
        return pltpu.make_async_remote_copy(
            nbr_ref, nbuf.at[slot], ns_sem.at[4 * o + b], nr_sem.at[slot], device_id={"atoms": dest}, device_id_type=MESH
        )

    order = [(b, o) for o in (2, 1, 3, 0) for b in range(4)]
    for make, source, store, sem in (
        (data_copy, lambda b: send_s.at[b], buf, r_sem),
        (nbr_copy, lambda b: nbr_ref, nbuf, nr_sem),
    ):
        for b, o in order:
            dest = far_dest(b, o)
            if o:
                make(b, o, dest).start()
            else:

                @pl.when(dest != me)
                def _():
                    make(b, o, dest).start()

                @pl.when(dest == me)
                def _():
                    pltpu.make_async_copy(source(b), store.at[slot], sem.at[slot]).start()

    to_next = pltpu.make_async_remote_copy(
        send_s.at[3], halo.at[0], hs_sem.at[0], hr_sem.at[0], device_id={"beads": next_bead}, device_id_type=MESH
    )
    to_prev = pltpu.make_async_remote_copy(
        send_s.at[0], halo.at[1], hs_sem.at[1], hr_sem.at[1], device_id={"beads": prev_bead}, device_id_type=MESH
    )
    to_next.start()
    to_prev.start()

    for load in loads[8:]:
        load.wait()
    nx, ny, nz = (k_ref[d : d + 1, :] for d in range(3))
    ax, ay, az = jnp.abs(nx), jnp.abs(ny), jnp.abs(nz)
    code = jnp.where(
        ax > 0,
        jnp.where(ay > 0, 8 * (ax - 1) + ay - 1, 72 + ax - 1),
        jnp.where(ay > 0, 64 + ay - 1, 80),
    )
    row_hot = jnp.where(lax.broadcasted_iota(jnp.int32, (96, KVEC), 0) == code, 1.0, 0.0).astype(bf16)
    lane_code = jnp.where(az > 0, az - 1, 8)
    lane_hot = lax.broadcasted_iota(jnp.int32, (16, KVEC), 0) == lane_code
    sx, sy, sz = (jnp.where(n < 0, -1.0, 1.0) for n in (nx, ny, nz))
    weight = kern_ref[...]
    parts = [[], []]
    for j, sign in enumerate((None, -sy * sz, -sx * sz, -sx * sy)):
        value = weight if sign is None else weight * sign
        high = value.astype(bf16).astype(f32)
        for part, piece in zip(parts, (high, value - high)):
            block = jnp.where(lane_hot, piece, 0.0)
            part += [block, -block if j in (1, 2) else block]
    grid = None
    for part in parts:
        term = lax.dot_general(row_hot, jnp.concatenate(part, 0).astype(bf16), NT, preferred_element_type=f32)
        grid = term if grid is None else grid + term
    lane = lax.broadcasted_iota(jnp.int32, (96, 128), 1)
    for j in range(4):
        kept = jnp.where(lane // 32 == j, grid, 0.0)
        kept = kept + pltpu.roll(kept, 64, 1)
        etab[j] = kept + pltpu.roll(kept, 32, 1)

    ex_s[0] = jnp.zeros((EXROWS, 256), f32)
    ex_s[3] = jnp.zeros((EXROWS, 256), f32)
    ex_s[1, 0:8, :] = jnp.zeros((8, 256), f32)
    ex_s[2, 0:8, :] = jnp.zeros((8, 256), f32)

    def gbf_rows(part):
        low, high = GPARTS[part]
        return slice(16 * low, 16 * high)

    def ex_rows(part):
        low, high = GPARTS[part]
        return slice(8 + 8 * low, 8 + 8 * high)

    def columns(values):
        high, low = split(values)
        high = high.astype(f32)
        pieces = [high[0:64], low[0:64], high[64:96], low[64:96], high[64:96], low[64:96]]
        return jnp.concatenate(pieces, 0)

    def put_split(target, g, at, both):
        part = 0 if g < GPARTS[0][1] else 1
        low, high = GPARTS[part]
        row = 8 * (g + low)
        ghigh, glow = split(both)
        target[row : row + 16, at] = ghigh
        row += 8 * (high - low)
        target[row : row + 16, at] = glow.astype(bf16)

    def fold(product):
        half = product.shape[0] // 2
        return product[0:half, :] + product[half:, :]

    first = jnp.where(lax.broadcasted_iota(jnp.int32, (8, 512), 0) == 0, 1.0, 0.0)
    zero8 = jnp.zeros((8, 512), f32)

    def arrive(step, carry):
        offset = jnp.where(step == 0, 0, jnp.where(step == 1, 1, jnp.where(step == 2, 3, 2)))
        base = ((quad + offset) % 4) * 4
        for m in range(4):
            pltpu.make_async_remote_copy(
                send_s.at[0],
                buf.at[base + m],
                s_sem.at[0],
                r_sem.at[base + m],
                device_id={"atoms": partner},
                device_id_type=MESH,
            ).wait_recv()
        rows = [jnp.concatenate([buf[base + m, r : r + 1, :] for m in range(4)], 1) for r in range(4)]
        at = pl.ds(pl.multiple_of(base * BLOCK, 512), 512)
        (cu, su), (cv, sv), (cw, sw) = (harmonics(rows[d]) for d in range(3))

        def put(t, low_tile, high_tile, g):
            both = jnp.concatenate([low_tile, high_tile], 0)
            utab[8 * t : 8 * t + 16, at] = both
            if g is not None:
                put_split(gone, g, slice(None), both * rows[3])
                put_split(gone.at[2 * GROWS : 4 * GROWS], g, slice(None), both)

        put(0, first, zero8, 0)
        put(2, cv, sv, 2)
        put(4, cu, su, 4)
        for a in range(8):
            for ta, u in ((0, cu), (1, su)):
                here = u[a : a + 1, :]
                put(core_tile(ta, 0, a), here * cv, here * sv, REST + 2 * (a - 1) + 2 * ta if a % 2 else None)

        w = jnp.concatenate([cw, first, sw, zero8], 0)
        whi, wlo = split(w)
        w3 = jnp.concatenate([w, w * cu[0:1, :], w * su[0:1, :]], 0)
        wcol[at, :] = columns(w3).T.astype(bf16)
        wlo = wlo.astype(bf16)
        wst[0:32, at] = whi
        wst[32:64, at] = whi
        wst[64:96, at] = wlo
        wst[96:128, at] = jnp.zeros((32, 512), bf16)
        product = jnp.dot(gone[...], wcol[at, :], preferred_element_type=f32)
        for part in range(2):
            mine = gbf_rows(part)
            ex_s[0, ex_rows(part), :] += fold(product[mine, :])
            ex_s[3, ex_rows(part), :] += fold(product[2 * GROWS + mine.start : 2 * GROWS + mine.stop, :])
        return carry

    lax.fori_loop(0, 4, arrive, 0)

    charge = buf[:, 3, :]
    chi = buf[:, 4, :]
    inv_hard = 1.0 / buf[:, 5, :]
    bond = buf[:, 6, :]

    def share(r, part):
        low, high = GPARTS[part]
        rows = pl.ds(0, 8 + 8 * high) if part == 0 else pl.ds(8 + 8 * low, 8 * (high - low))
        return pltpu.make_async_remote_copy(
            ex_s.at[r, rows],
            ex_r.at[r, rows],
            xs_sem.at[r, part],
            xr_sem.at[r, part],
            device_id={"atoms": partner},
            device_id_type=MESH,
        )

    def put_ends(r, weighted):
        ex_s[r, 0:8, 0:128] = jnp.concatenate(
            [weighted[0:1, :], weighted[15:16, :], bond[0:1, :], bond[15:16, :], jnp.zeros((4, 128), f32)], 0
        )

    ones_share = pltpu.make_async_remote_copy(
        ex_s.at[3], ex_r.at[3], xs_sem.at[3, 0], xr_sem.at[3, 0], device_id={"atoms": partner}, device_id_type=MESH
    )

    lane16 = lax.broadcasted_iota(jnp.int32, (16, 128), 1)
    number = jnp.where((lane16 & 15) < 8, (lane16 & 15) + 1, 0).astype(f32)
    slope = jnp.where((lane16 & 16) == 0, number, -number)

    def tensor(r, part):
        rows = ex_rows(part)
        sums = ex_s[r, rows, :] + ex_r[r, rows, :]
        plain, sines = sums[:, 0:128], sums[:, 128:256]
        plain = plain + pltpu.roll(plain, 64, 1)
        moved = pltpu.roll(plain, 32, 1)
        even = (lax.broadcasted_iota(jnp.int32, plain.shape, 1) & 32) == 0
        ones, cosines = jnp.where(even, plain, moved), jnp.where(even, moved, plain)
        sines = sines + pltpu.roll(sines, 32, 1)
        tiles = []
        base = 0
        if part == 0:
            tiles += [ones[0 : 8 * REST, :], cosines[16:32, :], sines[16:32, :]]
            base = REST
        for n in range(base, rows.stop // 8 - rows.start // 8, 4):
            both = slice(8 * n, 8 * n + 32)
            c, s = slice(8 * n, 8 * n + 16), slice(8 * n + 16, 8 * n + 32)
            tiles += [ones[both, :], cosines[c, :] - sines[s, :], cosines[s, :] + sines[c, :]]
        size = 8 * (PARTS[part][1] - PARTS[part][0])
        return jnp.concatenate(tiles, 0)[0:size, :]

    def mix(r, part, mean, slopes):
        low, high, numbers = PARTS[part]
        total = tensor(r, part)
        if r > 0:
            if part == 0:
                mean = total[0:1, 8:9] * (1.0 / ATOMS)
            total = total - mean * gtab[8 * low : 8 * high, :]
        swapped = flip(total)

        def store(t, pair):
            lhs[8 * t : 8 * t + 16, :] = expand(pair)
            if slopes:
                lhs[ROWS + 8 * t : ROWS + 8 * t + 16, :] = expand(flip(pair) * slope)

        if part == 0:
            zero = jnp.zeros((8, 128), f32)
            store(0, jnp.concatenate([etab[0, 80:88, :] * tile(total, 0), zero], 0))
            for t, row, j in ((2, 64, 1), (4, 72, 2)):
                e0 = etab[0, row : row + 8, :]
                ej = etab[j, row : row + 8, :]
                pair = [
                    e0 * tile(total, t) + ej * tile(swapped, t + 1),
                    e0 * tile(total, t + 1) - ej * tile(swapped, t),
                ]
                store(t, jnp.concatenate(pair, 0))
        for a in numbers:
            e = [etab[j, 8 * a : 8 * a + 8, :] for j in range(4)]
            for ta in range(2):
                pair = []
                for tb in range(2):
                    both = tile(total, core_tile(1 - ta, 1 - tb, a) - low)
                    over_b = tile(swapped, core_tile(ta, 1 - tb, a) - low)
                    over_a = tile(swapped, core_tile(1 - ta, tb, a) - low)
                    out = e[0] * tile(total, core_tile(ta, tb, a) - low)
                    out = out + e[3] * both if ta == tb else out - e[3] * both
                    out = out + e[1] * over_b if tb == 0 else out - e[1] * over_b
                    out = out + e[2] * over_a if ta == 0 else out - e[2] * over_a
                    pair.append(out)
                store(core_tile(ta, 0, a), jnp.concatenate(pair, 0))
        return mean

    def potential(part):
        low, high, _ = PARTS[part]
        rows = slice(8 * low, 8 * high)
        for i in range(HALF // 2048):
            whole = jnp.dot(lhs[rows, :], wst[:, i * 2048 : (i + 1) * 2048], preferred_element_type=f32)
            for k in range(2048 // 256):
                at = slice(i * 2048 + k * 256, i * 2048 + k * 256 + 256)
                fields = whole[:, k * 256 : k * 256 + 256]
                sums = [None] * 4
                for t in range(low, high):
                    term = tile(fields, t - low) * utab[8 * t : 8 * t + 8, at]
                    sums[t % 4] = term if sums[t % 4] is None else sums[t % 4] + term
                total = (sums[0] + sums[1]) + (sums[2] + sums[3])
                if part == 0:
                    acc[0, :, at] = total
                else:
                    row = jnp.sum(total + acc[0, :, at], 0, keepdims=True)
                    j = (i * 2048 + k * 256) // 128
                    phi_s[j : j + 1, :] = row[:, 0:128]
                    phi_s[j + 1 : j + 2, :] = row[:, 128:256]

    lane_at = lax.broadcasted_iota(jnp.int32, (8, BLOCK), 1)

    def near_sums(blocks, out):
        for j in blocks:
            target = lane_at + nbuf[j]
            index = target & (BLOCK - 1)
            low, mid, high = (
                jnp.take_along_axis(
                    jnp.broadcast_to(ext_s[j + d : j + d + 1, :], (8, BLOCK)), index, axis=1, mode="promise_in_bounds"
                )
                for d in range(3)
            )
            got = jnp.where(target < 0, low, jnp.where(target >= BLOCK, high, mid))
            out[j : j + 1, :] = jnp.sum(got, 0, keepdims=True)

    def inner_near(own, out):
        ext_s[1:17, :] = own
        near_sums(range(1, SLOTS - 1), out)

    def outer_near(own, left, right, out):
        ext_s[0:1, :] = left
        ext_s[1:17, :] = own
        ext_s[17:18, :] = right
        near_sums((0, SLOTS - 1), out)

    def refactor(r, values):
        for part in range(2):
            for j in range(SLOTS):
                at = slice(j * BLOCK, (j + 1) * BLOCK)
                row = values[j : j + 1, :]
                for g in range(GPARTS[part][0], GPARTS[part][1], 2):
                    n, ta = (g - REST) // 4, ((g - REST) // 2) % 2
                    t = g if g < REST else core_tile(ta, 0, 2 * n + 1)
                    put_split(gbf, g, at, utab[8 * t : 8 * t + 16, at] * row)
            ex_s[r, ex_rows(part), :] = fold(jnp.dot(gbf[gbf_rows(part), :], wcol[...], preferred_element_type=f32))
            share(r, part).start()

    def relax(charge, near):
        potential_here = ewald_scale * phi_s[...]
        return 0.5 * charge + 0.5 * (-(chi + potential_here + bond * near) * inv_hard)

    weighted = bond * charge
    put_ends(0, weighted)
    share(0, 0).start()
    share(0, 1).start()
    ones_share.start()

    def wait_nbr(j, carry):
        pltpu.make_async_remote_copy(
            nbr_ref, nbuf.at[j], ns_sem.at[0], nr_sem.at[j], device_id={"atoms": partner}, device_id_type=MESH
        ).wait_recv()
        return carry

    lax.fori_loop(0, SLOTS, wait_nbr, 0)
    inner_near(bond, nbond_s)
    inner_near(weighted, near_s)
    share(0, 0).wait()
    mix(0, 0, None, False)
    potential(0)
    ends = ex_r[0, 0:8, 0:128]
    outer_near(weighted, ends[1:2, :], ends[0:1, :], near_s)
    share(0, 1).wait()
    mix(0, 1, None, False)
    potential(1)
    relaxed = relax(charge, near_s[...])

    weighted = bond * relaxed
    put_ends(1, weighted)
    refactor(1, relaxed)
    inner_near(weighted, near_s)
    ones_share.wait()
    for part in range(2):
        gtab[8 * PARTS[part][0] : 8 * PARTS[part][1], :] = tensor(3, part)
    outer_near(bond, ends[3:4, :], ends[2:3, :], nbond_s)
    share(1, 0).wait()
    mean = mix(1, 0, None, False)
    potential(0)
    ends = ex_r[1, 0:8, 0:128]
    outer_near(weighted, ends[1:2, :], ends[0:1, :], near_s)
    share(1, 1).wait()
    mix(1, 1, mean, False)
    potential(1)
    charge = relaxed - mean
    relaxed = relax(charge, near_s[...] - mean * nbond_s[...])

    put_ends(2, relaxed)
    refactor(2, relaxed)

    ones = lax.broadcasted_iota(jnp.int32, (8, 256), 0).astype(f32) + 1.0

    my_bead = 2 * x_lo + z % 2

    def force_copy(k, m):
        i = (z + 1 + k) % 2
        home = core * 16 + (2 * quad + i) * 2 + m
        return home, pltpu.make_async_remote_copy(
            fsend.at[2 * k + m],
            frecv.at[my_bead],
            fs_sem.at[2 * k + m],
            fr_sem.at[my_bead],
            device_id={"atoms": home},
            device_id_type=MESH,
        )

    def force_start(k):
        for m in range(2):
            home, copy = force_copy(k, m)
            if k == 0:
                copy.start()
            else:

                @pl.when(home != me)
                def _():
                    copy.start()

                @pl.when(home == me)
                def _():
                    pltpu.make_async_copy(fsend.at[2 * k + m], frecv.at[my_bead], fr_sem.at[my_bead]).start()

    def force(part):
        low, high, numbers = PARTS[part]
        for k in range(2):
            i = (z + 1 + k) % 2
            at = pl.ds(pl.multiple_of(quad * 512 + i * 256, 256), 256)
            keep = slice(k * 256, k * 256 + 256)
            plain = jnp.dot(lhs[8 * low : 8 * high, :], wst[:, at], preferred_element_type=f32)
            sloped = jnp.dot(lhs[ROWS + 8 * low : ROWS + 8 * high, :], wst[:, at], preferred_element_type=f32)
            basis = {t: utab[8 * t : 8 * t + 8, at] for t in range(low, high)}
            f = {t: tile(plain, t - low) for t in range(low, high)}
            dz = [None] * 4
            for t in range(low, high):
                term = basis[t] * tile(sloped, t - low)
                dz[t % 4] = term if dz[t % 4] is None else dz[t % 4] + term
            dz = (dz[0] + dz[1]) + (dz[2] + dz[3])

            def turn(c, s):
                return basis[c] * f[s] - basis[s] * f[c]

            dx = dy = None
            for a in numbers:
                along_x = turn(core_tile(0, 0, a), core_tile(1, 0, a)) + turn(core_tile(0, 1, a), core_tile(1, 1, a))
                along_y = turn(core_tile(0, 0, a), core_tile(0, 1, a)) + turn(core_tile(1, 0, a), core_tile(1, 1, a))
                along_x = (a + 1.0) * along_x
                dx = along_x if dx is None else dx + along_x
                dy = along_y if dy is None else dy + along_y
            if part == 0:
                acc[0, :, keep] = dx + ones * turn(4, 5)
                acc[1, :, keep] = ones * (dy + turn(2, 3))
                acc[2, :, keep] = dz
            else:
                dx = dx + acc[0, :, keep]
                dy = ones * dy + acc[1, :, keep]
                dz = dz + acc[2, :, keep]
                dx, dy, dz = (jnp.sum(d, 0, keepdims=True) for d in (dx, dy, dz))
                for m in range(2):
                    own = near_s[pl.ds(quad * 4 + 2 * i + m, 1), :]
                    piece = slice(128 * m, 128 * m + 128)
                    fsend[2 * k + m] = jnp.concatenate(
                        [dx[:, piece], dy[:, piece], dz[:, piece], own, jnp.zeros((4, 128), f32)], 0
                    )
                force_start(k)

    share(2, 0).wait()
    mean = mix(2, 0, None, True)
    near_s[...] = relaxed - mean
    force(0)
    share(2, 1).wait()
    mix(2, 1, mean, True)
    force(1)

    for make in (data_copy, nbr_copy):
        for b, o in order:
            dest = far_dest(b, o)
            if o:
                make(b, o, dest).wait_send()
            else:

                @pl.when(dest != me)
                def _():
                    make(b, o, dest).wait_send()

    to_next.wait()
    to_prev.wait()
    inv_mass = 1.0 / mass_row
    for b in range(4):
        pltpu.make_async_remote_copy(
            fsend.at[0], frecv.at[b], fs_sem.at[0], fr_sem.at[b], device_id={"atoms": partner}, device_id_type=MESH
        ).wait_recv()
    charges = frecv[:, 3, :]
    out_ref[6] = charges
    for d in range(3):
        ewald_force = (-two_pi * ewald_scale) * charges * frecv[:, d, :]
        here = pos_s[d]
        before = jnp.concatenate([halo[0, d : d + 1, :], here[0:3, :]], 0)
        after = jnp.concatenate([here[1:4, :], halo[1, d : d + 1, :]], 0)
        laplace = 2.0 * here - before - after
        speed = vel_s[d] + time_step * (ewald_force * inv_mass - spring_rate * laplace)
        out_ref[3 + d] = speed
        out_ref[d] = here + time_step * speed
    for k in range(2):
        for m in range(2):
            home, copy = force_copy(k, m)
            if k == 0:
                copy.wait_send()
            else:

                @pl.when(home != me)
                def _():
                    copy.wait_send()


def emit_body(packed, npos_hbm, nvel_hbm, nchg_hbm, sems):
    copies = [
        pltpu.make_async_copy(source, target, sems.at[i])
        for i, (source, target) in enumerate(
            ((packed.at[0:3], npos_hbm), (packed.at[3:6], nvel_hbm), (packed.at[6], nchg_hbm))
        )
    ]
    for copy in copies:
        copy.start()
    for copy in copies:
        copy.wait()


def step(positions, velocities, charges_in, species, neighbors, k_index, kernel, chi, hard, bond, mass):
    vmem = pl.BlockSpec(memory_space=pltpu.VMEM)
    hbm = pl.BlockSpec(memory_space=pltpu.HBM)
    dma = pltpu.SemaphoreType.DMA
    packed = pl.pallas_call(
        kernel_body,
        out_shape=pltpu.VMEM((7, 4, BLOCK), f32),
        in_specs=[hbm] * 11,
        out_specs=vmem,
        scratch_shapes=[
            pltpu.VMEM((3, 4, BLOCK), f32),
            pltpu.VMEM((3, 4, BLOCK), f32),
            pltpu.VMEM((4, BLOCK), f32),
            pltpu.VMEM((1, BLOCK), jnp.int32),
            pltpu.VMEM((8, BLOCK), jnp.int32),
            pltpu.VMEM((3, KVEC), jnp.int32),
            pltpu.VMEM((1, KVEC), f32),
            pltpu.SMEM((4, SPECIES), f32),
            pltpu.VMEM((4, 8, 128), f32),
            pltpu.VMEM((SLOTS, 8, 128), f32),
            pltpu.VMEM((SLOTS, 8, 128), jnp.int32),
            pltpu.VMEM((ROWS, HALF), f32),
            pltpu.VMEM((2 * GROWS, HALF), bf16),
            pltpu.VMEM((4 * GROWS, 512), bf16),
            pltpu.VMEM((HALF, 256), bf16),
            pltpu.VMEM((128, HALF), bf16),
            pltpu.VMEM((4, 96, 128), f32),
            pltpu.VMEM((4, EXROWS, 256), f32),
            pltpu.VMEM((4, EXROWS, 256), f32),
            pltpu.VMEM((3, 8, HALF), f32),
            pltpu.VMEM((ROWS, 128), f32),
            pltpu.VMEM((2 * ROWS, 128), bf16),
            pltpu.VMEM((SLOTS, 128), f32),
            pltpu.VMEM((SLOTS, 128), f32),
            pltpu.VMEM((SLOTS, 128), f32),
            pltpu.VMEM((24, 128), f32),
            pltpu.VMEM((4, 8, 128), f32),
            pltpu.VMEM((4, 8, 128), f32),
            pltpu.VMEM((2, 8, 128), f32),
            dma((11,)),
            dma((16,)),
            dma((16,)),
            dma((16,)),
            dma((16,)),
            dma((4, 2)),
            dma((4, 2)),
            dma((4,)),
            dma((4,)),
            dma((2,)),
            dma((2,)),
        ],
        compiler_params=pltpu.CompilerParams(collective_id=0, has_side_effects=True),
        name="pimd_step",
    )(
        positions.transpose(1, 0, 2),
        velocities.transpose(1, 0, 2),
        charges_in,
        species.reshape(1, BLOCK),
        neighbors,
        k_index,
        kernel.reshape(1, KVEC),
        chi,
        hard,
        bond,
        mass,
    )
    spatial = jax.ShapeDtypeStruct((3, 4, BLOCK), f32)
    new_positions, new_velocities, charges = pl.pallas_call(
        emit_body,
        out_shape=(spatial, spatial, jax.ShapeDtypeStruct((4, BLOCK), f32)),
        in_specs=[vmem],
        out_specs=(hbm, hbm, hbm),
        scratch_shapes=[dma((3,))],
        name="emit",
    )(pltpu.with_memory_space_constraint(packed, pltpu.VMEM))
    return new_positions.transpose(1, 0, 2), new_velocities.transpose(1, 0, 2), charges


def solution(mesh):
    return jax.shard_map(
        step,
        mesh=mesh,
        in_specs=(
            P("beads", None, "atoms"),
            P("beads", None, "atoms"),
            P("beads", "atoms"),
            P("atoms"),
            P(None, "atoms"),
            P(),
            P(),
            P(),
            P(),
            P(),
            P(),
        ),
        out_specs=(P("beads", None, "atoms"), P("beads", None, "atoms"), P("beads", "atoms")),
        check_vma=False,
    )
```

```python
import math

import jax
import jax.numpy as jnp
from jax import lax
from jax.experimental import pallas as pl
from jax.experimental.pallas import tpu as pltpu
from jax.sharding import PartitionSpec as P

KVEC = 2048
SPECIES = 8
ATOMS = 4096
BEAD_AXIS = 8
BLOCK = 128
SLOTS = 16
HALF = SLOTS * BLOCK
TILES = 38
ROWS = TILES * 8
GROWS = 176
EXROWS = GROWS + 8
REST = 6
PARTS = ((0, REST + 12, (0, 1, 2)), (REST + 12, TILES, (3, 4, 5, 6, 7)))
GPARTS = ((0, REST + 4), (REST + 4, GROWS // 8))

two_pi = 2.0 * math.pi
ewald_scale = 4.0 / math.sqrt(KVEC * ATOMS)
time_step = 0.05
spring_rate = 0.5

COS = (1.0, -19.7392087, 64.9393891, -85.4566583, 60.2421313, -26.4046682, 7.80013144, -1.45311232)
SIN = (6.2831853, -41.3417004, 81.6051314, -76.7030154, 42.025927, -14.8998467, 3.2381375)

MESH = pl.DeviceIdType.MESH
NT = (((1,), (1,)), ((), ()))
f32 = jnp.float32
bf16 = jnp.bfloat16


def horner(coeffs, s):
    total = coeffs[-1] * s + coeffs[-2]
    for value in coeffs[-3::-1]:
        total = total * s + value
    return total


def harmonics(row):
    n = lax.broadcasted_iota(jnp.int32, (8, row.shape[1]), 0).astype(f32) + 1.0
    turns = n * row
    r = turns - jnp.floor(turns + 0.5)
    s = r * r
    return horner(COS, s), r * horner(SIN, s)


def split(x):
    high = x.astype(bf16)
    return high, x - high.astype(f32)


def tile(x, t):
    return x[8 * t : 8 * t + 8, :]


def flip(x):
    return pltpu.roll(x, 16, 1)


def core_tile(ta, tb, a):
    return REST + 4 * a + 2 * ta + tb


def expand(coeff):
    high, low = split(coeff)
    group = lax.broadcasted_iota(jnp.int32, coeff.shape, 1) // 32
    return jnp.where(group == 1, low, high.astype(f32)).astype(bf16)


def kernel_body(
    pos_hbm,
    vel_hbm,
    chg_hbm,
    spec_hbm,
    nbr_hbm,
    k_hbm,
    kern_hbm,
    chi_hbm,
    hard_hbm,
    bond_hbm,
    mass_hbm,
    out_ref,
    pos_s,
    vel_s,
    chg_s,
    spec_s,
    nbr_ref,
    k_ref,
    kern_ref,
    tables,
    send_s,
    buf,
    nbuf,
    utab,
    gbf,
    gone,
    wcol,
    wst,
    etab,
    ex_s,
    ex_r,
    acc,
    gtab,
    lhs,
    phi_s,
    near_s,
    nbond_s,
    ext_s,
    fsend,
    frecv,
    halo,
    in_sem,
    s_sem,
    r_sem,
    ns_sem,
    nr_sem,
    xs_sem,
    xr_sem,
    fs_sem,
    fr_sem,
    hs_sem,
    hr_sem,
):
    me = lax.axis_index("atoms")
    bead = lax.axis_index("beads")
    x_lo = me // 16
    z = (me // 2) % 8
    core = me % 2
    quad = z // 2
    partner = x_lo * 16 + z * 2 + (1 - core)
    next_bead = (bead + 1) % BEAD_AXIS
    prev_bead = (bead + BEAD_AXIS - 1) % BEAD_AXIS

    barrier = pltpu.get_barrier_semaphore()

    def greet(x, zz, c):
        pl.semaphore_signal(barrier, inc=1, device_id={"atoms": 16 * x + 2 * zz + c}, device_id_type=MESH)

    odd = x_lo ^ core
    for o in (4, 3, 5, 2, 6, 1, 7, 0):
        zz = (z + o) % 8
        greet(1 - x_lo, zz, core)
        greet(x_lo, zz, 1 - core)
        if o:
            greet(x_lo ^ odd, zz, core ^ odd)
        else:

            @pl.when(odd == 1)
            def _():
                greet(x_lo ^ odd, zz, core ^ odd)

    for other in (next_bead, prev_bead):
        pl.semaphore_signal(barrier, inc=1, device_id={"beads": other}, device_id_type=MESH)

    loads = [
        pltpu.make_async_copy(source, target, in_sem.at[i])
        for i, (source, target) in enumerate(
            (
                (pos_hbm, pos_s),
                (chg_hbm, chg_s),
                (spec_hbm, spec_s),
                (chi_hbm, tables.at[0]),
                (hard_hbm, tables.at[1]),
                (bond_hbm, tables.at[2]),
                (mass_hbm, tables.at[3]),
                (nbr_hbm, nbr_ref),
                (k_hbm, k_ref),
                (kern_hbm, kern_ref),
                (vel_hbm, vel_s),
            )
        )
    ]
    for load in loads:
        load.start()

    for load in loads[0:7]:
        load.wait()
    species = spec_s[...]

    def lookup(t):
        total = jnp.zeros((1, BLOCK), f32)
        for s in range(SPECIES):
            total = jnp.where(species == s, tables[t, s], total)
        return total

    chi_row, hard_row, bond_row, mass_row = (lookup(t) for t in range(4))
    for b in range(4):
        for d in range(3):
            send_s[b, d : d + 1, :] = pos_s[d, b : b + 1, :]
        send_s[b, 3:4, :] = chg_s[b : b + 1, :]
        send_s[b, 4:5, :] = chi_row
        send_s[b, 5:6, :] = hard_row
        send_s[b, 6:7, :] = bond_row
        send_s[b, 7:8, :] = bond_row
    loads[7].wait()

    pl.semaphore_wait(barrier, 25 + odd)

    slot = z * 2 + core

    def far_dest(b, o):
        return (b >> 1) * 16 + (2 * ((quad + o) % 4) + (b & 1)) * 2 + x_lo

    def data_copy(b, o, dest):
        return pltpu.make_async_remote_copy(
            send_s.at[b], buf.at[slot], s_sem.at[4 * o + b], r_sem.at[slot], device_id={"atoms": dest}, device_id_type=MESH
        )

    def nbr_copy(b, o, dest):
        return pltpu.make_async_remote_copy(
            nbr_ref, nbuf.at[slot], ns_sem.at[4 * o + b], nr_sem.at[slot], device_id={"atoms": dest}, device_id_type=MESH
        )

    order = [(b, o) for o in (2, 1, 3, 0) for b in range(4)]
    for make, source, store, sem in (
        (data_copy, lambda b: send_s.at[b], buf, r_sem),
        (nbr_copy, lambda b: nbr_ref, nbuf, nr_sem),
    ):
        for b, o in order:
            dest = far_dest(b, o)
            if o:
                make(b, o, dest).start()
            else:

                @pl.when(dest != me)
                def _():
                    make(b, o, dest).start()

                @pl.when(dest == me)
                def _():
                    pltpu.make_async_copy(source(b), store.at[slot], sem.at[slot]).start()

    to_next = pltpu.make_async_remote_copy(
        send_s.at[3], halo.at[0], hs_sem.at[0], hr_sem.at[0], device_id={"beads": next_bead}, device_id_type=MESH
    )
    to_prev = pltpu.make_async_remote_copy(
        send_s.at[0], halo.at[1], hs_sem.at[1], hr_sem.at[1], device_id={"beads": prev_bead}, device_id_type=MESH
    )
    to_next.start()
    to_prev.start()

    for load in loads[8:]:
        load.wait()
    nx, ny, nz = (k_ref[d : d + 1, :] for d in range(3))
    ax, ay, az = jnp.abs(nx), jnp.abs(ny), jnp.abs(nz)
    code = jnp.where(
        ax > 0,
        jnp.where(ay > 0, 8 * (ax - 1) + ay - 1, 72 + ax - 1),
        jnp.where(ay > 0, 64 + ay - 1, 80),
    )
    row_hot = jnp.where(lax.broadcasted_iota(jnp.int32, (96, KVEC), 0) == code, 1.0, 0.0).astype(bf16)
    lane_code = jnp.where(az > 0, az - 1, 8)
    lane_hot = lax.broadcasted_iota(jnp.int32, (16, KVEC), 0) == lane_code
    sx, sy, sz = (jnp.where(n < 0, -1.0, 1.0) for n in (nx, ny, nz))
    weight = kern_ref[...]
    parts = [[], []]
    for j, sign in enumerate((None, -sy * sz, -sx * sz, -sx * sy)):
        value = weight if sign is None else weight * sign
        high = value.astype(bf16).astype(f32)
        for part, piece in zip(parts, (high, value - high)):
            block = jnp.where(lane_hot, piece, 0.0)
            part += [block, -block if j in (1, 2) else block]
    grid = None
    for part in parts:
        term = lax.dot_general(row_hot, jnp.concatenate(part, 0).astype(bf16), NT, preferred_element_type=f32)
        grid = term if grid is None else grid + term
    lane = lax.broadcasted_iota(jnp.int32, (96, 128), 1)
    for j in range(4):
        kept = jnp.where(lane // 32 == j, grid, 0.0)
        kept = kept + pltpu.roll(kept, 64, 1)
        etab[j] = kept + pltpu.roll(kept, 32, 1)

    ex_s[0] = jnp.zeros((EXROWS, 256), f32)
    ex_s[3] = jnp.zeros((EXROWS, 256), f32)
    ex_s[1, 0:8, :] = jnp.zeros((8, 256), f32)
    ex_s[2, 0:8, :] = jnp.zeros((8, 256), f32)

    def gbf_rows(part):
        low, high = GPARTS[part]
        return slice(16 * low, 16 * high)

    def ex_rows(part):
        low, high = GPARTS[part]
        return slice(8 + 8 * low, 8 + 8 * high)

    def columns(values):
        high, low = split(values)
        high = high.astype(f32)
        pieces = [high[0:64], low[0:64], high[64:96], low[64:96], high[64:96], low[64:96]]
        return jnp.concatenate(pieces, 0)

    def put_split(target, g, at, both):
        part = 0 if g < GPARTS[0][1] else 1
        low, high = GPARTS[part]
        row = 8 * (g + low)
        ghigh, glow = split(both)
        target[row : row + 16, at] = ghigh
        row += 8 * (high - low)
        target[row : row + 16, at] = glow.astype(bf16)

    def fold(product):
        half = product.shape[0] // 2
        return product[0:half, :] + product[half:, :]

    first = jnp.where(lax.broadcasted_iota(jnp.int32, (8, 512), 0) == 0, 1.0, 0.0)
    zero8 = jnp.zeros((8, 512), f32)

    def arrive(step, carry):
        offset = jnp.where(step == 0, 0, jnp.where(step == 1, 1, jnp.where(step == 2, 3, 2)))
        base = ((quad + offset) % 4) * 4
        for m in range(4):
            pltpu.make_async_remote_copy(
                send_s.at[0],
                buf.at[base + m],
                s_sem.at[0],
                r_sem.at[base + m],
                device_id={"atoms": partner},
                device_id_type=MESH,
            ).wait_recv()
        rows = [jnp.concatenate([buf[base + m, r : r + 1, :] for m in range(4)], 1) for r in range(4)]
        at = pl.ds(pl.multiple_of(base * BLOCK, 512), 512)
        (cu, su), (cv, sv), (cw, sw) = (harmonics(rows[d]) for d in range(3))

        def put(t, low_tile, high_tile, g):
            both = jnp.concatenate([low_tile, high_tile], 0)
            utab[8 * t : 8 * t + 16, at] = both
            if g is not None:
                put_split(gone, g, slice(None), both * rows[3])
                put_split(gone.at[2 * GROWS : 4 * GROWS], g, slice(None), both)

        put(0, first, zero8, 0)
        put(2, cv, sv, 2)
        put(4, cu, su, 4)
        for a in range(8):
            for ta, u in ((0, cu), (1, su)):
                here = u[a : a + 1, :]
                put(core_tile(ta, 0, a), here * cv, here * sv, REST + 2 * (a - 1) + 2 * ta if a % 2 else None)

        w = jnp.concatenate([cw, first, sw, zero8], 0)
        whi, wlo = split(w)
        w3 = jnp.concatenate([w, w * cu[0:1, :], w * su[0:1, :]], 0)
        wcol[at, :] = columns(w3).T.astype(bf16)
        wlo = wlo.astype(bf16)
        wst[0:32, at] = whi
        wst[32:64, at] = whi
        wst[64:96, at] = wlo
        wst[96:128, at] = jnp.zeros((32, 512), bf16)
        product = jnp.dot(gone[...], wcol[at, :], preferred_element_type=f32)
        for part in range(2):
            mine = gbf_rows(part)
            ex_s[0, ex_rows(part), :] += fold(product[mine, :])
            ex_s[3, ex_rows(part), :] += fold(product[2 * GROWS + mine.start : 2 * GROWS + mine.stop, :])
        return carry

    lax.fori_loop(0, 4, arrive, 0)

    charge = buf[:, 3, :]
    chi = buf[:, 4, :]
    inv_hard = 1.0 / buf[:, 5, :]
    bond = buf[:, 6, :]

    def share(r, part):
        low, high = GPARTS[part]
        rows = pl.ds(0, 8 + 8 * high) if part == 0 else pl.ds(8 + 8 * low, 8 * (high - low))
        return pltpu.make_async_remote_copy(
            ex_s.at[r, rows],
            ex_r.at[r, rows],
            xs_sem.at[r, part],
            xr_sem.at[r, part],
            device_id={"atoms": partner},
            device_id_type=MESH,
        )

    def put_ends(r, weighted):
        ex_s[r, 0:8, 0:128] = jnp.concatenate(
            [weighted[0:1, :], weighted[15:16, :], bond[0:1, :], bond[15:16, :], jnp.zeros((4, 128), f32)], 0
        )

    ones_share = pltpu.make_async_remote_copy(
        ex_s.at[3], ex_r.at[3], xs_sem.at[3, 0], xr_sem.at[3, 0], device_id={"atoms": partner}, device_id_type=MESH
    )

    lane16 = lax.broadcasted_iota(jnp.int32, (16, 128), 1)
    number = jnp.where((lane16 & 15) < 8, (lane16 & 15) + 1, 0).astype(f32)
    slope = jnp.where((lane16 & 16) == 0, number, -number)

    def tensor(r, part):
        rows = ex_rows(part)
        sums = ex_s[r, rows, :] + ex_r[r, rows, :]
        plain, sines = sums[:, 0:128], sums[:, 128:256]
        plain = plain + pltpu.roll(plain, 64, 1)
        moved = pltpu.roll(plain, 32, 1)
        even = (lax.broadcasted_iota(jnp.int32, plain.shape, 1) & 32) == 0
        ones, cosines = jnp.where(even, plain, moved), jnp.where(even, moved, plain)
        sines = sines + pltpu.roll(sines, 32, 1)
        tiles = []
        base = 0
        if part == 0:
            tiles += [ones[0 : 8 * REST, :], cosines[16:32, :], sines[16:32, :]]
            base = REST
        for n in range(base, rows.stop // 8 - rows.start // 8, 4):
            both = slice(8 * n, 8 * n + 32)
            c, s = slice(8 * n, 8 * n + 16), slice(8 * n + 16, 8 * n + 32)
            tiles += [ones[both, :], cosines[c, :] - sines[s, :], cosines[s, :] + sines[c, :]]
        size = 8 * (PARTS[part][1] - PARTS[part][0])
        return jnp.concatenate(tiles, 0)[0:size, :]

    def mix(r, part, mean, slopes):
        low, high, numbers = PARTS[part]
        total = tensor(r, part)
        if r > 0:
            if part == 0:
                whole = ex_s[r, 8:9, 0:128] + ex_r[r, 8:9, 0:128]
                mean = (whole[:, 8:9] + whole[:, 72:73]) * (1.0 / ATOMS)
            total = total - mean * gtab[8 * low : 8 * high, :]
        swapped = flip(total)

        def store(t, pair):
            lhs[8 * t : 8 * t + 16, :] = expand(pair)
            if slopes:
                lhs[ROWS + 8 * t : ROWS + 8 * t + 16, :] = expand(flip(pair) * slope)

        if part == 0:
            zero = jnp.zeros((8, 128), f32)
            store(0, jnp.concatenate([etab[0, 80:88, :] * tile(total, 0), zero], 0))
            for t, row, j in ((2, 64, 1), (4, 72, 2)):
                e0 = etab[0, row : row + 8, :]
                ej = etab[j, row : row + 8, :]
                pair = [
                    e0 * tile(total, t) + ej * tile(swapped, t + 1),
                    e0 * tile(total, t + 1) - ej * tile(swapped, t),
                ]
                store(t, jnp.concatenate(pair, 0))
        for a in numbers:
            e = [etab[j, 8 * a : 8 * a + 8, :] for j in range(4)]
            for ta in range(2):
                pair = []
                for tb in range(2):
                    both = tile(total, core_tile(1 - ta, 1 - tb, a) - low)
                    over_b = tile(swapped, core_tile(ta, 1 - tb, a) - low)
                    over_a = tile(swapped, core_tile(1 - ta, tb, a) - low)
                    out = e[0] * tile(total, core_tile(ta, tb, a) - low)
                    out = out + e[3] * both if ta == tb else out - e[3] * both
                    out = out + e[1] * over_b if tb == 0 else out - e[1] * over_b
                    out = out + e[2] * over_a if ta == 0 else out - e[2] * over_a
                    pair.append(out)
                store(core_tile(ta, 0, a), jnp.concatenate(pair, 0))
        return mean

    def potential(part):
        low, high, _ = PARTS[part]
        rows = slice(8 * low, 8 * high)
        for i in range(HALF // 2048):
            whole = jnp.dot(lhs[rows, :], wst[:, i * 2048 : (i + 1) * 2048], preferred_element_type=f32)
            for k in range(2048 // 256):
                at = slice(i * 2048 + k * 256, i * 2048 + k * 256 + 256)
                fields = whole[:, k * 256 : k * 256 + 256]
                sums = [None] * 4
                for t in range(low, high):
                    term = tile(fields, t - low) * utab[8 * t : 8 * t + 8, at]
                    sums[t % 4] = term if sums[t % 4] is None else sums[t % 4] + term
                total = (sums[0] + sums[1]) + (sums[2] + sums[3])
                if part == 0:
                    acc[0, :, at] = total
                else:
                    row = jnp.sum(total + acc[0, :, at], 0, keepdims=True)
                    j = (i * 2048 + k * 256) // 128
                    phi_s[j : j + 1, :] = row[:, 0:128]
                    phi_s[j + 1 : j + 2, :] = row[:, 128:256]

    lane_at = lax.broadcasted_iota(jnp.int32, (8, BLOCK), 1)

    def near_sums(blocks, out):
        for j in blocks:
            target = lane_at + nbuf[j]
            index = target & (BLOCK - 1)
            low, mid, high = (
                jnp.take_along_axis(
                    jnp.broadcast_to(ext_s[j + d : j + d + 1, :], (8, BLOCK)), index, axis=1, mode="promise_in_bounds"
                )
                for d in range(3)
            )
            got = jnp.where(target < 0, low, jnp.where(target >= BLOCK, high, mid))
            out[j : j + 1, :] = jnp.sum(got, 0, keepdims=True)

    def inner_near(own, out):
        ext_s[1:17, :] = own
        near_sums(range(1, SLOTS - 1), out)

    def outer_near(own, left, right, out):
        ext_s[0:1, :] = left
        ext_s[1:17, :] = own
        ext_s[17:18, :] = right
        near_sums((0, SLOTS - 1), out)

    def refactor(r, values):
        for part in range(2):
            for j in range(SLOTS):
                at = slice(j * BLOCK, (j + 1) * BLOCK)
                row = values[j : j + 1, :]
                for g in range(GPARTS[part][0], GPARTS[part][1], 2):
                    n, ta = (g - REST) // 4, ((g - REST) // 2) % 2
                    t = g if g < REST else core_tile(ta, 0, 2 * n + 1)
                    put_split(gbf, g, at, utab[8 * t : 8 * t + 16, at] * row)
            ex_s[r, ex_rows(part), :] = fold(jnp.dot(gbf[gbf_rows(part), :], wcol[...], preferred_element_type=f32))
            share(r, part).start()

    def relax(charge, near):
        potential_here = ewald_scale * phi_s[...]
        return 0.5 * charge + 0.5 * (-(chi + potential_here + bond * near) * inv_hard)

    weighted = bond * charge
    put_ends(0, weighted)
    share(0, 0).start()
    share(0, 1).start()
    ones_share.start()

    def wait_nbr(j, carry):
        pltpu.make_async_remote_copy(
            nbr_ref, nbuf.at[j], ns_sem.at[0], nr_sem.at[j], device_id={"atoms": partner}, device_id_type=MESH
        ).wait_recv()
        return carry

    lax.fori_loop(0, SLOTS, wait_nbr, 0)
    inner_near(bond, nbond_s)
    inner_near(weighted, near_s)
    share(0, 0).wait()
    mix(0, 0, None, False)
    potential(0)
    ends = ex_r[0, 0:8, 0:128]
    outer_near(weighted, ends[1:2, :], ends[0:1, :], near_s)
    share(0, 1).wait()
    mix(0, 1, None, False)
    potential(1)
    relaxed = relax(charge, near_s[...])

    weighted = bond * relaxed
    put_ends(1, weighted)
    refactor(1, relaxed)
    inner_near(weighted, near_s)
    ones_share.wait()
    for part in range(2):
        gtab[8 * PARTS[part][0] : 8 * PARTS[part][1], :] = tensor(3, part)
    outer_near(bond, ends[3:4, :], ends[2:3, :], nbond_s)
    share(1, 0).wait()
    mean = mix(1, 0, None, False)
    potential(0)
    ends = ex_r[1, 0:8, 0:128]
    outer_near(weighted, ends[1:2, :], ends[0:1, :], near_s)
    share(1, 1).wait()
    mix(1, 1, mean, False)
    potential(1)
    charge = relaxed - mean
    relaxed = relax(charge, near_s[...] - mean * nbond_s[...])

    put_ends(2, relaxed)
    refactor(2, relaxed)

    ones = lax.broadcasted_iota(jnp.int32, (8, 256), 0).astype(f32) + 1.0

    my_bead = 2 * x_lo + z % 2

    def force_copy(k, m):
        i = (z + 1 + k) % 2
        home = core * 16 + (2 * quad + i) * 2 + m
        return home, pltpu.make_async_remote_copy(
            fsend.at[2 * k + m],
            frecv.at[my_bead],
            fs_sem.at[2 * k + m],
            fr_sem.at[my_bead],
            device_id={"atoms": home},
            device_id_type=MESH,
        )

    def force_start(k):
        for m in range(2):
            home, copy = force_copy(k, m)
            if k == 0:
                copy.start()
            else:

                @pl.when(home != me)
                def _():
                    copy.start()

                @pl.when(home == me)
                def _():
                    pltpu.make_async_copy(fsend.at[2 * k + m], frecv.at[my_bead], fr_sem.at[my_bead]).start()

    def force(part):
        low, high, numbers = PARTS[part]
        for k in range(2):
            i = (z + 1 + k) % 2
            at = pl.ds(pl.multiple_of(quad * 512 + i * 256, 256), 256)
            keep = slice(k * 256, k * 256 + 256)
            plain = jnp.dot(lhs[8 * low : 8 * high, :], wst[:, at], preferred_element_type=f32)
            sloped = jnp.dot(lhs[ROWS + 8 * low : ROWS + 8 * high, :], wst[:, at], preferred_element_type=f32)
            basis = {t: utab[8 * t : 8 * t + 8, at] for t in range(low, high)}
            f = {t: tile(plain, t - low) for t in range(low, high)}
            dz = [None] * 4
            for t in range(low, high):
                term = basis[t] * tile(sloped, t - low)
                dz[t % 4] = term if dz[t % 4] is None else dz[t % 4] + term
            dz = (dz[0] + dz[1]) + (dz[2] + dz[3])

            def turn(c, s):
                return basis[c] * f[s] - basis[s] * f[c]

            dx = dy = None
            for a in numbers:
                along_x = turn(core_tile(0, 0, a), core_tile(1, 0, a)) + turn(core_tile(0, 1, a), core_tile(1, 1, a))
                along_y = turn(core_tile(0, 0, a), core_tile(0, 1, a)) + turn(core_tile(1, 0, a), core_tile(1, 1, a))
                along_x = (a + 1.0) * along_x
                dx = along_x if dx is None else dx + along_x
                dy = along_y if dy is None else dy + along_y
            if part == 0:
                acc[0, :, keep] = dx + ones * turn(4, 5)
                acc[1, :, keep] = ones * (dy + turn(2, 3))
                acc[2, :, keep] = dz
            else:
                dx = dx + acc[0, :, keep]
                dy = ones * dy + acc[1, :, keep]
                dz = dz + acc[2, :, keep]
                dx, dy, dz = (jnp.sum(d, 0, keepdims=True) for d in (dx, dy, dz))
                for m in range(2):
                    own = near_s[pl.ds(quad * 4 + 2 * i + m, 1), :]
                    piece = slice(128 * m, 128 * m + 128)
                    fsend[2 * k + m] = jnp.concatenate(
                        [dx[:, piece], dy[:, piece], dz[:, piece], own, jnp.zeros((4, 128), f32)], 0
                    )
                force_start(k)

    share(2, 0).wait()
    mean = mix(2, 0, None, True)
    near_s[...] = relaxed - mean
    force(0)
    share(2, 1).wait()
    mix(2, 1, mean, True)
    force(1)

    for make in (data_copy, nbr_copy):
        for b, o in order:
            dest = far_dest(b, o)
            if o:
                make(b, o, dest).wait_send()
            else:

                @pl.when(dest != me)
                def _():
                    make(b, o, dest).wait_send()

    to_next.wait()
    to_prev.wait()
    inv_mass = 1.0 / mass_row
    for b in range(4):
        pltpu.make_async_remote_copy(
            fsend.at[0], frecv.at[b], fs_sem.at[0], fr_sem.at[b], device_id={"atoms": partner}, device_id_type=MESH
        ).wait_recv()
    charges = frecv[:, 3, :]
    out_ref[6] = charges
    for d in range(3):
        ewald_force = (-two_pi * ewald_scale) * charges * frecv[:, d, :]
        here = pos_s[d]
        before = jnp.concatenate([halo[0, d : d + 1, :], here[0:3, :]], 0)
        after = jnp.concatenate([here[1:4, :], halo[1, d : d + 1, :]], 0)
        laplace = 2.0 * here - before - after
        speed = vel_s[d] + time_step * (ewald_force * inv_mass - spring_rate * laplace)
        out_ref[3 + d] = speed
        out_ref[d] = here + time_step * speed
    for k in range(2):
        for m in range(2):
            home, copy = force_copy(k, m)
            if k == 0:
                copy.wait_send()
            else:

                @pl.when(home != me)
                def _():
                    copy.wait_send()


def emit_body(packed, npos_hbm, nvel_hbm, nchg_hbm, sems):
    copies = [
        pltpu.make_async_copy(source, target, sems.at[i])
        for i, (source, target) in enumerate(
            ((packed.at[0:3], npos_hbm), (packed.at[3:6], nvel_hbm), (packed.at[6], nchg_hbm))
        )
    ]
    for copy in copies:
        copy.start()
    for copy in copies:
        copy.wait()


def step(positions, velocities, charges_in, species, neighbors, k_index, kernel, chi, hard, bond, mass):
    vmem = pl.BlockSpec(memory_space=pltpu.VMEM)
    hbm = pl.BlockSpec(memory_space=pltpu.HBM)
    dma = pltpu.SemaphoreType.DMA
    packed = pl.pallas_call(
        kernel_body,
        out_shape=pltpu.VMEM((7, 4, BLOCK), f32),
        in_specs=[hbm] * 11,
        out_specs=vmem,
        scratch_shapes=[
            pltpu.VMEM((3, 4, BLOCK), f32),
            pltpu.VMEM((3, 4, BLOCK), f32),
            pltpu.VMEM((4, BLOCK), f32),
            pltpu.VMEM((1, BLOCK), jnp.int32),
            pltpu.VMEM((8, BLOCK), jnp.int32),
            pltpu.VMEM((3, KVEC), jnp.int32),
            pltpu.VMEM((1, KVEC), f32),
            pltpu.SMEM((4, SPECIES), f32),
            pltpu.VMEM((4, 8, 128), f32),
            pltpu.VMEM((SLOTS, 8, 128), f32),
            pltpu.VMEM((SLOTS, 8, 128), jnp.int32),
            pltpu.VMEM((ROWS, HALF), f32),
            pltpu.VMEM((2 * GROWS, HALF), bf16),
            pltpu.VMEM((4 * GROWS, 512), bf16),
            pltpu.VMEM((HALF, 256), bf16),
            pltpu.VMEM((128, HALF), bf16),
            pltpu.VMEM((4, 96, 128), f32),
            pltpu.VMEM((4, EXROWS, 256), f32),
            pltpu.VMEM((4, EXROWS, 256), f32),
            pltpu.VMEM((3, 8, HALF), f32),
            pltpu.VMEM((ROWS, 128), f32),
            pltpu.VMEM((2 * ROWS, 128), bf16),
            pltpu.VMEM((SLOTS, 128), f32),
            pltpu.VMEM((SLOTS, 128), f32),
            pltpu.VMEM((SLOTS, 128), f32),
            pltpu.VMEM((24, 128), f32),
            pltpu.VMEM((4, 8, 128), f32),
            pltpu.VMEM((4, 8, 128), f32),
            pltpu.VMEM((2, 8, 128), f32),
            dma((11,)),
            dma((16,)),
            dma((16,)),
            dma((16,)),
            dma((16,)),
            dma((4, 2)),
            dma((4, 2)),
            dma((4,)),
            dma((4,)),
            dma((2,)),
            dma((2,)),
        ],
        compiler_params=pltpu.CompilerParams(collective_id=0, has_side_effects=True),
        name="pimd_step",
    )(
        positions.transpose(1, 0, 2),
        velocities.transpose(1, 0, 2),
        charges_in,
        species.reshape(1, BLOCK),
        neighbors,
        k_index,
        kernel.reshape(1, KVEC),
        chi,
        hard,
        bond,
        mass,
    )
    spatial = jax.ShapeDtypeStruct((3, 4, BLOCK), f32)
    new_positions, new_velocities, charges = pl.pallas_call(
        emit_body,
        out_shape=(spatial, spatial, jax.ShapeDtypeStruct((4, BLOCK), f32)),
        in_specs=[vmem],
        out_specs=(hbm, hbm, hbm),
        scratch_shapes=[dma((3,))],
        name="emit",
    )(pltpu.with_memory_space_constraint(packed, pltpu.VMEM))
    return new_positions.transpose(1, 0, 2), new_velocities.transpose(1, 0, 2), charges


def solution(mesh):
    return jax.shard_map(
        step,
        mesh=mesh,
        in_specs=(
            P("beads", None, "atoms"),
            P("beads", None, "atoms"),
            P("beads", "atoms"),
            P("atoms"),
            P(None, "atoms"),
            P(),
            P(),
            P(),
            P(),
            P(),
            P(),
        ),
        out_specs=(P("beads", None, "atoms"), P("beads", None, "atoms"), P("beads", "atoms")),
        check_vma=False,
    )
```

```python
import math

import jax
import jax.numpy as jnp
from jax import lax
from jax.experimental import pallas as pl
from jax.experimental.pallas import tpu as pltpu
from jax.sharding import PartitionSpec as P

KVEC = 2048
SPECIES = 8
ATOMS = 4096
BEAD_AXIS = 8
BLOCK = 128
SLOTS = 16
HALF = SLOTS * BLOCK
TILES = 38
ROWS = TILES * 8
GROWS = 176
EXROWS = GROWS + 8
REST = 6
PARTS = ((0, REST + 12, (0, 1, 2)), (REST + 12, TILES, (3, 4, 5, 6, 7)))
GPARTS = ((0, REST + 4), (REST + 4, GROWS // 8))

two_pi = 2.0 * math.pi
ewald_scale = 4.0 / math.sqrt(KVEC * ATOMS)
time_step = 0.05
spring_rate = 0.5

COS = (1.0, -19.7392087, 64.9393891, -85.4566583, 60.2421313, -26.4046682, 7.80013144, -1.45311232)
SIN = (6.2831853, -41.3417004, 81.6051314, -76.7030154, 42.025927, -14.8998467, 3.2381375)

MESH = pl.DeviceIdType.MESH
NT = (((1,), (1,)), ((), ()))
f32 = jnp.float32
bf16 = jnp.bfloat16


def horner(coeffs, s):
    total = coeffs[-1] * s + coeffs[-2]
    for value in coeffs[-3::-1]:
        total = total * s + value
    return total


def harmonics(row):
    n = lax.broadcasted_iota(jnp.int32, (8, row.shape[1]), 0).astype(f32) + 1.0
    turns = n * row
    r = turns - jnp.floor(turns + 0.5)
    s = r * r
    return horner(COS, s), r * horner(SIN, s)


def split(x):
    high = x.astype(bf16)
    return high, x - high.astype(f32)


def tile(x, t):
    return x[8 * t : 8 * t + 8, :]


def flip(x):
    return pltpu.roll(x, 16, 1)


def core_tile(ta, tb, a):
    return REST + 4 * a + 2 * ta + tb


def expand(coeff):
    high, low = split(coeff)
    group = lax.broadcasted_iota(jnp.int32, coeff.shape, 1) // 32
    return jnp.where(group == 1, low, high.astype(f32)).astype(bf16)


def kernel_body(
    pos_hbm,
    vel_hbm,
    chg_hbm,
    spec_hbm,
    nbr_hbm,
    k_hbm,
    kern_hbm,
    chi_hbm,
    hard_hbm,
    bond_hbm,
    mass_hbm,
    out_ref,
    pos_s,
    vel_s,
    chg_s,
    spec_s,
    nbr_ref,
    k_ref,
    kern_ref,
    tables,
    send_s,
    buf,
    nbuf,
    utab,
    gbf,
    gone,
    wcol,
    wst,
    etab,
    ex_s,
    ex_r,
    acc,
    gtab,
    lhs,
    phi_s,
    near_s,
    nbond_s,
    ext_s,
    fsend,
    frecv,
    halo,
    in_sem,
    s_sem,
    r_sem,
    ns_sem,
    nr_sem,
    xs_sem,
    xr_sem,
    fs_sem,
    fr_sem,
    hs_sem,
    hr_sem,
):
    me = lax.axis_index("atoms")
    bead = lax.axis_index("beads")
    x_lo = me // 16
    z = (me // 2) % 8
    core = me % 2
    quad = z // 2
    partner = x_lo * 16 + z * 2 + (1 - core)
    next_bead = (bead + 1) % BEAD_AXIS
    prev_bead = (bead + BEAD_AXIS - 1) % BEAD_AXIS

    barrier = pltpu.get_barrier_semaphore()

    def greet(x, zz, c):
        pl.semaphore_signal(barrier, inc=1, device_id={"atoms": 16 * x + 2 * zz + c}, device_id_type=MESH)

    odd = x_lo ^ core
    for o in (4, 3, 5, 2, 6, 1, 7, 0):
        zz = (z + o) % 8
        greet(1 - x_lo, zz, core)
        greet(x_lo, zz, 1 - core)
        if o:
            greet(x_lo ^ odd, zz, core ^ odd)
        else:

            @pl.when(odd == 1)
            def _():
                greet(x_lo ^ odd, zz, core ^ odd)

    for other in (next_bead, prev_bead):
        pl.semaphore_signal(barrier, inc=1, device_id={"beads": other}, device_id_type=MESH)

    loads = [
        pltpu.make_async_copy(source, target, in_sem.at[i])
        for i, (source, target) in enumerate(
            (
                (pos_hbm, pos_s),
                (chg_hbm, chg_s),
                (spec_hbm, spec_s),
                (chi_hbm, tables.at[0]),
                (hard_hbm, tables.at[1]),
                (bond_hbm, tables.at[2]),
                (mass_hbm, tables.at[3]),
                (nbr_hbm, nbr_ref),
                (k_hbm, k_ref),
                (kern_hbm, kern_ref),
                (vel_hbm, vel_s),
            )
        )
    ]
    for load in loads:
        load.start()

    for load in loads[0:7]:
        load.wait()
    species = spec_s[...]

    def lookup(t):
        total = jnp.zeros((1, BLOCK), f32)
        for s in range(SPECIES):
            total = jnp.where(species == s, tables[t, s], total)
        return total

    chi_row, hard_row, bond_row, mass_row = (lookup(t) for t in range(4))
    for b in range(4):
        for d in range(3):
            send_s[b, d : d + 1, :] = pos_s[d, b : b + 1, :]
        send_s[b, 3:4, :] = chg_s[b : b + 1, :]
        send_s[b, 4:5, :] = chi_row
        send_s[b, 5:6, :] = hard_row
        send_s[b, 6:7, :] = bond_row
        send_s[b, 7:8, :] = bond_row
    loads[7].wait()

    pl.semaphore_wait(barrier, 25 + odd)

    slot = z * 2 + core

    def far_dest(b, o):
        return (b >> 1) * 16 + (2 * ((quad + o) % 4) + (b & 1)) * 2 + x_lo

    def data_copy(b, o, dest):
        return pltpu.make_async_remote_copy(
            send_s.at[b], buf.at[slot], s_sem.at[4 * o + b], r_sem.at[slot], device_id={"atoms": dest}, device_id_type=MESH
        )

    def nbr_copy(b, o, dest):
        return pltpu.make_async_remote_copy(
            nbr_ref, nbuf.at[slot], ns_sem.at[4 * o + b], nr_sem.at[slot], device_id={"atoms": dest}, device_id_type=MESH
        )

    order = [(b, o) for o in (2, 1, 3, 0) for b in range(4)]
    for make, source, store, sem in (
        (data_copy, lambda b: send_s.at[b], buf, r_sem),
        (nbr_copy, lambda b: nbr_ref, nbuf, nr_sem),
    ):
        for b, o in order:
            dest = far_dest(b, o)
            if o:
                make(b, o, dest).start()
            else:

                @pl.when(dest != me)
                def _():
                    make(b, o, dest).start()

                @pl.when(dest == me)
                def _():
                    pltpu.make_async_copy(source(b), store.at[slot], sem.at[slot]).start()

    to_next = pltpu.make_async_remote_copy(
        send_s.at[3], halo.at[0], hs_sem.at[0], hr_sem.at[0], device_id={"beads": next_bead}, device_id_type=MESH
    )
    to_prev = pltpu.make_async_remote_copy(
        send_s.at[0], halo.at[1], hs_sem.at[1], hr_sem.at[1], device_id={"beads": prev_bead}, device_id_type=MESH
    )
    to_next.start()
    to_prev.start()

    for load in loads[8:]:
        load.wait()
    nx, ny, nz = (k_ref[d : d + 1, :] for d in range(3))
    ax, ay, az = jnp.abs(nx), jnp.abs(ny), jnp.abs(nz)
    code = jnp.where(
        ax > 0,
        jnp.where(ay > 0, 8 * (ax - 1) + ay - 1, 72 + ax - 1),
        jnp.where(ay > 0, 64 + ay - 1, 80),
    )
    row_hot = jnp.where(lax.broadcasted_iota(jnp.int32, (96, KVEC), 0) == code, 1.0, 0.0).astype(bf16)
    lane_code = jnp.where(az > 0, az - 1, 8)
    lane_hot = lax.broadcasted_iota(jnp.int32, (16, KVEC), 0) == lane_code
    sx, sy, sz = (jnp.where(n < 0, -1.0, 1.0) for n in (nx, ny, nz))
    weight = kern_ref[...]
    parts = [[], []]
    for j, sign in enumerate((None, -sy * sz, -sx * sz, -sx * sy)):
        value = weight if sign is None else weight * sign
        high = value.astype(bf16).astype(f32)
        for part, piece in zip(parts, (high, value - high)):
            block = jnp.where(lane_hot, piece, 0.0)
            part += [block, -block if j in (1, 2) else block]
    grid = None
    for part in parts:
        term = lax.dot_general(row_hot, jnp.concatenate(part, 0).astype(bf16), NT, preferred_element_type=f32)
        grid = term if grid is None else grid + term
    lane = lax.broadcasted_iota(jnp.int32, (96, 128), 1)
    for j in range(4):
        kept = jnp.where(lane // 32 == j, grid, 0.0)
        kept = kept + pltpu.roll(kept, 64, 1)
        etab[j] = kept + pltpu.roll(kept, 32, 1)

    ex_s[0] = jnp.zeros((EXROWS, 256), f32)
    ex_s[3] = jnp.zeros((EXROWS, 256), f32)
    ex_s[1, 0:8, :] = jnp.zeros((8, 256), f32)
    ex_s[2, 0:8, :] = jnp.zeros((8, 256), f32)

    def gbf_rows(part):
        low, high = GPARTS[part]
        return slice(16 * low, 16 * high)

    def ex_rows(part):
        low, high = GPARTS[part]
        return slice(8 + 8 * low, 8 + 8 * high)

    def columns(values):
        high, low = split(values)
        high = high.astype(f32)
        pieces = [high[0:64], low[0:64], high[64:96], low[64:96], high[64:96], low[64:96]]
        return jnp.concatenate(pieces, 0)

    def put_split(target, g, at, both):
        part = 0 if g < GPARTS[0][1] else 1
        low, high = GPARTS[part]
        row = 8 * (g + low)
        ghigh, glow = split(both)
        target[row : row + 16, at] = ghigh
        row += 8 * (high - low)
        target[row : row + 16, at] = glow.astype(bf16)

    def fold(product):
        half = product.shape[0] // 2
        return product[0:half, :] + product[half:, :]

    first = jnp.where(lax.broadcasted_iota(jnp.int32, (8, 512), 0) == 0, 1.0, 0.0)
    zero8 = jnp.zeros((8, 512), f32)

    def arrive(step, carry):
        offset = jnp.where(step == 0, 0, jnp.where(step == 1, 1, jnp.where(step == 2, 3, 2)))
        base = ((quad + offset) % 4) * 4
        for m in range(4):
            pltpu.make_async_remote_copy(
                send_s.at[0],
                buf.at[base + m],
                s_sem.at[0],
                r_sem.at[base + m],
                device_id={"atoms": partner},
                device_id_type=MESH,
            ).wait_recv()
        rows = [jnp.concatenate([buf[base + m, r : r + 1, :] for m in range(4)], 1) for r in range(4)]
        at = pl.ds(pl.multiple_of(base * BLOCK, 512), 512)
        (cu, su), (cv, sv), (cw, sw) = (harmonics(rows[d]) for d in range(3))

        def put(t, low_tile, high_tile, g):
            both = jnp.concatenate([low_tile, high_tile], 0)
            utab[8 * t : 8 * t + 16, at] = both
            if g is not None:
                put_split(gone, g, slice(None), both * rows[3])
                put_split(gone.at[2 * GROWS : 4 * GROWS], g, slice(None), both)

        put(0, first, zero8, 0)
        put(2, cv, sv, 2)
        put(4, cu, su, 4)
        for a in range(8):
            for ta, u in ((0, cu), (1, su)):
                here = u[a : a + 1, :]
                put(core_tile(ta, 0, a), here * cv, here * sv, REST + 2 * (a - 1) + 2 * ta if a % 2 else None)

        w = jnp.concatenate([cw, first, sw, zero8], 0)
        whi, wlo = split(w)
        w3 = jnp.concatenate([w, w * cu[0:1, :], w * su[0:1, :]], 0)
        wcol[at, :] = columns(w3).T.astype(bf16)
        wlo = wlo.astype(bf16)
        wst[0:32, at] = whi
        wst[32:64, at] = whi
        wst[64:96, at] = wlo
        wst[96:128, at] = jnp.zeros((32, 512), bf16)
        product = jnp.dot(gone[...], wcol[at, :], preferred_element_type=f32)
        for part in range(2):
            mine = gbf_rows(part)
            ex_s[0, ex_rows(part), :] += fold(product[mine, :])
            ex_s[3, ex_rows(part), :] += fold(product[2 * GROWS + mine.start : 2 * GROWS + mine.stop, :])
        return carry

    lax.fori_loop(0, 4, arrive, 0)

    charge = buf[:, 3, :]
    chi = buf[:, 4, :]
    inv_hard = 1.0 / buf[:, 5, :]
    bond = buf[:, 6, :]

    def share(r, part):
        low, high = GPARTS[part]
        rows = pl.ds(0, 8 + 8 * high) if part == 0 else pl.ds(8 + 8 * low, 8 * (high - low))
        return pltpu.make_async_remote_copy(
            ex_s.at[r, rows],
            ex_r.at[r, rows],
            xs_sem.at[r, part],
            xr_sem.at[r, part],
            device_id={"atoms": partner},
            device_id_type=MESH,
        )

    def put_ends(r, weighted):
        ex_s[r, 0:8, 0:128] = jnp.concatenate(
            [weighted[0:1, :], weighted[15:16, :], bond[0:1, :], bond[15:16, :], jnp.zeros((4, 128), f32)], 0
        )

    ones_share = pltpu.make_async_remote_copy(
        ex_s.at[3], ex_r.at[3], xs_sem.at[3, 0], xr_sem.at[3, 0], device_id={"atoms": partner}, device_id_type=MESH
    )

    lane16 = lax.broadcasted_iota(jnp.int32, (16, 128), 1)
    number = jnp.where((lane16 & 15) < 8, (lane16 & 15) + 1, 0).astype(f32)
    slope = jnp.where((lane16 & 16) == 0, number, -number)

    def tensor(r, part):
        rows = ex_rows(part)
        sums = ex_s[r, rows, :] + ex_r[r, rows, :]
        plain, sines = sums[:, 0:128], sums[:, 128:256]
        plain = plain + pltpu.roll(plain, 64, 1)
        moved = pltpu.roll(plain, 32, 1)
        even = (lax.broadcasted_iota(jnp.int32, plain.shape, 1) & 32) == 0
        ones, cosines = jnp.where(even, plain, moved), jnp.where(even, moved, plain)
        sines = sines + pltpu.roll(sines, 32, 1)
        tiles = []
        base = 0
        if part == 0:
            tiles += [ones[0 : 8 * REST, :], cosines[16:32, :], sines[16:32, :]]
            base = REST
        for n in range(base, rows.stop // 8 - rows.start // 8, 4):
            both = slice(8 * n, 8 * n + 32)
            c, s = slice(8 * n, 8 * n + 16), slice(8 * n + 16, 8 * n + 32)
            tiles += [ones[both, :], cosines[c, :] - sines[s, :], cosines[s, :] + sines[c, :]]
        size = 8 * (PARTS[part][1] - PARTS[part][0])
        return jnp.concatenate(tiles, 0)[0:size, :]

    def mix(r, part, mean, slopes):
        low, high, numbers = PARTS[part]
        total = tensor(r, part)
        if r > 0:
            if part == 0:
                whole = ex_s[r, 8:9, 0:128] + ex_r[r, 8:9, 0:128]
                mean = (whole[:, 8:9] + whole[:, 72:73]) * (1.0 / ATOMS)
            total = total - mean * gtab[8 * low : 8 * high, :]
        swapped = flip(total)

        def store(t, pair):
            lhs[8 * t : 8 * t + 16, :] = expand(pair)
            if slopes:
                lhs[ROWS + 8 * t : ROWS + 8 * t + 16, :] = expand(flip(pair) * slope)

        if part == 0:
            zero = jnp.zeros((8, 128), f32)
            store(0, jnp.concatenate([etab[0, 80:88, :] * tile(total, 0), zero], 0))
            for t, row, j in ((2, 64, 1), (4, 72, 2)):
                e0 = etab[0, row : row + 8, :]
                ej = etab[j, row : row + 8, :]
                pair = [
                    e0 * tile(total, t) + ej * tile(swapped, t + 1),
                    e0 * tile(total, t + 1) - ej * tile(swapped, t),
                ]
                store(t, jnp.concatenate(pair, 0))
        for a in numbers:
            e = [etab[j, 8 * a : 8 * a + 8, :] for j in range(4)]
            for ta in range(2):
                pair = []
                for tb in range(2):
                    both = tile(total, core_tile(1 - ta, 1 - tb, a) - low)
                    over_b = tile(swapped, core_tile(ta, 1 - tb, a) - low)
                    over_a = tile(swapped, core_tile(1 - ta, tb, a) - low)
                    out = e[0] * tile(total, core_tile(ta, tb, a) - low)
                    out = out + e[3] * both if ta == tb else out - e[3] * both
                    out = out + e[1] * over_b if tb == 0 else out - e[1] * over_b
                    out = out + e[2] * over_a if ta == 0 else out - e[2] * over_a
                    pair.append(out)
                store(core_tile(ta, 0, a), jnp.concatenate(pair, 0))
        return mean

    def potential(part):
        low, high, _ = PARTS[part]
        rows = slice(8 * low, 8 * high)
        for i in range(HALF // 2048):
            whole = jnp.dot(lhs[rows, :], wst[:, i * 2048 : (i + 1) * 2048], preferred_element_type=f32)
            for k in range(2048 // 256):
                at = slice(i * 2048 + k * 256, i * 2048 + k * 256 + 256)
                fields = whole[:, k * 256 : k * 256 + 256]
                sums = [None] * 4
                for t in range(low, high):
                    term = tile(fields, t - low) * utab[8 * t : 8 * t + 8, at]
                    sums[t % 4] = term if sums[t % 4] is None else sums[t % 4] + term
                total = (sums[0] + sums[1]) + (sums[2] + sums[3])
                if part == 0:
                    acc[0, :, at] = total
                else:
                    row = jnp.sum(total + acc[0, :, at], 0, keepdims=True)
                    j = (i * 2048 + k * 256) // 128
                    phi_s[j : j + 1, :] = row[:, 0:128]
                    phi_s[j + 1 : j + 2, :] = row[:, 128:256]

    lane_at = lax.broadcasted_iota(jnp.int32, (8, BLOCK), 1)

    def near_sums(blocks, out):
        for j in blocks:
            target = lane_at + nbuf[j]
            index = target & (BLOCK - 1)
            low, mid, high = (
                jnp.take_along_axis(
                    jnp.broadcast_to(ext_s[j + d : j + d + 1, :], (8, BLOCK)), index, axis=1, mode="promise_in_bounds"
                )
                for d in range(3)
            )
            got = jnp.where(target < 0, low, jnp.where(target >= BLOCK, high, mid))
            out[j : j + 1, :] = jnp.sum(got, 0, keepdims=True)

    def inner_near(own, out):
        ext_s[1:17, :] = own
        near_sums(range(1, SLOTS - 1), out)

    def outer_near(own, left, right, out):
        ext_s[0:1, :] = left
        ext_s[1:17, :] = own
        ext_s[17:18, :] = right
        near_sums((0, SLOTS - 1), out)

    def refactor(r, values):
        for part in range(2):
            for j in range(SLOTS):
                at = slice(j * BLOCK, (j + 1) * BLOCK)
                row = values[j : j + 1, :]
                for g in range(GPARTS[part][0], GPARTS[part][1], 2):
                    n, ta = (g - REST) // 4, ((g - REST) // 2) % 2
                    t = g if g < REST else core_tile(ta, 0, 2 * n + 1)
                    put_split(gbf, g, at, utab[8 * t : 8 * t + 16, at] * row)
            ex_s[r, ex_rows(part), :] = fold(jnp.dot(gbf[gbf_rows(part), :], wcol[...], preferred_element_type=f32))
            share(r, part).start()

    def relax(charge, near):
        potential_here = ewald_scale * phi_s[...]
        return 0.5 * charge + 0.5 * (-(chi + potential_here + bond * near) * inv_hard)

    weighted = bond * charge
    put_ends(0, weighted)
    share(0, 0).start()
    share(0, 1).start()
    ones_share.start()

    def wait_nbr(j, carry):
        pltpu.make_async_remote_copy(
            nbr_ref, nbuf.at[j], ns_sem.at[0], nr_sem.at[j], device_id={"atoms": partner}, device_id_type=MESH
        ).wait_recv()
        return carry

    lax.fori_loop(0, SLOTS, wait_nbr, 0)
    inner_near(bond, nbond_s)
    inner_near(weighted, near_s)
    share(0, 0).wait()
    mix(0, 0, None, False)
    potential(0)
    ends = ex_r[0, 0:8, 0:128]
    outer_near(weighted, ends[1:2, :], ends[0:1, :], near_s)
    share(0, 1).wait()
    mix(0, 1, None, False)
    potential(1)
    relaxed = relax(charge, near_s[...])

    weighted = bond * relaxed
    put_ends(1, weighted)
    refactor(1, relaxed)
    inner_near(weighted, near_s)
    ones_share.wait()
    for part in range(2):
        gtab[8 * PARTS[part][0] : 8 * PARTS[part][1], :] = tensor(3, part)
    outer_near(bond, ends[3:4, :], ends[2:3, :], nbond_s)
    share(1, 0).wait()
    mean = mix(1, 0, None, False)
    potential(0)
    ends = ex_r[1, 0:8, 0:128]
    outer_near(weighted, ends[1:2, :], ends[0:1, :], near_s)
    share(1, 1).wait()
    mix(1, 1, mean, False)
    potential(1)
    charge = relaxed - mean
    relaxed = relax(charge, near_s[...] - mean * nbond_s[...])

    put_ends(2, relaxed)
    refactor(2, relaxed)

    ones = lax.broadcasted_iota(jnp.int32, (8, 256), 0).astype(f32) + 1.0

    my_bead = 2 * x_lo + z % 2

    def force_copy(k, m):
        i = (z + 1 + k) % 2
        home = core * 16 + (2 * quad + i) * 2 + m
        return home, pltpu.make_async_remote_copy(
            fsend.at[2 * k + m],
            frecv.at[my_bead],
            fs_sem.at[2 * k + m],
            fr_sem.at[my_bead],
            device_id={"atoms": home},
            device_id_type=MESH,
        )

    def force_start(k):
        for m in range(2):
            home, copy = force_copy(k, m)
            if k == 0:
                copy.start()
            else:

                @pl.when(home != me)
                def _():
                    copy.start()

                @pl.when(home == me)
                def _():
                    pltpu.make_async_copy(fsend.at[2 * k + m], frecv.at[my_bead], fr_sem.at[my_bead]).start()

    def force(part):
        low, high, numbers = PARTS[part]
        for k in range(2):
            i = (z + 1 + k) % 2
            at = pl.ds(pl.multiple_of(quad * 512 + i * 256, 256), 256)
            keep = slice(k * 256, k * 256 + 256)
            plain = jnp.dot(lhs[8 * low : 8 * high, :], wst[:, at], preferred_element_type=f32)
            sloped = jnp.dot(lhs[ROWS + 8 * low : ROWS + 8 * high, :], wst[:, at], preferred_element_type=f32)
            basis = {t: utab[8 * t : 8 * t + 8, at] for t in range(low, high)}
            f = {t: tile(plain, t - low) for t in range(low, high)}
            dz = [None] * 4
            for t in range(low, high):
                term = basis[t] * tile(sloped, t - low)
                dz[t % 4] = term if dz[t % 4] is None else dz[t % 4] + term
            dz = (dz[0] + dz[1]) + (dz[2] + dz[3])

            def turn(c, s):
                return basis[c] * f[s] - basis[s] * f[c]

            dx = dy = None
            for a in numbers:
                along_x = turn(core_tile(0, 0, a), core_tile(1, 0, a)) + turn(core_tile(0, 1, a), core_tile(1, 1, a))
                along_y = turn(core_tile(0, 0, a), core_tile(0, 1, a)) + turn(core_tile(1, 0, a), core_tile(1, 1, a))
                along_x = (a + 1.0) * along_x
                dx = along_x if dx is None else dx + along_x
                dy = along_y if dy is None else dy + along_y
            if part == 0:
                acc[0, :, keep] = dx + ones * turn(4, 5)
                acc[1, :, keep] = ones * (dy + turn(2, 3))
                acc[2, :, keep] = dz
            else:
                dx = dx + acc[0, :, keep]
                dy = ones * dy + acc[1, :, keep]
                dz = dz + acc[2, :, keep]
                dx, dy, dz = (jnp.sum(d, 0, keepdims=True) for d in (dx, dy, dz))
                for m in range(2):
                    own = near_s[pl.ds(quad * 4 + 2 * i + m, 1), :]
                    piece = slice(128 * m, 128 * m + 128)
                    fsend[2 * k + m] = jnp.concatenate(
                        [dx[:, piece], dy[:, piece], dz[:, piece], own, jnp.zeros((4, 128), f32)], 0
                    )
                force_start(k)

    share(2, 0).wait()
    mean = mix(2, 0, None, True)
    near_s[...] = relaxed - mean
    force(0)
    share(2, 1).wait()
    mix(2, 1, mean, True)
    force(1)

    for make in (data_copy, nbr_copy):
        for b, o in order:
            dest = far_dest(b, o)
            if o:
                make(b, o, dest).wait_send()
            else:

                @pl.when(dest != me)
                def _():
                    make(b, o, dest).wait_send()

    to_next.wait()
    to_prev.wait()
    gain = (-two_pi * ewald_scale * time_step) / mass_row
    drift = []
    for d in range(3):
        here = pos_s[d]
        before = jnp.concatenate([halo[0, d : d + 1, :], here[0:3, :]], 0)
        after = jnp.concatenate([here[1:4, :], halo[1, d : d + 1, :]], 0)
        drift.append(vel_s[d] - (time_step * spring_rate) * (2.0 * here - before - after))
    for b in range(4):
        pltpu.make_async_remote_copy(
            fsend.at[0], frecv.at[b], fs_sem.at[0], fr_sem.at[b], device_id={"atoms": partner}, device_id_type=MESH
        ).wait_recv()
    charges = frecv[:, 3, :]
    out_ref[6] = charges
    for d in range(3):
        here = pos_s[d]
        speed = drift[d] + gain * charges * frecv[:, d, :]
        out_ref[3 + d] = speed
        out_ref[d] = here + time_step * speed
    for k in range(2):
        for m in range(2):
            home, copy = force_copy(k, m)
            if k == 0:
                copy.wait_send()
            else:

                @pl.when(home != me)
                def _():
                    copy.wait_send()


def emit_body(packed, npos_hbm, nvel_hbm, nchg_hbm, sems):
    copies = [
        pltpu.make_async_copy(source, target, sems.at[i])
        for i, (source, target) in enumerate(
            ((packed.at[0:3], npos_hbm), (packed.at[3:6], nvel_hbm), (packed.at[6], nchg_hbm))
        )
    ]
    for copy in copies:
        copy.start()
    for copy in copies:
        copy.wait()


def step(positions, velocities, charges_in, species, neighbors, k_index, kernel, chi, hard, bond, mass):
    vmem = pl.BlockSpec(memory_space=pltpu.VMEM)
    hbm = pl.BlockSpec(memory_space=pltpu.HBM)
    dma = pltpu.SemaphoreType.DMA
    packed = pl.pallas_call(
        kernel_body,
        out_shape=pltpu.VMEM((7, 4, BLOCK), f32),
        in_specs=[hbm] * 11,
        out_specs=vmem,
        scratch_shapes=[
            pltpu.VMEM((3, 4, BLOCK), f32),
            pltpu.VMEM((3, 4, BLOCK), f32),
            pltpu.VMEM((4, BLOCK), f32),
            pltpu.VMEM((1, BLOCK), jnp.int32),
            pltpu.VMEM((8, BLOCK), jnp.int32),
            pltpu.VMEM((3, KVEC), jnp.int32),
            pltpu.VMEM((1, KVEC), f32),
            pltpu.SMEM((4, SPECIES), f32),
            pltpu.VMEM((4, 8, 128), f32),
            pltpu.VMEM((SLOTS, 8, 128), f32),
            pltpu.VMEM((SLOTS, 8, 128), jnp.int32),
            pltpu.VMEM((ROWS, HALF), f32),
            pltpu.VMEM((2 * GROWS, HALF), bf16),
            pltpu.VMEM((4 * GROWS, 512), bf16),
            pltpu.VMEM((HALF, 256), bf16),
            pltpu.VMEM((128, HALF), bf16),
            pltpu.VMEM((4, 96, 128), f32),
            pltpu.VMEM((4, EXROWS, 256), f32),
            pltpu.VMEM((4, EXROWS, 256), f32),
            pltpu.VMEM((3, 8, HALF), f32),
            pltpu.VMEM((ROWS, 128), f32),
            pltpu.VMEM((2 * ROWS, 128), bf16),
            pltpu.VMEM((SLOTS, 128), f32),
            pltpu.VMEM((SLOTS, 128), f32),
            pltpu.VMEM((SLOTS, 128), f32),
            pltpu.VMEM((24, 128), f32),
            pltpu.VMEM((4, 8, 128), f32),
            pltpu.VMEM((4, 8, 128), f32),
            pltpu.VMEM((2, 8, 128), f32),
            dma((11,)),
            dma((16,)),
            dma((16,)),
            dma((16,)),
            dma((16,)),
            dma((4, 2)),
            dma((4, 2)),
            dma((4,)),
            dma((4,)),
            dma((2,)),
            dma((2,)),
        ],
        compiler_params=pltpu.CompilerParams(collective_id=0, has_side_effects=True),
        name="pimd_step",
    )(
        positions.transpose(1, 0, 2),
        velocities.transpose(1, 0, 2),
        charges_in,
        species.reshape(1, BLOCK),
        neighbors,
        k_index,
        kernel.reshape(1, KVEC),
        chi,
        hard,
        bond,
        mass,
    )
    spatial = jax.ShapeDtypeStruct((3, 4, BLOCK), f32)
    new_positions, new_velocities, charges = pl.pallas_call(
        emit_body,
        out_shape=(spatial, spatial, jax.ShapeDtypeStruct((4, BLOCK), f32)),
        in_specs=[vmem],
        out_specs=(hbm, hbm, hbm),
        scratch_shapes=[dma((3,))],
        name="emit",
    )(pltpu.with_memory_space_constraint(packed, pltpu.VMEM))
    return new_positions.transpose(1, 0, 2), new_velocities.transpose(1, 0, 2), charges


def solution(mesh):
    return jax.shard_map(
        step,
        mesh=mesh,
        in_specs=(
            P("beads", None, "atoms"),
            P("beads", None, "atoms"),
            P("beads", "atoms"),
            P("atoms"),
            P(None, "atoms"),
            P(),
            P(),
            P(),
            P(),
            P(),
            P(),
        ),
        out_specs=(P("beads", None, "atoms"), P("beads", None, "atoms"), P("beads", "atoms")),
        check_vma=False,
    )
```
